32 devices in a mesh: seq: 8 (over z, y), head: 4 (over x, core).
Axes of the slice: x: 2, y: 2, z: 4, core: 2. Of those that a mesh axis runs over, the one named last changes fastest.
Arguments:
- inputs: bfloat16 [2048, 2560], P('seq', 'head'), may hold values from -6 to 6
- step_sizes: float32 [40, 2048], P('head', 'seq'), may hold values from 0.1 to 1
- input_map: bfloat16 [2048, 128], P('seq'), may hold values from -1.78125 to 1.78125
- output_map: bfloat16 [2048, 128], P('seq'), may hold values from -1.78125 to 1.78125
- level_table: float32 [40, 2, 12], P('head'), may hold values from 0.25 to 2
- token_class: int32 [2048], P('seq'), may hold values from 0 to 1
- cotangent: bfloat16 [2048, 2560], P('seq', 'head'), may hold values from -6 to 6
Outputs:
- layer_out: bfloat16 [2048, 2560], P('seq', 'head')
- input_grad: bfloat16 [2048, 2560], P('seq', 'head')
- step_grad: float32 [40, 2048], P('head', 'seq')
- input_map_grad: float32 [2048, 128], P('seq')
- output_map_grad: float32 [2048, 128], P('seq')
- table_grad: float32 [40, 2, 12], P('head')
The draws below stay inside these ranges and needn't reach their ends.
All inputs are finite; a program needn't handle non-finite values.
Results may differ from the reference program's by a relative error of at most 0.006.
Values may be sent and summed in bfloat16 or wider, within the bound.
A program may use at most 64 MiB of HBM per device.

```python
import math
import jax
import jax.numpy as jnp
from jax import lax

H = 40
P_SIZE = 64
N = 128
Q = 128
CLASSES = 2
TOK_DEV = 256
TOKENS = 2048
TOK_BITS = 8
STRETCH_BITS = 7
LEVELS = 12
N_SEQ = 8


def plant(drawn, rng, low, largest):
    longest = drawn.shape.index(max(drawn.shape))
    spots = []
    for shift in (0, 1):
        where = [jax.random.randint(jax.random.fold_in(rng, axis), (), 0, length) for axis, length in enumerate(drawn.shape)]
        where[longest] = (where[longest] + shift) % drawn.shape[longest]
        spots.append(tuple(where))
    return drawn.at[spots[0]].set(low).at[spots[1]].set(largest)


def levels(rng, dims, split, low, largest):
    level, own = 1.0, jax.random.fold_in(rng, 6)
    for dim, blocks in split:
        heights = jnp.exp(jax.random.uniform(jax.random.fold_in(own, dim), (blocks,), jnp.float32, low / len(split), largest / len(split)))
        level = level * jnp.repeat(heights, dims[dim] // blocks).reshape([-1 if axis == dim else 1 for axis in range(len(dims))])
    return level


def bell_draw(own_key, extent, spread, limit, shards=(), held_as=jnp.bfloat16):
    array = jax.random.normal(own_key, extent, jnp.float32) * spread
    if len(shards) > 0:
        array = levels(own_key, extent, shards, -0.22, 0.18) * array
    return jnp.clip(array, min=-limit, max=limit).astype(held_as)


def setup_inputs(seed: int = 0) -> dict:
    keys = jax.random.split(jax.random.key(seed), 8)
    inputs = bell_draw(keys[0], (TOKENS, H * P_SIZE), 1.0, 6.0, ((0, 8), (1, 4)))
    step_sizes = jnp.clip(jnp.exp(math.log(1.0) - 2.3025851 * jax.random.uniform(keys[1], (H, TOKENS), jnp.float32) ** levels(keys[1], (H, TOKENS), ((0, 4), (1, 8)), -0.2, 0.2)), 0.1, 1.0)
    input_map = bell_draw(keys[2], (TOKENS, N), (N ** -0.25), 1.78125, ((0, 8),))
    output_map = bell_draw(keys[3], (TOKENS, N), (N ** -0.25), 1.78125, ((0, 8),))
    level_table = jnp.clip(jnp.exp(math.log(2.0) - 2.0794415 * jax.random.uniform(keys[4], (H, CLASSES, LEVELS), jnp.float32) ** levels(keys[4], (H, CLASSES, LEVELS), ((0, 4),), -0.2, 0.2)), 0.25, 2.0)
    token_class = plant(jax.random.randint(keys[5], (TOKENS,), 0, CLASSES), jax.random.fold_in(keys[5], 1), 0, CLASSES - 1).astype(jnp.int32)
    cotangent = bell_draw(keys[6], (TOKENS, H * P_SIZE), 1.0, 6.0, ((0, 8), (1, 4)))
    return dict(inputs=inputs, step_sizes=step_sizes, input_map=input_map, output_map=output_map, level_table=level_table, token_class=token_class, cotangent=cotangent)


highest = lax.Precision.HIGHEST

def level_of(differ, bit_count):
    result = jnp.zeros(differ.shape, jnp.int32)
    for bit_index in range(bit_count):
        result = result + (differ >= 1 << bit_index).astype(jnp.int32)
    return result

def level_scale(level_count):
    ladder = jnp.arange(level_count).astype(jnp.float32)
    return jnp.where(ladder > 0, jnp.exp2(-0.5 * (ladder - 1.0)), 1.0).astype(jnp.float32)

def rounded(value):
    return lax.optimization_barrier(value.astype(jnp.bfloat16)).astype(jnp.float32)

def reference(inputs, step_sizes, input_map, output_map, level_table, token_class, cotangent):
    stretch_count = TOKENS // Q
    per_device = TOK_DEV // Q
    position = jnp.arange(Q, dtype=jnp.int32)
    near = level_of(position[:, None] ^ position[None, :], STRETCH_BITS)
    causal = position[:, None] >= position[None, :]
    near_onehot = jnp.stack([(near == level_index) & causal for level_index in range(STRETCH_BITS + 1)]).astype(jnp.float32)
    scales = level_scale(LEVELS)
    class_onehot = (token_class[:, None] == jnp.arange(CLASSES, dtype=jnp.int32)[None, :]).astype(jnp.float32)
    class_stretches = class_onehot.reshape(stretch_count, Q, CLASSES)
    class_first = jnp.transpose(class_stretches, (2, 0, 1))
    map_in = input_map.reshape(stretch_count, Q, N).astype(jnp.float32)
    map_out = output_map.reshape(stretch_count, Q, N).astype(jnp.float32)
    scores = jnp.einsum('ctn,csn->cts', map_out, map_in, precision=highest)
    head_inputs = jnp.transpose(inputs.reshape(TOKENS, H, P_SIZE), (1, 0, 2))
    head_grads = jnp.transpose(cotangent.reshape(TOKENS, H, P_SIZE), (1, 0, 2))

    def per_head(carry, packed):
        head_in, head_cot, head_step, head_table = packed
        values = head_in.reshape(stretch_count, Q, P_SIZE).astype(jnp.float32)
        grads = head_cot.reshape(stretch_count, Q, P_SIZE).astype(jnp.float32)
        step_stretches = head_step.reshape(stretch_count, Q)
        weighted = head_table * scales[None, :]
        coeff = jnp.dot(class_onehot, weighted[:, :STRETCH_BITS + 1], precision=highest).reshape(stretch_count, Q, STRETCH_BITS + 1)
        weight = jnp.einsum('ctl,lts->cts', coeff, near_onehot, precision=highest)
        mixing = rounded(scores * weight * step_stretches[:, None, :])
        intra_out = jnp.einsum('cts,csp->ctp', mixing, values, precision=highest)
        scaled_in = rounded(values * step_stretches[:, :, None])
        stretch_state = jnp.einsum('csp,csn->cpn', scaled_in, map_in, precision=highest)
        block_state = rounded(stretch_state.reshape(N_SEQ, per_device, P_SIZE, N).sum(axis=1))
        masked = grads[None] * class_first[:, :, :, None]
        query_state = jnp.einsum('kctp,ctn->kcpn', masked, map_out, precision=highest)
        query_block = query_state.reshape(CLASSES, N_SEQ, per_device, P_SIZE, N).sum(axis=2)
        class_state = jnp.zeros((CLASSES, stretch_count, P_SIZE, N), jnp.float32)
        source_state = jnp.zeros((stretch_count, P_SIZE, N), jnp.float32)
        far_grad = []
        for level_index in range(STRETCH_BITS + 1, LEVELS):
            if level_index <= TOK_BITS:
                span = 2 ** (level_index - 1 - STRETCH_BITS)
                unit = 1
                source_base = stretch_state
                query_base = query_state
            else:
                span = 2 ** (level_index - 1 - TOK_BITS)
                unit = per_device
                source_base = block_state
                query_base = query_block
            blocks = source_base.reshape(-1, span, P_SIZE, N).sum(axis=1)
            query_blocks = query_base.reshape(CLASSES, -1, span, P_SIZE, N).sum(axis=2)
            odd = (jnp.arange(blocks.shape[0]) % 2 == 1)[:, None, None]
            earlier = jnp.concatenate([jnp.zeros_like(blocks[:1]), blocks[:-1]], axis=0)
            later = jnp.concatenate([query_blocks[:, 1:], jnp.zeros_like(query_blocks[:, :1])], axis=1)
            segment = jnp.repeat(jnp.where(odd, earlier, 0.0), span * unit, axis=0)
            back = jnp.repeat(jnp.where(odd[None], 0.0, later), span * unit, axis=1)
            class_state = class_state + weighted[:, level_index][:, None, None, None] * segment[None]
            source_state = source_state + jnp.einsum('k,kcpn->cpn', weighted[:, level_index], back, precision=highest)
            far_grad.append(scales[level_index] * lax.optimization_barrier(jnp.sum(segment[None] * query_state, axis=(1, 2, 3))))
        class_round = rounded(class_state)
        reads = jnp.einsum('ctn,kcpn->kctp', map_out, class_round, precision=highest)
        far_out = lax.optimization_barrier(jnp.sum(class_first[:, :, :, None] * reads, axis=0))
        layer = (intra_out + far_out).astype(jnp.bfloat16).reshape(TOKENS, P_SIZE)
        source_round = rounded(source_state)
        value_grad = jnp.einsum('csn,cpn->csp', map_in, source_round, precision=highest)
        mix_grad = jnp.einsum('ctp,csp->cts', grads, values, precision=highest)
        score_grad = rounded(mix_grad * weight * step_stretches[:, None, :])
        back_values = jnp.einsum('cts,ctp->csp', mixing, grads, precision=highest)
        input_grad = (back_values + step_stretches[:, :, None] * value_grad).astype(jnp.bfloat16).reshape(TOKENS, P_SIZE)
        step_grad = (lax.optimization_barrier(jnp.sum(mix_grad * scores * weight, axis=1)) + lax.optimization_barrier(jnp.sum(values * value_grad, axis=2))).reshape(TOKENS)
        map_in_grad = jnp.einsum('cts,ctn->csn', score_grad, map_out, precision=highest) + jnp.einsum('csp,cpn->csn', scaled_in, source_round, precision=highest)
        out_reads = jnp.einsum('ctp,kcpn->kctn', grads, class_round, precision=highest)
        map_out_grad = jnp.einsum('cts,csn->ctn', score_grad, map_in, precision=highest) + lax.optimization_barrier(jnp.sum(class_first[:, :, :, None] * out_reads, axis=0))
        near_terms = mix_grad * scores * step_stretches[:, None, :]
        per_level = jnp.einsum('cts,lts->ctl', near_terms, near_onehot, precision=highest)
        near_grad = jnp.einsum('ctk,ctl->kl', class_stretches, per_level, precision=highest) * scales[None, :STRETCH_BITS + 1]
        table_grad = jnp.concatenate([near_grad, jnp.stack(far_grad, axis=1)], axis=1) / jnp.sqrt(jnp.float32(TOKENS))
        new_carry = (carry[0] + map_in_grad.reshape(TOKENS, N), carry[1] + map_out_grad.reshape(TOKENS, N))
        return (new_carry, (layer, input_grad, step_grad, table_grad))
    zeros = jnp.zeros((TOKENS, N), jnp.float32)
    sums, stacked = lax.scan(per_head, (zeros, zeros), (head_inputs, head_grads, step_sizes, level_table))
    layer_out = jnp.transpose(stacked[0], (1, 0, 2)).reshape(TOKENS, H * P_SIZE)
    input_grad = jnp.transpose(stacked[1], (1, 0, 2)).reshape(TOKENS, H * P_SIZE)
    return (layer_out, input_grad, stacked[2], sums[0], sums[1], stacked[3])
```

```python
import functools
import math

import jax
import jax.numpy as jnp
from jax import lax
from jax.experimental import pallas as pl
from jax.experimental.pallas import tpu as pltpu
from jax.sharding import PartitionSpec as P

Q = 128
LANES = 128
F32 = jnp.float32
BF16 = jnp.bfloat16
HIGH = lax.Precision.HIGHEST
MESH = pl.DeviceIdType.MESH


def dot(a, b, ca, cb, precision=None):
    return lax.dot_general(
        a, b, (((ca,), (cb,)), ((), ())), precision=precision, preferred_element_type=F32
    )


def scale_of(level):
    return 1.0 if level == 0 else 2.0 ** (-(level - 1) / 2)


def kernel(
    dims,
    x_hbm,
    step_hbm,
    bin_hbm,
    cout_hbm,
    table_hbm,
    class_hbm,
    g_hbm,
    out_ref,
    xg_ref,
    sg_ref,
    ing_ref,
    outg_ref,
    tg_ref,
    step_pad,
    step_t,
    bin_t,
    mo2_t,
    stepx,
    scaled,
    clsb,
    lev,
    scores,
    mo2,
    s0,
    q1,
    qown,
    frun,
    rrun,
    fcs,
    fsrc,
    nout,
    nback,
    score_sum,
    grad,
    out_acc,
    tab,
    send_f,
    recv_f,
    send_r,
    recv_r,
    core_recv,
    x_send,
    x_recv,
    final,
    final_recv,
    tsend,
    trecv,
    f_ssem,
    f_rsem,
    r_ssem,
    r_rsem,
    c_ssem,
    c_rsem,
    x_ssem,
    x_rsem,
    a_ssem,
    a_rsem,
    t_ssem,
    t_rsem,
    known,
    steprow,
    sgrow,
    x_ref,
    step_ref,
    bin_ref,
    cout_ref,
    class_ref,
    g_ref,
    table_ref,
    in_sem,
):
    heads, width, tokens, state, levels, nb, n_head, total = dims
    per = LANES // width
    pairs = heads // per
    sb = Q.bit_length() - 1
    mid = sb + 1
    far0 = mid + 1
    device = lax.axis_index("seq")
    mine = lax.axis_index("head")
    low = lax.rem(mine, 2)
    group = mine // 2
    groups = n_head // 2
    beside = mine + 1 - 2 * low

    def across(i):
        return {"head": 2 * lax.rem(group + i, groups) + low}

    barrier = pltpu.get_barrier_semaphore()
    for b in range(nb):
        pl.semaphore_signal(
            barrier, inc=1, device_id={"seq": device ^ (1 << b)}, device_id_type=MESH
        )
    for i in range(1, groups):
        pl.semaphore_signal(barrier, inc=1, device_id=across(i), device_id_type=MESH)
    pl.semaphore_signal(barrier, inc=1, device_id={"head": beside}, device_id_type=MESH)

    loads = [
        pltpu.make_async_copy(src, dst, in_sem.at[i])
        for i, (src, dst) in enumerate(
            [
                (class_hbm, class_ref),
                (cout_hbm, cout_ref),
                (bin_hbm, bin_ref),
                (step_hbm, step_ref),
                (x_hbm, x_ref),
                (g_hbm, g_ref),
                (table_hbm, table_ref),
            ]
        )
    ]
    for load in loads:
        load.start()

    lane = lax.broadcasted_iota(jnp.int32, (1, LANES), 1)
    halves = [(lane // width == j) for j in range(per)]
    half_f = [m.astype(F32) for m in halves]
    half_b = [m.astype(F32).astype(BF16) for m in halves]
    padded = step_pad.shape[0]

    def wrow(p, k, level):
        row = jnp.zeros((1, LANES), F32)
        for j in range(per):
            row = jnp.where(halves[j], table_ref[p * per + j, k, level] * scale_of(level), row)
        return row

    def cols(p):
        return pl.ds(pl.multiple_of(p * LANES, LANES), LANES)

    spans = [slice(c * Q, (c + 1) * Q) for c in range(2)]
    for load in loads[:4]:
        load.wait()
    row = class_ref[...].astype(F32)
    clsb[...] = dot(
        jnp.broadcast_to(row, (16, tokens)).astype(BF16),
        jnp.full((16, LANES), 0.0625, BF16),
        0,
        0,
    )
    step_pad[...] = jnp.zeros_like(step_pad)
    step_pad[:heads, :] = step_ref[...]
    rest = step_pad[...]
    parts = []
    for _ in range(3):
        parts.append(rest.astype(BF16))
        rest = rest - parts[-1].astype(F32)
    step_t[...] = jnp.concatenate(parts, axis=0).T
    for c in range(2):
        bin_t[c] = bin_ref[spans[c], :].T
        one = clsb[spans[c], :]
        mo = cout_ref[spans[c], :].astype(F32)
        for k, mask in ((0, 1.0 - one), (1, one)):
            masked = (mo * mask).astype(BF16)
            mo2[c, :, k * state : (k + 1) * state] = masked
            mo2_t[c, k * state : (k + 1) * state, :] = masked.T

    bit_of = [(device >> b) & 1 for b in range(nb)]
    above = [device >> (b + 1) for b in range(nb)]
    ones = [(1 << (nb - b - 1)) - 1 for b in range(nb)]
    f_sent = [(bit_of[b] == 0) | (above[b] != ones[b]) for b in range(nb)]
    f_came = [(bit_of[b] == 1) | (above[b] != ones[b]) for b in range(nb)]
    f_on = [above[b] != ones[b] for b in range(nb)]
    count = [sum(bit_of[b + 1 :], jnp.int32(0)) for b in range(nb)]
    by_class = [count[b] >= 3 for b in range(nb)]
    by_level = [count[b] <= 2 for b in range(nb)]
    c_sent = [(bit_of[b] == 1) & by_level[b] for b in range(nb)]
    c_came = [(bit_of[b] == 0) & by_level[b] for b in range(nb)]
    top = bit_of[nb - 1]

    def f_copy(b, p):
        return pltpu.make_async_remote_copy(
            send_f.at[b, p], recv_f.at[b, p], f_ssem.at[b, p], f_rsem.at[b, p],
            device_id={"seq": device ^ (1 << b)}, device_id_type=MESH,
        )

    def r_copy(b, slot, p):
        return pltpu.make_async_remote_copy(
            send_r.at[b, slot, p], recv_r.at[b, slot, p],
            r_ssem.at[b, slot, p], r_rsem.at[b, slot, p],
            device_id={"seq": device ^ (1 << b)}, device_id_type=MESH,
        )

    def above_rows(b, p, k):
        high = jnp.zeros((1, LANES), F32)
        second = high
        for other in range(b + 1, nb):
            row = wrow(p, k, far0 + other)
            second = jnp.where(bit_of[other] == 1, high, second)
            high = jnp.where(bit_of[other] == 1, row, high)
        return high, second

    def prepare_back(b, p, r0, r1):
        if nb - 1 - b >= 3:

            @pl.when(by_class[b])
            def _():
                send_r[b, 0, p] = r0.astype(BF16)
                send_r[b, 1, p] = r1.astype(BF16)

        if b + 1 < nb:

            @pl.when(by_level[b] & (count[b] >= 1))
            def _():
                high = above_rows(b, p, 0)[0] * r0 + above_rows(b, p, 1)[0] * r1
                rrun[0, p] = high
                send_r[b, 0, p] = high.astype(BF16)

    def prepare_rest(b, p, r0, r1):
        @pl.when(c_sent[b])
        def _():
            own = wrow(p, 0, far0 + b) * r0 + wrow(p, 1, far0 + b) * r1
            send_r[b, 2, p] = own.astype(BF16)

        if b + 2 < nb:

            @pl.when(count[b] == 2)
            def _():
                second = above_rows(b, p, 0)[1] * r0 + above_rows(b, p, 1)[1] * r1
                rrun[1, p] = second
                send_r[b, 1, p] = second.astype(BF16)

    def when_started(flag, copy):
        @pl.when(flag)
        def _():
            copy.start()

    def start_high(b, p):
        if b + 1 < nb:
            when_started(count[b] >= 1, r_copy(b, 0, p))

    def start_second(b, p):
        if b + 2 < nb:
            when_started(count[b] >= 2, r_copy(b, 1, p))

    def put_rows(k, level, p, value):
        for j in range(per):
            tab[k * levels + level, pl.ds(p * per + j, 1), :] = value * half_f[j]

    def take_f(b, p):
        @pl.when(f_came[b])
        def _():
            f_copy(b, p).wait_recv()
            got = recv_f[b, p].astype(F32)
            if b + 1 < nb:
                grown = frun[p] + got
                frun[p] = grown

                @pl.when(f_sent[b + 1])
                def _():
                    send_f[b + 1, p] = grown.astype(BF16)
                    f_copy(b + 1, p).start()

            @pl.when(bit_of[b] == 1)
            def _():
                for k in range(2):
                    fcs[k, p] = fcs[k, p] + wrow(p, k, far0 + b) * got
                    put_rows(k, far0 + b, p, jnp.sum(got * qown[k, p], axis=0, keepdims=True))

    def take_high(b, p):
        if b + 1 == nb:
            return

        @pl.when((count[b] >= 1) & by_level[b])
        def _():
            r_copy(b, 0, p).wait_recv()
            high = rrun[0, p] + recv_r[b, 0, p].astype(F32)
            rrun[0, p] = high
            last = (count[b + 1] == 0) & (bit_of[b + 1] == 1)

            @pl.when(last)
            def _():
                send_r[b + 1, 2, p] = high.astype(BF16)
                r_copy(b + 1, 2, p).start()

            if b + 2 < nb:

                @pl.when(count[b + 1] >= 1)
                def _():
                    send_r[b + 1, 0, p] = high.astype(BF16)
                    r_copy(b + 1, 0, p).start()

        if nb - 1 - b >= 3:

            @pl.when(by_class[b])
            def _():
                got = []
                for k in range(2):
                    r_copy(b, k, p).wait_recv()
                    got.append(recv_r[b, k, p].astype(F32))
                    rrun[k, p] = rrun[k, p] + got[k]

                @pl.when(bit_of[b] == 0)
                def _():
                    fsrc[p] = (
                        fsrc[p]
                        + wrow(p, 0, far0 + b) * got[0]
                        + wrow(p, 1, far0 + b) * got[1]
                    )

                r0 = rrun[0, p]
                r1 = rrun[1, p]
                prepare_back(b + 1, p, r0, r1)
                start_high(b + 1, p)
                prepare_rest(b + 1, p, r0, r1)
                start_second(b + 1, p)
                when_started(c_sent[b + 1], r_copy(b + 1, 2, p))

    def take_second(b, p):
        if b + 2 >= nb:
            return

        @pl.when(count[b] == 2)
        def _():
            r_copy(b, 1, p).wait_recv()
            second = rrun[1, p] + recv_r[b, 1, p].astype(F32)
            rrun[1, p] = second

            @pl.when(bit_of[b + 1] == 1)
            def _():
                send_r[b + 1, 2, p] = second.astype(BF16)
                r_copy(b + 1, 2, p).start()

            if b + 3 < nb:

                @pl.when(bit_of[b + 1] == 0)
                def _():
                    send_r[b + 1, 1, p] = second.astype(BF16)
                    r_copy(b + 1, 1, p).start()

    def take_own(b, p):
        @pl.when(c_came[b])
        def _():
            r_copy(b, 2, p).wait_recv()
            fsrc[p] = fsrc[p] + recv_r[b, 2, p].astype(F32)

    def primary(b, p):
        @pl.when(top == 0)
        def _():
            take_f(b, p)

        @pl.when(top == 1)
        def _():
            take_high(b, p)

    def secondary(b, p):
        @pl.when(top == 0)
        def _():
            take_high(b, p)

        take_second(b, p)

        @pl.when(top == 1)
        def _():
            take_f(b, p)

    def sources(p):
        picks = (
            lax.rem(lax.broadcasted_iota(jnp.int32, step_t.shape[1:] + (LANES,), 0), padded)
            == p * per + lax.broadcasted_iota(jnp.int32, step_t.shape[1:] + (LANES,), 1) // width
        ).astype(F32)
        grown = dot(step_t[...], picks.astype(BF16), 1, 0)
        sc = (x_ref[:, cols(p)].astype(F32) * grown).astype(BF16)
        st = [dot(bin_t[c], sc[spans[c]], 1, 0) for c in range(2)]
        block = st[0] + st[1]
        send_f[0, p] = block.astype(BF16)
        when_started(f_sent[0], f_copy(0, p))
        stepx[p] = grown
        scaled[p] = sc
        s0[p] = st[0]
        frun[p] = block

    def queries(p):
        q = [dot(mo2_t[c], g_ref[spans[c], cols(p)], 1, 0) for c in range(2)]
        both = [q[0][k * state : (k + 1) * state] + q[1][k * state : (k + 1) * state] for k in range(2)]
        if nb > 3:
            for k in range(2):
                rrun[k, p] = both[k]
        prepare_back(0, p, *both)
        start_high(0, p)
        if nb > 3:
            when_started(by_class[0], r_copy(0, 1, p))
        for k in range(2):
            q1[k, p] = q[1][k * state : (k + 1) * state]
            qown[k, p] = both[k]

    def rest_of(p):
        prepare_rest(0, p, qown[0, p], qown[1, p])
        if nb > 2:
            when_started(count[0] == 2, r_copy(0, 1, p))

    def each(body):
        def step(p, carry):
            body(p)
            return carry

        lax.fori_loop(0, pairs, step, 0)

    for load in loads[4:]:
        load.wait()
    pl.semaphore_wait(barrier, nb + groups)

    def send_own(i, carry):
        second = i >= pairs
        p = jnp.where(second, i - pairs, i)
        forward = second == (top == 1)

        @pl.when(second & (top == 1))
        def _():
            rest_of(p)

        @pl.when(forward)
        def _():
            sources(p)

        @pl.when(jnp.logical_not(forward))
        def _():
            queries(p)

        return carry

    lax.fori_loop(0, 2 * pairs, send_own, 0)

    def last_own(p):
        @pl.when(top == 0)
        def _():
            rest_of(p)

        when_started(c_sent[0], r_copy(0, 2, p))

    each(last_own)

    def tell(b):
        pl.semaphore_signal(
            known.at[b], inc=1, device_id={"seq": device ^ (1 << b)}, device_id_type=MESH
        )

    if nb > 1:
        tell(0)

    t_id = lax.broadcasted_iota(jnp.int32, (Q, Q), 0)
    s_id = lax.broadcasted_iota(jnp.int32, (Q, Q), 1)
    differ = t_id ^ s_id
    level_id = jnp.zeros((Q, Q), jnp.int32)
    for bit in range(sb):
        level_id = level_id + (differ >= (1 << bit)).astype(jnp.int32)
    lev[...] = jnp.where(t_id >= s_id, level_id, -1)
    for c in range(2):
        scores[c] = dot(cout_ref[spans[c], :], bin_ref[spans[c], :], 1, 1)
    for h in range(heads):
        for c in range(2):
            steprow[h, c : c + 1, :] = step_ref[h : h + 1, spans[c]]
    score_sum[...] = jnp.zeros_like(score_sum)
    out_acc[...] = jnp.zeros_like(out_acc)
    tab[...] = jnp.zeros_like(tab)
    fcs[...] = jnp.zeros_like(fcs)
    fsrc[...] = jnp.zeros_like(fsrc)

    def near(p, carry):
        lv = lev[...]
        hit = [lv == level for level in range(sb + 1)]
        weights = []
        for j in range(per):
            rows = []
            for k in range(2):
                acc = jnp.zeros((Q, Q), F32)
                for level in range(sb + 1):
                    acc = jnp.where(
                        hit[level], table_ref[p * per + j, k, level] * scale_of(level), acc
                    )
                rows.append(acc)
            weights.append(rows)
        terms = [[jnp.zeros((Q, Q), F32) for k in range(2)] for j in range(per)]
        for c in range(2):
            x = x_ref[spans[c], cols(p)]
            g = g_ref[spans[c], cols(p)]
            xs = jnp.concatenate([x * half_b[j] for j in range(per)], axis=0)
            gs = jnp.concatenate([g * half_b[j] for j in range(per)], axis=0)
            mg = dot(gs, x, 1, 1)
            is_one = clsb[spans[c], :] > 0.5
            score = scores[c]
            mixes = []
            total_sg = score_sum[c]
            for j in range(per):
                head = p * per + j
                step = steprow[head, c : c + 1, :]
                weight = jnp.where(is_one, weights[j][1], weights[j][0])
                ws = weight * step
                mgj = mg[j * Q : (j + 1) * Q]
                mixes.append((score * ws).astype(BF16))
                total_sg = total_sg + mgj * ws
                graded = mgj * score
                sgrow[head, c : c + 1, :] = jnp.sum(graded * weight, axis=0, keepdims=True)
                term = graded * step
                terms[j][0] = terms[j][0] + jnp.where(is_one, 0.0, term)
                terms[j][1] = terms[j][1] + jnp.where(is_one, term, 0.0)
            score_sum[c] = total_sg
            nout[p, spans[c], :] = dot(jnp.concatenate(mixes, axis=1), xs, 1, 0)
            nback[p, spans[c], :] = dot(jnp.concatenate(mixes, axis=0), gs, 0, 0)
        for j in range(per):
            for k in range(2):
                term = terms[j][k]
                for level in range(sb + 1):
                    if level <= 3:
                        value = jnp.sum(jnp.where(hit[level], term, 0.0), axis=0, keepdims=True)
                    else:
                        size = 1 << (level - 1)
                        value = jnp.zeros((1, LANES), F32)
                        for odd in range(1, Q // size, 2):
                            rows = jnp.sum(term[odd * size : (odd + 1) * size], axis=0, keepdims=True)
                            value = jnp.where(lane // size == odd - 1, rows, value)
                    tab[k * levels + level, pl.ds(p * per + j, 1), :] = value
        return carry
    def table_of(some):
        summed = jnp.zeros((heads, LANES), F32)
        for k in range(2):
            for level in some:
                at = k * levels + level
                col = jnp.sum(tab[at], axis=1, keepdims=True)
                summed = jnp.where(lane == at, col * (scale_of(level) / math.sqrt(total)), summed)
        return summed

    def forward_map(p, c):
        cs = []
        for k in range(2):
            value = fcs[k, p]
            if c == 1:
                value = value + wrow(p, k, mid) * s0[p]
            cs.append(value.astype(BF16))
        return jnp.concatenate(cs, axis=0)

    def backward_map(p, c):
        src = fsrc[p]
        if c == 0:
            src = src + wrow(p, 0, mid) * q1[0, p] + wrow(p, 1, mid) * q1[1, p]
        return src.astype(BF16)

    def far_forward(p):
        for c in range(2):
            cs = forward_map(p, c)
            out_acc[c] = out_acc[c] + dot(g_ref[spans[c], cols(p)], cs, 1, 1)
            read = dot(mo2[c], cs, 1, 0)
            out_ref[spans[c], cols(p)] = (nout[p, spans[c], :] + read).astype(BF16)

    def far_backward(p):
        for c in range(2):
            src = backward_map(p, c)
            grad[0, c] = grad[0, c] + dot(scaled[p, spans[c], :], src, 1, 1)
            vg = dot(bin_ref[spans[c], :], src, 1, 0)
            xg_ref[spans[c], cols(p)] = (
                nback[p, spans[c], :] + stepx[p, spans[c], :] * vg
            ).astype(BF16)
            picks = jnp.concatenate(half_f + [jnp.zeros((8 - per, LANES), F32)], axis=0)
            far_step = dot(picks, x_ref[spans[c], cols(p)].astype(F32) * vg, 1, 1, HIGH)
            for j in range(per):
                at = (p * per + j, slice(c, c + 1), slice(None))
                sgrow[at] = sgrow[at] + far_step[j : j + 1]

    def finish_forward():
        for c in range(2):
            is_one = clsb[spans[c], :] > 0.5
            acc = out_acc[c]
            grad[1, c] = grad[1, c] + jnp.where(is_one, acc[:, state:], acc[:, :state])

    def beside_copy(kind):
        return pltpu.make_async_remote_copy(
            grad.at[kind, 1 - low], core_recv.at[kind], c_ssem.at[kind], c_rsem.at[kind],
            device_id={"head": beside}, device_id_type=MESH,
        )

    def across_copy(kind, i, slot):
        return pltpu.make_async_remote_copy(
            x_send.at[kind], x_recv.at[kind, slot], x_ssem.at[kind, i], x_rsem.at[kind, i],
            device_id=across(i), device_id_type=MESH,
        )

    def share_copy(kind):
        return pltpu.make_async_remote_copy(
            final.at[kind], final_recv.at[kind], a_ssem.at[kind], a_rsem.at[kind],
            device_id={"head": beside}, device_id_type=MESH,
        )

    def sum_beside(kind):
        beside_copy(kind).wait_recv()
        part = (grad[kind, low] + core_recv[kind]).astype(BF16)
        x_send[kind] = part
        x_recv[kind, group] = part
        for i in range(1, groups):
            across_copy(kind, i, group).start()

    def sum_across(kind):
        for i in range(1, groups):
            across_copy(kind, i, lax.rem(group - i + groups, groups)).wait_recv()
        whole = x_recv[kind, 0].astype(F32)
        for i in range(1, groups):
            whole = whole + x_recv[kind, i].astype(F32)
        final[kind] = whole
        share_copy(kind).start()

    for stage in range(nb):

        def rounds(p, stage=stage):
            if stage < nb - 1:
                primary(stage, p)
            if stage == 0:
                near(p, 0)
                for k in range(2):
                    put_rows(k, mid, p, jnp.sum(s0[p] * q1[k, p], axis=0, keepdims=True))
            if stage >= 1:
                secondary(stage - 1, p)
            if stage >= 2:
                take_own(stage - 2, p)

        each(rounds)
        if stage == 0:
            for c in range(2):
                sgb = score_sum[c].astype(BF16)
                grad[0, c] = dot(sgb, cout_ref[spans[c], :], 0, 0)
                grad[1, c] = dot(sgb, bin_ref[spans[c], :], 1, 0)
            near_table = table_of(range(mid + 1))
            for b in range(nb - 1):
                pl.semaphore_wait(known.at[b], 1)
                if b + 1 < nb - 1:
                    tell(b + 1)

    early = 1 - top

    def first_kind(p):
        if nb >= 2:
            take_own(nb - 2, p)

        @pl.when(top == 0)
        def _():
            far_forward(p)

        @pl.when(top == 1)
        def _():
            far_backward(p)

    each(first_kind)

    @pl.when(top == 0)
    def _():
        finish_forward()

    beside_copy(early).start()

    def last_kind(p, carry):
        @pl.when(top == 0)
        def _():
            take_own(nb - 1, p)
            far_backward(p)

        @pl.when(top == 1)
        def _():
            take_f(nb - 1, p)
            far_forward(p)

        @pl.when(p == 0)
        def _():
            sum_beside(early)

        return carry

    lax.fori_loop(0, pairs, last_kind, 0)

    @pl.when(top == 1)
    def _():
        finish_forward()

    late = top
    beside_copy(late).start()

    def table_copy(i):
        return pltpu.make_async_remote_copy(
            tsend, trecv.at[i], t_ssem.at[i], t_rsem.at[i],
            device_id={"seq": device ^ i}, device_id_type=MESH,
        )

    table_sum = near_table + table_of(range(far0, levels))
    tsend[:heads, :] = table_sum
    trecv[0, :heads, :] = table_sum
    for i in range(1, 1 << nb):
        table_copy(i).start()

    sum_beside(late)
    sum_across(early)
    for h in range(heads):
        for c in range(2):
            sg_ref[h : h + 1, spans[c]] = sgrow[h, c : c + 1, :]
    for b in range(nb):

        def drain(p, b=b):
            @pl.when(f_sent[b])
            def _():
                f_copy(b, p).wait_send()

            @pl.when(c_sent[b])
            def _():
                r_copy(b, 2, p).wait_send()

            for slot in range(min(2, nb - 1 - b)):

                @pl.when(count[b] > slot)
                def _(slot=slot):
                    r_copy(b, slot, p).wait_send()

        each(drain)
    sum_across(late)
    for i in range(1, 1 << nb):
        table_copy(i).wait_recv()
    table_sum = trecv[device, :heads, :]
    for owner in range(1, 1 << nb):
        table_sum = table_sum + trecv[device ^ owner, :heads, :]
    for k in range(2):
        tg_ref[:, k, :] = table_sum[:, k * levels : (k + 1) * levels]

    def half(which):
        return pl.ds(pl.multiple_of(which * Q, Q), Q), slice(None)

    for kind, ref in ((0, ing_ref), (1, outg_ref)):
        ref[half(low)] = final[kind]
    for kind in (early, late):
        share_copy(kind).wait_recv()
    for kind, ref in ((0, ing_ref), (1, outg_ref)):
        ref[half(1 - low)] = final_recv[kind]

    for kind in range(2):
        beside_copy(kind).wait_send()
        share_copy(kind).wait_send()
        for i in range(1, groups):
            across_copy(kind, i, group).wait_send()
    for i in range(1, 1 << nb):
        table_copy(i).wait_send()


def write_out(*refs):
    sem = refs[-1]
    copies = [pltpu.make_async_copy(refs[i], refs[6 + i], sem.at[i]) for i in range(6)]
    for copy in copies:
        copy.start()
    for copy in copies:
        copy.wait()


def local(inputs, step_sizes, input_map, output_map, level_table, token_class, cotangent):
    tokens, state = input_map.shape
    heads = step_sizes.shape[0]
    width = inputs.shape[1] // heads
    levels = level_table.shape[2]
    n_seq = lax.axis_size("seq")
    n_head = lax.axis_size("head")
    nb = n_seq.bit_length() - 1
    per = LANES // width
    pairs = heads // per
    assert tokens == 2 * Q and heads % per == 0 and n_head % 2 == 0 and nb > 0
    assert level_table.shape[1] == 2 and state == Q and 2 * levels <= LANES
    dims = (heads, width, tokens, state, levels, nb, n_head, float(tokens * n_seq))
    vmem = pl.BlockSpec(memory_space=pltpu.VMEM)
    hbm = pl.BlockSpec(memory_space=pltpu.HBM)
    dma = pltpu.SemaphoreType.DMA
    unit = (pairs, state, LANES)
    tall = (pairs, tokens, LANES)
    padded = -(-heads // 16) * 16
    placed = [
        pltpu.with_memory_space_constraint(a, pltpu.HBM)
        for a in (
            inputs, step_sizes, input_map, output_map, level_table,
            token_class.reshape(1, tokens), cotangent,
        )
    ]
    results = pl.pallas_call(
        functools.partial(kernel, dims),
        out_shape=(
            jax.ShapeDtypeStruct(inputs.shape, BF16),
            jax.ShapeDtypeStruct(inputs.shape, BF16),
            jax.ShapeDtypeStruct(step_sizes.shape, F32),
            jax.ShapeDtypeStruct(input_map.shape, F32),
            jax.ShapeDtypeStruct(output_map.shape, F32),
            jax.ShapeDtypeStruct(level_table.shape, F32),
        ),
        in_specs=[hbm] * 7,
        out_specs=(vmem,) * 6,
        scratch_shapes=[
            pltpu.VMEM((padded, tokens), F32),
            pltpu.VMEM((tokens, 3 * padded), BF16),
            pltpu.VMEM((2, state, Q), BF16),
            pltpu.VMEM((2, 2 * state, Q), BF16),
            pltpu.VMEM(tall, F32),
            pltpu.VMEM(tall, BF16),
            pltpu.VMEM((tokens, LANES), F32),
            pltpu.VMEM((Q, Q), jnp.int32),
            pltpu.VMEM((2, Q, Q), F32),
            pltpu.VMEM((2, Q, 2 * state), BF16),
            pltpu.VMEM(unit, F32),
            pltpu.VMEM((2, *unit), F32),
            pltpu.VMEM((2, *unit), F32),
            pltpu.VMEM(unit, F32),
            pltpu.VMEM((2, *unit), F32),
            pltpu.VMEM((2, *unit), F32),
            pltpu.VMEM(unit, F32),
            pltpu.VMEM(tall, F32),
            pltpu.VMEM(tall, F32),
            pltpu.VMEM((2, Q, Q), F32),
            pltpu.VMEM((2, 2, Q, state), F32),
            pltpu.VMEM((2, Q, 2 * state), F32),
            pltpu.VMEM((2 * levels, heads, LANES), F32),
            pltpu.VMEM((nb, *unit), BF16),
            pltpu.VMEM((nb, *unit), BF16),
            pltpu.VMEM((nb, 3, *unit), BF16),
            pltpu.VMEM((nb, 3, *unit), BF16),
            pltpu.VMEM((2, Q, state), F32),
            pltpu.VMEM((2, Q, state), BF16),
            pltpu.VMEM((2, n_head // 2, Q, state), BF16),
            pltpu.VMEM((2, Q, state), F32),
            pltpu.VMEM((2, Q, state), F32),
            pltpu.VMEM((padded, LANES), F32),
            pltpu.VMEM((n_seq, padded, LANES), F32),
            dma((nb, pairs)),
            dma((nb, pairs)),
            dma((nb, 3, pairs)),
            dma((nb, 3, pairs)),
            dma((2,)),
            dma((2,)),
            dma((2, n_head // 2)),
            dma((2, n_head // 2)),
            dma((2,)),
            dma((2,)),
            dma((n_seq,)),
            dma((n_seq,)),
            pltpu.SemaphoreType.REGULAR((nb,)),
            pltpu.VMEM((heads, 2, LANES), F32),
            pltpu.VMEM((heads, 2, LANES), F32),
            pltpu.VMEM(inputs.shape, BF16),
            pltpu.VMEM(step_sizes.shape, F32),
            pltpu.VMEM(input_map.shape, BF16),
            pltpu.VMEM(output_map.shape, BF16),
            pltpu.VMEM((1, tokens), jnp.int32),
            pltpu.VMEM(cotangent.shape, BF16),
            pltpu.SMEM(level_table.shape, F32),
            dma((7,)),
        ],
        compiler_params=pltpu.CompilerParams(
            collective_id=0, has_side_effects=True, vmem_limit_bytes=48 << 20
        ),
    )(*placed)
    return pl.pallas_call(
        write_out,
        out_shape=tuple(jax.ShapeDtypeStruct(r.shape, r.dtype) for r in results),
        in_specs=[vmem] * 6,
        out_specs=(hbm,) * 6,
        scratch_shapes=[dma((6,))],
        compiler_params=pltpu.CompilerParams(vmem_limit_bytes=8 << 20),
    )(*results)


def solution(mesh):
    placed = (
        P("seq", "head"),
        P("head", "seq"),
        P("seq", None),
        P("seq", None),
        P("head", None, None),
        P("seq"),
        P("seq", "head"),
    )
    return jax.shard_map(
        local,
        mesh=mesh,
        in_specs=placed,
        out_specs=(
            P("seq", "head"),
            P("seq", "head"),
            P("head", "seq"),
            P("seq", None),
            P("seq", None),
            P("head", None, None),
        ),
        check_vma=False,
    )
```

```python
import functools
import math

import jax
import jax.numpy as jnp
from jax import lax
from jax.experimental import pallas as pl
from jax.experimental.pallas import tpu as pltpu
from jax.sharding import PartitionSpec as P

Q = 128
LANES = 128
F32 = jnp.float32
BF16 = jnp.bfloat16
HIGH = lax.Precision.HIGHEST
MESH = pl.DeviceIdType.MESH


def dot(a, b, ca, cb, precision=None):
    return lax.dot_general(
        a, b, (((ca,), (cb,)), ((), ())), precision=precision, preferred_element_type=F32
    )


def scale_of(level):
    return 1.0 if level == 0 else 2.0 ** (-(level - 1) / 2)


def kernel(
    dims,
    x_hbm,
    step_hbm,
    bin_hbm,
    cout_hbm,
    table_hbm,
    class_hbm,
    g_hbm,
    out_ref,
    xg_ref,
    sg_ref,
    ing_ref,
    outg_ref,
    tg_ref,
    step_pad,
    step_t,
    bin_t,
    mo2_t,
    stepx,
    scaled,
    clsb,
    lev,
    scores,
    mo2,
    s0,
    q1,
    qown,
    frun,
    rrun,
    fcs,
    fsrc,
    nout,
    nback,
    score_sum,
    grad,
    out_acc,
    tab,
    send_f,
    recv_f,
    send_r,
    recv_r,
    core_recv,
    x_recv,
    maps,
    source_maps,
    tsend,
    trecv,
    f_ssem,
    f_rsem,
    r_ssem,
    r_rsem,
    c_ssem,
    c_rsem,
    x_ssem,
    x_rsem,
    t_ssem,
    t_rsem,
    l_ssem,
    l_rsem,
    h_ssem,
    h_rsem,
    known,
    steprow,
    sgrow,
    x_ref,
    step_ref,
    bin_ref,
    cout_ref,
    class_ref,
    g_ref,
    table_ref,
    in_sem,
):
    heads, width, tokens, state, levels, nb, n_head, total = dims
    per = LANES // width
    pairs = heads // per
    sb = Q.bit_length() - 1
    mid = sb + 1
    far0 = mid + 1
    device = lax.axis_index("seq")
    mine = lax.axis_index("head")
    low = lax.rem(mine, 2)
    group = mine // 2
    groups = n_head // 2

    def across(i, other):
        return {"head": 2 * lax.rem(group + i, groups) + (1 - low if other else low)}

    barrier = pltpu.get_barrier_semaphore()
    for b in range(nb):
        pl.semaphore_signal(
            barrier, inc=1, device_id={"seq": device ^ (1 << b)}, device_id_type=MESH
        )
    for i in range(groups):
        for other in range(2):
            if i or other:
                pl.semaphore_signal(
                    barrier, inc=1, device_id=across(i, other), device_id_type=MESH
                )

    loads = [
        pltpu.make_async_copy(src, dst, in_sem.at[i])
        for i, (src, dst) in enumerate(
            [
                (class_hbm, class_ref),
                (cout_hbm, cout_ref),
                (bin_hbm, bin_ref),
                (step_hbm, step_ref),
                (x_hbm, x_ref),
                (g_hbm, g_ref),
                (table_hbm, table_ref),
            ]
        )
    ]
    for load in loads:
        load.start()

    lane = lax.broadcasted_iota(jnp.int32, (1, LANES), 1)
    halves = [(lane // width == j) for j in range(per)]
    picks = (
        lax.broadcasted_iota(jnp.int32, (16, 2 * LANES), 0)
        == lax.rem(lax.broadcasted_iota(jnp.int32, (16, 2 * LANES), 1), LANES) // width
    ).astype(F32).astype(BF16)
    half_f = [m.astype(F32) for m in halves]
    half_b = [m.astype(F32).astype(BF16) for m in halves]
    padded = step_pad.shape[0]
    relayed = (pairs + 1) // 2

    def wrow(p, k, level):
        row = jnp.zeros((1, LANES), F32)
        for j in range(per):
            row = jnp.where(halves[j], table_ref[p * per + j, k, level] * scale_of(level), row)
        return row

    def cols(p):
        return pl.ds(pl.multiple_of(p * LANES, LANES), LANES)

    spans = [slice(c * Q, (c + 1) * Q) for c in range(2)]
    for load in loads[:4]:
        load.wait()
    row = class_ref[...].astype(F32)
    clsb[...] = dot(
        jnp.broadcast_to(row, (16, tokens)).astype(BF16),
        jnp.full((16, LANES), 0.0625, BF16),
        0,
        0,
    )
    step_pad[...] = jnp.zeros_like(step_pad)
    step_pad[:heads, :] = step_ref[...]
    rest = step_pad[...]
    parts = []
    for _ in range(3):
        parts.append(rest.astype(BF16))
        rest = rest - parts[-1].astype(F32)
    step_t[...] = jnp.concatenate(parts, axis=0).T
    for c in range(2):
        bin_t[c] = bin_ref[spans[c], :].T
        one = clsb[spans[c], :]
        mo = cout_ref[spans[c], :].astype(F32)
        for k, mask in ((0, 1.0 - one), (1, one)):
            masked = (mo * mask).astype(BF16)
            mo2[c, :, k * state : (k + 1) * state] = masked
            mo2_t[c, k * state : (k + 1) * state, :] = masked.T

    bit_of = [(device >> b) & 1 for b in range(nb)]
    above = [device >> (b + 1) for b in range(nb)]
    ones = [(1 << (nb - b - 1)) - 1 for b in range(nb)]
    f_sent = [(bit_of[b] == 0) | (above[b] != ones[b]) for b in range(nb)]
    f_came = [(bit_of[b] == 1) | (above[b] != ones[b]) for b in range(nb)]
    f_on = [above[b] != ones[b] for b in range(nb)]
    count = [sum(bit_of[b + 1 :], jnp.int32(0)) for b in range(nb)]
    by_class = [count[b] >= 3 for b in range(nb)]
    by_level = [count[b] <= 2 for b in range(nb)]
    c_sent = [(bit_of[b] == 1) & by_level[b] for b in range(nb)]
    c_came = [(bit_of[b] == 0) & by_level[b] for b in range(nb)]
    top = bit_of[nb - 1]
    side = bit_of[nb - 2]
    end = nb - 1
    inner = top != side
    f_sent[end - 1] = side == 0
    f_came[end - 1] = side == 1
    f_sent[end] = inner & (top == 0)
    f_came[end] = top == 1
    c_sent[end] = inner & (top == 1)
    high_sent = [count[b] >= 1 for b in range(nb)]
    high_came = list(high_sent)
    high_sent[end - 1] = (top == 1) & (side == 1)
    high_came[end - 1] = (top == 1) & (side == 0)

    def f_copy(b, p):
        return pltpu.make_async_remote_copy(
            send_f.at[b, p], recv_f.at[b, p], f_ssem.at[b, p], f_rsem.at[b, p],
            device_id={"seq": device ^ (1 << b)}, device_id_type=MESH,
        )

    def r_copy(b, slot, p):
        return pltpu.make_async_remote_copy(
            send_r.at[b, slot, p], recv_r.at[b, slot, p],
            r_ssem.at[b, slot, p], r_rsem.at[b, slot, p],
            device_id={"seq": device ^ (1 << b)}, device_id_type=MESH,
        )

    def last_copy(src, dst, far, p):
        return pltpu.make_async_remote_copy(
            src, dst, l_ssem.at[far, p], l_rsem.at[p],
            device_id={"seq": device ^ (2 << (end - 1) if far else 3 << (end - 1))},
            device_id_type=MESH,
        )

    def f_last(far, p):
        return last_copy(send_f.at[end, p], recv_f.at[end, p], far, p)

    def c_last(far, p):
        return last_copy(send_r.at[end, 2, p], recv_r.at[end, 2, p], far, p)

    def relay_copy(ref, p):
        return pltpu.make_async_remote_copy(
            ref, ref, h_ssem.at[p], h_rsem.at[p],
            device_id={"seq": device ^ (1 << (end - 1))}, device_id_type=MESH,
        )

    def f_relay(p):
        return relay_copy(recv_f.at[end, p], p)

    def c_relay(p):
        return relay_copy(recv_r.at[end, 2, p], p)

    def start_last(copy, p):
        copy(0, p).start()

        @pl.when(p >= relayed)
        def _():
            copy(1, p).start()

    def above_rows(b, p, k):
        high = jnp.zeros((1, LANES), F32)
        second = high
        for other in range(b + 1, nb):
            row = wrow(p, k, far0 + other)
            second = jnp.where(bit_of[other] == 1, high, second)
            high = jnp.where(bit_of[other] == 1, row, high)
        return high, second

    def prepare_back(b, p, r0, r1):
        if nb - 1 - b >= 3:

            @pl.when(by_class[b])
            def _():
                send_r[b, 0, p] = r0.astype(BF16)
                send_r[b, 1, p] = r1.astype(BF16)

        if b + 1 < nb:

            @pl.when(by_level[b] & (count[b] >= 1))
            def _():
                high = above_rows(b, p, 0)[0] * r0 + above_rows(b, p, 1)[0] * r1
                rrun[0, p] = high
                send_r[b, 0, p] = high.astype(BF16)

    def prepare_rest(b, p, r0, r1):
        @pl.when(c_sent[b])
        def _():
            own = wrow(p, 0, far0 + b) * r0 + wrow(p, 1, far0 + b) * r1
            send_r[b, 2, p] = own.astype(BF16)

        if b + 2 < nb:

            @pl.when(count[b] == 2)
            def _():
                second = above_rows(b, p, 0)[1] * r0 + above_rows(b, p, 1)[1] * r1
                rrun[1, p] = second
                send_r[b, 1, p] = second.astype(BF16)

    def when_started(flag, copy):
        @pl.when(flag)
        def _():
            copy.start()

    def start_high(b, p):
        if b + 1 < nb:
            when_started(high_sent[b], r_copy(b, 0, p))

    def start_second(b, p):
        if b + 2 < nb:
            when_started(count[b] >= 2, r_copy(b, 1, p))

    def put_rows(k, level, p, value):
        for j in range(per):
            tab[k * levels + level, pl.ds(p * per + j, 1), :] = value * half_f[j]

    def arrive(b, p, copy, relay):
        if b < end:
            copy.wait_recv()
        else:

            @pl.when(p >= relayed)
            def _():
                copy.wait_recv()

            @pl.when((p < relayed) & jnp.logical_not(inner))
            def _():
                relay(p).wait_recv()

    def take_f(b, p):
        @pl.when(f_came[b])
        def _():
            arrive(b, p, f_copy(b, p) if b < end else f_last(0, p), f_relay)
            got = recv_f[b, p].astype(F32)
            if b + 1 < nb:
                grown = frun[p] + got
                frun[p] = grown

                @pl.when(f_sent[b + 1])
                def _():
                    send_f[b + 1, p] = grown.astype(BF16)
                    if b + 1 == end:
                        start_last(f_last, p)
                    else:
                        f_copy(b + 1, p).start()

            @pl.when(bit_of[b] == 1)
            def _():
                for k in range(2):
                    fcs[k, p] = fcs[k, p] + wrow(p, k, far0 + b) * got
                    put_rows(k, far0 + b, p, jnp.sum(got * qown[k, p], axis=0, keepdims=True))

    def take_high(b, p):
        if b + 1 == nb:
            return

        @pl.when(high_came[b] & by_level[b])
        def _():
            r_copy(b, 0, p).wait_recv()
            high = rrun[0, p] + recv_r[b, 0, p].astype(F32)
            rrun[0, p] = high
            last = (count[b + 1] == 0) & (bit_of[b + 1] == 1)

            @pl.when(last)
            def _():
                send_r[b + 1, 2, p] = high.astype(BF16)
                if b + 1 == end:
                    start_last(c_last, p)
                else:
                    r_copy(b + 1, 2, p).start()

            if b + 2 < nb:

                @pl.when(high_sent[b + 1])
                def _():
                    send_r[b + 1, 0, p] = high.astype(BF16)
                    r_copy(b + 1, 0, p).start()

        if nb - 1 - b >= 3:

            @pl.when(by_class[b])
            def _():
                got = []
                for k in range(2):
                    r_copy(b, k, p).wait_recv()
                    got.append(recv_r[b, k, p].astype(F32))
                    rrun[k, p] = rrun[k, p] + got[k]

                @pl.when(bit_of[b] == 0)
                def _():
                    fsrc[p] = (
                        fsrc[p]
                        + wrow(p, 0, far0 + b) * got[0]
                        + wrow(p, 1, far0 + b) * got[1]
                    )

                r0 = rrun[0, p]
                r1 = rrun[1, p]
                prepare_back(b + 1, p, r0, r1)
                start_high(b + 1, p)
                prepare_rest(b + 1, p, r0, r1)
                start_second(b + 1, p)
                when_started(c_sent[b + 1], r_copy(b + 1, 2, p))

    def take_second(b, p):
        if b + 2 >= nb:
            return

        @pl.when(count[b] == 2)
        def _():
            r_copy(b, 1, p).wait_recv()
            second = rrun[1, p] + recv_r[b, 1, p].astype(F32)
            rrun[1, p] = second

            @pl.when(bit_of[b + 1] == 1)
            def _():
                send_r[b + 1, 2, p] = second.astype(BF16)
                r_copy(b + 1, 2, p).start()

            if b + 3 < nb:

                @pl.when(bit_of[b + 1] == 0)
                def _():
                    send_r[b + 1, 1, p] = second.astype(BF16)
                    r_copy(b + 1, 1, p).start()

    def take_own(b, p):
        @pl.when(c_came[b])
        def _():
            arrive(b, p, r_copy(b, 2, p) if b < end else c_last(0, p), c_relay)
            fsrc[p] = fsrc[p] + recv_r[b, 2, p].astype(F32)

    def primary(b, p):
        @pl.when(top == 0)
        def _():
            take_f(b, p)

        @pl.when(top == 1)
        def _():
            take_high(b, p)

    def secondary(b, p):
        @pl.when(top == 0)
        def _():
            take_high(b, p)

        take_second(b, p)

        @pl.when(top == 1)
        def _():
            take_f(b, p)

    def sources(p):
        picks = (
            lax.rem(lax.broadcasted_iota(jnp.int32, step_t.shape[1:] + (LANES,), 0), padded)
            == p * per + lax.broadcasted_iota(jnp.int32, step_t.shape[1:] + (LANES,), 1) // width
        ).astype(F32)
        grown = dot(step_t[...], picks.astype(BF16), 1, 0)
        sc = (x_ref[:, cols(p)].astype(F32) * grown).astype(BF16)
        st = [dot(bin_t[c], sc[spans[c]], 1, 0) for c in range(2)]
        block = st[0] + st[1]
        send_f[0, p] = block.astype(BF16)
        when_started(f_sent[0], f_copy(0, p))
        stepx[p] = grown
        scaled[p] = sc
        s0[p] = st[0]
        frun[p] = block

    def queries(p):
        q = [dot(mo2_t[c], g_ref[spans[c], cols(p)], 1, 0) for c in range(2)]
        both = [q[0][k * state : (k + 1) * state] + q[1][k * state : (k + 1) * state] for k in range(2)]
        if nb > 3:
            for k in range(2):
                rrun[k, p] = both[k]
        prepare_back(0, p, *both)
        start_high(0, p)
        if nb > 3:
            when_started(by_class[0], r_copy(0, 1, p))
        for k in range(2):
            q1[k, p] = q[1][k * state : (k + 1) * state]
            qown[k, p] = both[k]

    def rest_of(p):
        prepare_rest(0, p, qown[0, p], qown[1, p])
        if nb > 2:
            when_started(count[0] == 2, r_copy(0, 1, p))

    def each(body):
        def step(p, carry):
            body(p)
            return carry

        lax.fori_loop(0, pairs, step, 0)

    for load in loads[4:]:
        load.wait()
    pl.semaphore_wait(barrier, nb + n_head - 1)

    def send_own(i, carry):
        second = i >= pairs
        p = jnp.where(second, i - pairs, i)
        forward = second == (top == 1)

        @pl.when(second & (top == 1))
        def _():
            rest_of(p)

        @pl.when(forward)
        def _():
            sources(p)

        @pl.when(jnp.logical_not(forward))
        def _():
            queries(p)

        return carry

    lax.fori_loop(0, 2 * pairs, send_own, 0)

    def last_own(p):
        @pl.when(top == 0)
        def _():
            rest_of(p)

        when_started(c_sent[0], r_copy(0, 2, p))

    each(last_own)

    def tell(b):
        pl.semaphore_signal(
            known.at[b], inc=1, device_id={"seq": device ^ (1 << b)}, device_id_type=MESH
        )

    if nb > 1:
        tell(0)

    t_id = lax.broadcasted_iota(jnp.int32, (Q, Q), 0)
    s_id = lax.broadcasted_iota(jnp.int32, (Q, Q), 1)
    differ = t_id ^ s_id
    level_id = jnp.zeros((Q, Q), jnp.int32)
    for bit in range(sb):
        level_id = level_id + (differ >= (1 << bit)).astype(jnp.int32)
    lev[...] = jnp.where(t_id >= s_id, level_id, -1)
    for c in range(2):
        scores[c] = dot(cout_ref[spans[c], :], bin_ref[spans[c], :], 1, 1)
    for h in range(heads):
        for c in range(2):
            steprow[h, c : c + 1, :] = step_ref[h : h + 1, spans[c]]
    score_sum[...] = jnp.zeros_like(score_sum)
    out_acc[...] = jnp.zeros_like(out_acc)
    tab[...] = jnp.zeros_like(tab)
    fcs[...] = jnp.zeros_like(fcs)
    fsrc[...] = jnp.zeros_like(fsrc)

    def near(p, carry):
        lv = lev[...]
        hit = [lv == level for level in range(sb + 1)]
        weights = []
        for j in range(per):
            rows = []
            for k in range(2):
                acc = jnp.zeros((Q, Q), F32)
                for level in range(sb + 1):
                    acc = jnp.where(
                        hit[level], table_ref[p * per + j, k, level] * scale_of(level), acc
                    )
                rows.append(acc)
            weights.append(rows)
        terms = [[jnp.zeros((Q, Q), F32) for k in range(2)] for j in range(per)]
        for c in range(2):
            x = x_ref[spans[c], cols(p)]
            g = g_ref[spans[c], cols(p)]
            xs = jnp.concatenate([x * half_b[j] for j in range(per)], axis=0)
            gs = jnp.concatenate([g * half_b[j] for j in range(per)], axis=0)
            mg = dot(gs, x, 1, 1)
            is_one = clsb[spans[c], :] > 0.5
            score = scores[c]
            mixes = []
            total_sg = score_sum[c]
            for j in range(per):
                head = p * per + j
                step = steprow[head, c : c + 1, :]
                weight = jnp.where(is_one, weights[j][1], weights[j][0])
                ws = weight * step
                mgj = mg[j * Q : (j + 1) * Q]
                mixes.append((score * ws).astype(BF16))
                total_sg = total_sg + mgj * ws
                graded = mgj * score
                sgrow[head, c : c + 1, :] = jnp.sum(graded * weight, axis=0, keepdims=True)
                term = graded * step
                terms[j][0] = terms[j][0] + jnp.where(is_one, 0.0, term)
                terms[j][1] = terms[j][1] + jnp.where(is_one, term, 0.0)
            score_sum[c] = total_sg
            nout[p, spans[c], :] = dot(jnp.concatenate(mixes, axis=1), xs, 1, 0)
            nback[p, spans[c], :] = dot(jnp.concatenate(mixes, axis=0), gs, 0, 0)
        for j in range(per):
            for k in range(2):
                term = terms[j][k]
                for level in range(sb + 1):
                    if level <= 3:
                        value = jnp.sum(jnp.where(hit[level], term, 0.0), axis=0, keepdims=True)
                    else:
                        size = 1 << (level - 1)
                        value = jnp.zeros((1, LANES), F32)
                        for odd in range(1, Q // size, 2):
                            rows = jnp.sum(term[odd * size : (odd + 1) * size], axis=0, keepdims=True)
                            value = jnp.where(lane // size == odd - 1, rows, value)
                    tab[k * levels + level, pl.ds(p * per + j, 1), :] = value
        return carry
    def table_of(some):
        summed = jnp.zeros((heads, LANES), F32)
        for k in range(2):
            for level in some:
                at = k * levels + level
                col = jnp.sum(tab[at], axis=1, keepdims=True)
                summed = jnp.where(lane == at, col * (scale_of(level) / math.sqrt(total)), summed)
        return summed

    def forward_map(p, c):
        cs = []
        for k in range(2):
            value = fcs[k, p]
            if c == 1:
                value = value + wrow(p, k, mid) * s0[p]
            cs.append(value.astype(BF16))
        return jnp.concatenate(cs, axis=0)

    def backward_map(p, c):
        src = fsrc[p]
        if c == 0:
            src = src + wrow(p, 0, mid) * q1[0, p] + wrow(p, 1, mid) * q1[1, p]
        return src.astype(BF16)

    def map_forward(p):
        for c in range(2):
            cs = forward_map(p, c)
            maps[c, p] = cs
            out_acc[c] = out_acc[c] + dot(g_ref[spans[c], cols(p)], cs, 1, 1)

    def values_forward(p):
        for c in range(2):
            read = dot(mo2[c], maps[c, p], 1, 0)
            out_ref[spans[c], cols(p)] = (nout[p, spans[c], :] + read).astype(BF16)

    def map_backward(p):
        for c in range(2):
            src = backward_map(p, c)
            source_maps[c, p] = src
            grad[0, c] = grad[0, c] + dot(scaled[p, spans[c], :], src, 1, 1)

    def values_backward(p):
        for c in range(2):
            vg = dot(bin_ref[spans[c], :], source_maps[c, p], 1, 0)
            xg_ref[spans[c], cols(p)] = (
                nback[p, spans[c], :] + stepx[p, spans[c], :] * vg
            ).astype(BF16)
            whole = x_ref[spans[c], cols(p)].astype(F32) * vg
            coarse = whole.astype(BF16)
            fine = (whole - coarse.astype(F32)).astype(BF16)
            far_step = dot(picks, jnp.concatenate([coarse, fine], axis=1), 1, 1)
            for j in range(per):
                at = (p * per + j, slice(c, c + 1), slice(None))
                sgrow[at] = sgrow[at] + far_step[j : j + 1]

    def finish_forward():
        for c in range(2):
            is_one = clsb[spans[c], :] > 0.5
            acc = out_acc[c]
            grad[1, c] = grad[1, c] + jnp.where(is_one, acc[:, state:], acc[:, :state])

    def beside_copy(kind):
        return pltpu.make_async_remote_copy(
            grad.at[kind], core_recv.at[kind], c_ssem.at[kind], c_rsem.at[kind],
            device_id=across(0, 1), device_id_type=MESH,
        )

    def across_copy(kind, i, other, slot, part):
        return pltpu.make_async_remote_copy(
            x_recv.at[kind, group, low], x_recv.at[kind, slot, part],
            x_ssem.at[kind, i, other], x_rsem.at[kind, i, other],
            device_id=across(i, other), device_id_type=MESH,
        )

    def sum_beside(kind):
        beside_copy(kind).wait_recv()
        for c in range(2):
            x_recv[kind, group, c] = (grad[kind, c] + core_recv[kind, c]).astype(BF16)
        for i in range(1, groups):
            for other in range(2):
                across_copy(kind, i, other, group, low).start()

    def sum_across(kind):
        for i in range(1, groups):
            slot = lax.rem(group - i + groups, groups)
            for other in range(2):
                part = 1 - low if other else low
                across_copy(kind, i, other, slot, part).wait_recv()

    def whole_sum(kind, c):
        whole = x_recv[kind, 0, c].astype(F32)
        for i in range(1, groups):
            whole = whole + x_recv[kind, i, c].astype(F32)
        return whole

    for stage in range(nb):

        def rounds(p, stage=stage):
            if stage < nb - 1:
                primary(stage, p)
            if stage == 0:
                near(p, 0)
                for k in range(2):
                    put_rows(k, mid, p, jnp.sum(s0[p] * q1[k, p], axis=0, keepdims=True))
            if stage >= 1:
                secondary(stage - 1, p)
        each(rounds)
        if stage == 0:
            for c in range(2):
                sgb = score_sum[c].astype(BF16)
                grad[0, c] = dot(sgb, cout_ref[spans[c], :], 0, 0)
                grad[1, c] = dot(sgb, bin_ref[spans[c], :], 1, 0)
            near_table = table_of(range(mid + 1))
            for b in range(nb - 1):
                pl.semaphore_wait(known.at[b], 1)
                if b + 1 < nb - 1:
                    tell(b + 1)

    early = 1 - top

    @pl.when(inner)
    def _():
        def hand_on(p, carry):
            @pl.when(top == 0)
            def _():
                c_last(0, p).wait_recv()
                c_relay(p).start()

            @pl.when(top == 1)
            def _():
                f_last(0, p).wait_recv()
                f_relay(p).start()

            return carry

        lax.fori_loop(0, relayed, hand_on, 0)

    @pl.when(top == 0)
    def _():
        def forward(p):
            map_forward(p)
            values_forward(p)

        each(forward)
        finish_forward()
        beside_copy(1).start()

    def last_values(p):
        values_backward(p)

        @pl.when(top == 1)
        def _():
            values_forward(p)

    def last_kind(p, carry):
        for b in range(nb - 1):
            take_own(b, p)

        @pl.when(top == 0)
        def _():
            @pl.when(p == 0)
            def _():
                sum_beside(1)

            take_own(nb - 1, p)
            map_backward(p)

        @pl.when(top == 1)
        def _():
            map_backward(p)

            @pl.when(p == pairs - 1)
            def _():
                beside_copy(0).start()

            take_f(nb - 1, p)
            map_forward(p)

        return carry

    lax.fori_loop(0, pairs, last_kind, 0)

    @pl.when(top == 1)
    def _():
        finish_forward()

    late = top
    beside_copy(late).start()

    @pl.when(top == 1)
    def _():
        sum_beside(0)

    def table_copy(i):
        return pltpu.make_async_remote_copy(
            tsend, trecv.at[i], t_ssem.at[i], t_rsem.at[i],
            device_id={"seq": device ^ i}, device_id_type=MESH,
        )

    table_sum = near_table + table_of(range(far0, levels))
    tsend[:heads, :] = table_sum
    trecv[0, :heads, :] = table_sum
    for i in range(1, 1 << nb):
        table_copy(i).start()

    sum_beside(late)
    each(last_values)
    for h in range(heads):
        for c in range(2):
            sg_ref[h : h + 1, spans[c]] = sgrow[h, c : c + 1, :]
    sum_across(early)
    for b in range(end):

        def drain(p, b=b):
            @pl.when(f_sent[b])
            def _():
                f_copy(b, p).wait_send()

            @pl.when(c_sent[b])
            def _():
                r_copy(b, 2, p).wait_send()

            for slot in range(min(2, nb - 1 - b)):

                @pl.when(high_sent[b] if slot == 0 else count[b] > slot)
                def _(slot=slot):
                    r_copy(b, slot, p).wait_send()

        each(drain)

    def drain_last(p, copy, relay):
        copy(0, p).wait_send()

        @pl.when(p >= relayed)
        def _():
            copy(1, p).wait_send()

        @pl.when(p < relayed)
        def _():
            relay(p).wait_send()

    @pl.when(f_sent[end])
    def _():
        each(lambda p: drain_last(p, f_last, c_relay))

    @pl.when(c_sent[end])
    def _():
        each(lambda p: drain_last(p, c_last, f_relay))

    sum_across(late)
    for i in range(1, 1 << nb):
        table_copy(i).wait_recv()
    table_sum = trecv[device, :heads, :]
    for owner in range(1, 1 << nb):
        table_sum = table_sum + trecv[device ^ owner, :heads, :]
    for k in range(2):
        tg_ref[:, k, :] = table_sum[:, k * levels : (k + 1) * levels]

    for kind, ref in ((0, ing_ref), (1, outg_ref)):
        for c in range(2):
            ref[spans[c], :] = whole_sum(kind, c)

    for kind in range(2):
        beside_copy(kind).wait_send()
        for i in range(1, groups):
            for other in range(2):
                across_copy(kind, i, other, group, low).wait_send()
    for i in range(1, 1 << nb):
        table_copy(i).wait_send()


def write_out(*refs):
    sem = refs[-1]
    copies = [pltpu.make_async_copy(refs[i], refs[6 + i], sem.at[i]) for i in range(6)]
    for copy in copies:
        copy.start()
    for copy in copies:
        copy.wait()


def local(inputs, step_sizes, input_map, output_map, level_table, token_class, cotangent):
    tokens, state = input_map.shape
    heads = step_sizes.shape[0]
    width = inputs.shape[1] // heads
    levels = level_table.shape[2]
    n_seq = lax.axis_size("seq")
    n_head = lax.axis_size("head")
    nb = n_seq.bit_length() - 1
    per = LANES // width
    pairs = heads // per
    assert tokens == 2 * Q and heads % per == 0 and n_head % 2 == 0 and nb > 2
    assert level_table.shape[1] == 2 and state == Q and 2 * levels <= LANES
    dims = (heads, width, tokens, state, levels, nb, n_head, float(tokens * n_seq))
    vmem = pl.BlockSpec(memory_space=pltpu.VMEM)
    hbm = pl.BlockSpec(memory_space=pltpu.HBM)
    dma = pltpu.SemaphoreType.DMA
    unit = (pairs, state, LANES)
    tall = (pairs, tokens, LANES)
    padded = -(-heads // 16) * 16
    placed = [
        pltpu.with_memory_space_constraint(a, pltpu.HBM)
        for a in (
            inputs, step_sizes, input_map, output_map, level_table,
            token_class.reshape(1, tokens), cotangent,
        )
    ]
    results = pl.pallas_call(
        functools.partial(kernel, dims),
        out_shape=(
            jax.ShapeDtypeStruct(inputs.shape, BF16),
            jax.ShapeDtypeStruct(inputs.shape, BF16),
            jax.ShapeDtypeStruct(step_sizes.shape, F32),
            jax.ShapeDtypeStruct(input_map.shape, F32),
            jax.ShapeDtypeStruct(output_map.shape, F32),
            jax.ShapeDtypeStruct(level_table.shape, F32),
        ),
        in_specs=[hbm] * 7,
        out_specs=(vmem,) * 6,
        scratch_shapes=[
            pltpu.VMEM((padded, tokens), F32),
            pltpu.VMEM((tokens, 3 * padded), BF16),
            pltpu.VMEM((2, state, Q), BF16),
            pltpu.VMEM((2, 2 * state, Q), BF16),
            pltpu.VMEM(tall, F32),
            pltpu.VMEM(tall, BF16),
            pltpu.VMEM((tokens, LANES), F32),
            pltpu.VMEM((Q, Q), jnp.int32),
            pltpu.VMEM((2, Q, Q), F32),
            pltpu.VMEM((2, Q, 2 * state), BF16),
            pltpu.VMEM(unit, F32),
            pltpu.VMEM((2, *unit), F32),
            pltpu.VMEM((2, *unit), F32),
            pltpu.VMEM(unit, F32),
            pltpu.VMEM((2, *unit), F32),
            pltpu.VMEM((2, *unit), F32),
            pltpu.VMEM(unit, F32),
            pltpu.VMEM(tall, F32),
            pltpu.VMEM(tall, F32),
            pltpu.VMEM((2, Q, Q), F32),
            pltpu.VMEM((2, 2, Q, state), F32),
            pltpu.VMEM((2, Q, 2 * state), F32),
            pltpu.VMEM((2 * levels, heads, LANES), F32),
            pltpu.VMEM((nb, *unit), BF16),
            pltpu.VMEM((nb, *unit), BF16),
            pltpu.VMEM((nb, 3, *unit), BF16),
            pltpu.VMEM((nb, 3, *unit), BF16),
            pltpu.VMEM((2, 2, Q, state), F32),
            pltpu.VMEM((2, n_head // 2, 2, Q, state), BF16),
            pltpu.VMEM((2, pairs, 2 * state, LANES), BF16),
            pltpu.VMEM((2, *unit), BF16),
            pltpu.VMEM((padded, LANES), F32),
            pltpu.VMEM((n_seq, padded, LANES), F32),
            dma((nb, pairs)),
            dma((nb, pairs)),
            dma((nb, 3, pairs)),
            dma((nb, 3, pairs)),
            dma((2,)),
            dma((2,)),
            dma((2, n_head // 2, 2)),
            dma((2, n_head // 2, 2)),
            dma((n_seq,)),
            dma((n_seq,)),
            dma((2, pairs)),
            dma((pairs,)),
            dma((pairs,)),
            dma((pairs,)),
            pltpu.SemaphoreType.REGULAR((nb,)),
            pltpu.VMEM((heads, 2, LANES), F32),
            pltpu.VMEM((heads, 2, LANES), F32),
            pltpu.VMEM(inputs.shape, BF16),
            pltpu.VMEM(step_sizes.shape, F32),
            pltpu.VMEM(input_map.shape, BF16),
            pltpu.VMEM(output_map.shape, BF16),
            pltpu.VMEM((1, tokens), jnp.int32),
            pltpu.VMEM(cotangent.shape, BF16),
            pltpu.SMEM(level_table.shape, F32),
            dma((7,)),
        ],
        compiler_params=pltpu.CompilerParams(
            collective_id=0, has_side_effects=True, vmem_limit_bytes=48 << 20
        ),
    )(*placed)
    return pl.pallas_call(
        write_out,
        out_shape=tuple(jax.ShapeDtypeStruct(r.shape, r.dtype) for r in results),
        in_specs=[vmem] * 6,
        out_specs=(hbm,) * 6,
        scratch_shapes=[dma((6,))],
        compiler_params=pltpu.CompilerParams(vmem_limit_bytes=8 << 20),
    )(*results)


def solution(mesh):
    placed = (
        P("seq", "head"),
        P("head", "seq"),
        P("seq", None),
        P("seq", None),
        P("head", None, None),
        P("seq"),
        P("seq", "head"),
    )
    return jax.shard_map(
        local,
        mesh=mesh,
        in_specs=placed,
        out_specs=(
            P("seq", "head"),
            P("seq", "head"),
            P("head", "seq"),
            P("seq", None),
            P("seq", None),
            P("head", None, None),
        ),
        check_vma=False,
    )
```

```python
import functools
import math

import jax
import jax.numpy as jnp
from jax import lax
from jax.experimental import pallas as pl
from jax.experimental.pallas import tpu as pltpu
from jax.sharding import PartitionSpec as P

Q = 128
LANES = 128
F32 = jnp.float32
BF16 = jnp.bfloat16
HIGH = lax.Precision.HIGHEST
MESH = pl.DeviceIdType.MESH


def dot(a, b, ca, cb, precision=None):
    return lax.dot_general(
        a, b, (((ca,), (cb,)), ((), ())), precision=precision, preferred_element_type=F32
    )


def scale_of(level):
    return 1.0 if level == 0 else 2.0 ** (-(level - 1) / 2)


def kernel(
    dims,
    x_hbm,
    step_hbm,
    bin_hbm,
    cout_hbm,
    table_hbm,
    class_hbm,
    g_hbm,
    out_ref,
    xg_ref,
    sg_ref,
    ing_ref,
    outg_ref,
    tg_ref,
    step_pad,
    step_t,
    bin_t,
    mo2_t,
    stepx,
    scaled,
    clsb,
    lev,
    scores,
    mo2,
    s0,
    q1,
    qown,
    frun,
    rrun,
    fcs,
    fsrc,
    nout,
    nback,
    score_sum,
    grad,
    out_acc,
    tab,
    send_f,
    recv_f,
    send_r,
    recv_r,
    core_recv,
    x_recv,
    maps,
    source_maps,
    near_sum,
    tsend,
    trecv,
    f_ssem,
    f_rsem,
    r_ssem,
    r_rsem,
    c_ssem,
    c_rsem,
    x_ssem,
    x_rsem,
    t_ssem,
    t_rsem,
    l_ssem,
    l_rsem,
    h_ssem,
    h_rsem,
    known,
    steprow,
    sgrow,
    x_ref,
    step_ref,
    bin_ref,
    cout_ref,
    class_ref,
    g_ref,
    table_ref,
    in_sem,
):
    heads, width, tokens, state, levels, nb, n_head, total = dims
    per = LANES // width
    pairs = heads // per
    sb = Q.bit_length() - 1
    mid = sb + 1
    far0 = mid + 1
    device = lax.axis_index("seq")
    mine = lax.axis_index("head")
    low = lax.rem(mine, 2)
    group = mine // 2
    groups = n_head // 2

    def across(i, other):
        return {"head": 2 * lax.rem(group + i, groups) + (1 - low if other else low)}

    barrier = pltpu.get_barrier_semaphore()
    for b in range(nb):
        pl.semaphore_signal(
            barrier, inc=1, device_id={"seq": device ^ (1 << b)}, device_id_type=MESH
        )
    for i in range(groups):
        for other in range(2):
            if i or other:
                pl.semaphore_signal(
                    barrier, inc=1, device_id=across(i, other), device_id_type=MESH
                )

    loads = [
        pltpu.make_async_copy(src, dst, in_sem.at[i])
        for i, (src, dst) in enumerate(
            [
                (class_hbm, class_ref),
                (cout_hbm, cout_ref),
                (bin_hbm, bin_ref),
                (step_hbm, step_ref),
                (x_hbm, x_ref),
                (g_hbm, g_ref),
                (table_hbm, table_ref),
            ]
        )
    ]
    for load in loads:
        load.start()

    lane = lax.broadcasted_iota(jnp.int32, (1, LANES), 1)
    halves = [(lane // width == j) for j in range(per)]
    picks = (
        lax.broadcasted_iota(jnp.int32, (16, 2 * LANES), 0)
        == lax.rem(lax.broadcasted_iota(jnp.int32, (16, 2 * LANES), 1), LANES) // width
    ).astype(F32).astype(BF16)
    half_f = [m.astype(F32) for m in halves]
    half_b = [m.astype(F32).astype(BF16) for m in halves]
    padded = step_pad.shape[0]
    relayed = 0

    def wrow(p, k, level):
        row = jnp.zeros((1, LANES), F32)
        for j in range(per):
            row = jnp.where(halves[j], table_ref[p * per + j, k, level] * scale_of(level), row)
        return row

    def cols(p):
        return pl.ds(pl.multiple_of(p * LANES, LANES), LANES)

    spans = [slice(c * Q, (c + 1) * Q) for c in range(2)]
    for load in loads[:4]:
        load.wait()
    row = class_ref[...].astype(F32)
    clsb[...] = dot(
        jnp.broadcast_to(row, (16, tokens)).astype(BF16),
        jnp.full((16, LANES), 0.0625, BF16),
        0,
        0,
    )
    step_pad[...] = jnp.zeros_like(step_pad)
    step_pad[:heads, :] = step_ref[...]
    rest = step_pad[...]
    parts = []
    for _ in range(3):
        parts.append(rest.astype(BF16))
        rest = rest - parts[-1].astype(F32)
    step_t[...] = jnp.concatenate(parts, axis=0).T
    for c in range(2):
        bin_t[c] = bin_ref[spans[c], :].T
        one = clsb[spans[c], :]
        mo = cout_ref[spans[c], :].astype(F32)
        for k, mask in ((0, 1.0 - one), (1, one)):
            masked = (mo * mask).astype(BF16)
            mo2[c, :, k * state : (k + 1) * state] = masked
            mo2_t[c, k * state : (k + 1) * state, :] = masked.T

    bit_of = [(device >> b) & 1 for b in range(nb)]
    above = [device >> (b + 1) for b in range(nb)]
    ones = [(1 << (nb - b - 1)) - 1 for b in range(nb)]
    f_sent = [(bit_of[b] == 0) | (above[b] != ones[b]) for b in range(nb)]
    f_came = [(bit_of[b] == 1) | (above[b] != ones[b]) for b in range(nb)]
    f_on = [above[b] != ones[b] for b in range(nb)]
    count = [sum(bit_of[b + 1 :], jnp.int32(0)) for b in range(nb)]
    by_class = [count[b] >= 3 for b in range(nb)]
    by_level = [count[b] <= 2 for b in range(nb)]
    c_sent = [(bit_of[b] == 1) & by_level[b] for b in range(nb)]
    c_came = [(bit_of[b] == 0) & by_level[b] for b in range(nb)]
    top = bit_of[nb - 1]
    side = bit_of[nb - 2]
    end = nb - 1
    inner = top != side
    f_sent[end - 1] = side == 0
    f_came[end - 1] = side == 1
    f_sent[end] = inner & (top == 0)
    f_came[end] = top == 1
    c_sent[end] = inner & (top == 1)
    high_sent = [count[b] >= 1 for b in range(nb)]
    high_came = list(high_sent)
    high_sent[end - 1] = (top == 1) & (side == 1)
    high_came[end - 1] = (top == 1) & (side == 0)

    def f_copy(b, p):
        return pltpu.make_async_remote_copy(
            send_f.at[b, p], recv_f.at[b, p], f_ssem.at[b, p], f_rsem.at[b, p],
            device_id={"seq": device ^ (1 << b)}, device_id_type=MESH,
        )

    def r_copy(b, slot, p):
        return pltpu.make_async_remote_copy(
            send_r.at[b, slot, p], recv_r.at[b, slot, p],
            r_ssem.at[b, slot, p], r_rsem.at[b, slot, p],
            device_id={"seq": device ^ (1 << b)}, device_id_type=MESH,
        )

    def last_copy(src, dst, far, p):
        return pltpu.make_async_remote_copy(
            src, dst, l_ssem.at[far, p], l_rsem.at[p],
            device_id={"seq": device ^ (2 << (end - 1) if far else 3 << (end - 1))},
            device_id_type=MESH,
        )

    def f_last(far, p):
        return last_copy(send_f.at[end, p], recv_f.at[end, p], far, p)

    def c_last(far, p):
        return last_copy(send_r.at[end, 2, p], recv_r.at[end, 2, p], far, p)

    def relay_copy(ref, p):
        return pltpu.make_async_remote_copy(
            ref, ref, h_ssem.at[p], h_rsem.at[p],
            device_id={"seq": device ^ (1 << (end - 1))}, device_id_type=MESH,
        )

    def f_relay(p):
        return relay_copy(recv_f.at[end, p], p)

    def c_relay(p):
        return relay_copy(recv_r.at[end, 2, p], p)

    def start_last(copy, p):
        copy(0, p).start()

        @pl.when(p >= relayed)
        def _():
            copy(1, p).start()

    def above_rows(b, p, k):
        high = jnp.zeros((1, LANES), F32)
        second = high
        for other in range(b + 1, nb):
            row = wrow(p, k, far0 + other)
            second = jnp.where(bit_of[other] == 1, high, second)
            high = jnp.where(bit_of[other] == 1, row, high)
        return high, second

    def prepare_back(b, p, r0, r1):
        if nb - 1 - b >= 3:

            @pl.when(by_class[b])
            def _():
                send_r[b, 0, p] = r0.astype(BF16)
                send_r[b, 1, p] = r1.astype(BF16)

        if b + 1 < nb:

            @pl.when(by_level[b] & (count[b] >= 1))
            def _():
                high = above_rows(b, p, 0)[0] * r0 + above_rows(b, p, 1)[0] * r1
                rrun[0, p] = high
                send_r[b, 0, p] = high.astype(BF16)

    def prepare_rest(b, p, r0, r1):
        @pl.when(c_sent[b])
        def _():
            own = wrow(p, 0, far0 + b) * r0 + wrow(p, 1, far0 + b) * r1
            send_r[b, 2, p] = own.astype(BF16)

        if b + 2 < nb:

            @pl.when(count[b] == 2)
            def _():
                second = above_rows(b, p, 0)[1] * r0 + above_rows(b, p, 1)[1] * r1
                rrun[1, p] = second
                send_r[b, 1, p] = second.astype(BF16)

    def when_started(flag, copy):
        @pl.when(flag)
        def _():
            copy.start()

    def start_high(b, p):
        if b + 1 < nb:
            when_started(high_sent[b], r_copy(b, 0, p))

    def start_second(b, p):
        if b + 2 < nb:
            when_started(count[b] >= 2, r_copy(b, 1, p))

    def put_rows(k, level, p, value):
        for j in range(per):
            tab[k * levels + level, pl.ds(p * per + j, 1), :] = value * half_f[j]

    def arrive(b, p, copy, relay):
        if b < end:
            copy.wait_recv()
        else:

            @pl.when(p >= relayed)
            def _():
                copy.wait_recv()

            @pl.when((p < relayed) & jnp.logical_not(inner))
            def _():
                relay(p).wait_recv()

    def take_f(b, p):
        @pl.when(f_came[b])
        def _():
            arrive(b, p, f_copy(b, p) if b < end else f_last(0, p), f_relay)
            got = recv_f[b, p].astype(F32)
            if b + 1 < nb:
                grown = frun[p] + got
                frun[p] = grown

                @pl.when(f_sent[b + 1])
                def _():
                    send_f[b + 1, p] = grown.astype(BF16)
                    if b + 1 == end:
                        start_last(f_last, p)
                    else:
                        f_copy(b + 1, p).start()

            @pl.when(bit_of[b] == 1)
            def _():
                for k in range(2):
                    fcs[k, p] = fcs[k, p] + wrow(p, k, far0 + b) * got
                    put_rows(k, far0 + b, p, jnp.sum(got * qown[k, p], axis=0, keepdims=True))

    def take_high(b, p):
        if b + 1 == nb:
            return

        @pl.when(high_came[b] & by_level[b])
        def _():
            r_copy(b, 0, p).wait_recv()
            high = rrun[0, p] + recv_r[b, 0, p].astype(F32)
            rrun[0, p] = high
            last = (count[b + 1] == 0) & (bit_of[b + 1] == 1)

            @pl.when(last)
            def _():
                send_r[b + 1, 2, p] = high.astype(BF16)
                if b + 1 == end:
                    start_last(c_last, p)
                else:
                    r_copy(b + 1, 2, p).start()

            if b + 2 < nb:

                @pl.when(high_sent[b + 1])
                def _():
                    send_r[b + 1, 0, p] = high.astype(BF16)
                    r_copy(b + 1, 0, p).start()

        if nb - 1 - b >= 3:

            @pl.when(by_class[b])
            def _():
                got = []
                for k in range(2):
                    r_copy(b, k, p).wait_recv()
                    got.append(recv_r[b, k, p].astype(F32))
                    rrun[k, p] = rrun[k, p] + got[k]

                @pl.when(bit_of[b] == 0)
                def _():
                    fsrc[p] = (
                        fsrc[p]
                        + wrow(p, 0, far0 + b) * got[0]
                        + wrow(p, 1, far0 + b) * got[1]
                    )

                r0 = rrun[0, p]
                r1 = rrun[1, p]
                prepare_back(b + 1, p, r0, r1)
                start_high(b + 1, p)
                prepare_rest(b + 1, p, r0, r1)
                start_second(b + 1, p)
                when_started(c_sent[b + 1], r_copy(b + 1, 2, p))

    def take_second(b, p):
        if b + 2 >= nb:
            return

        @pl.when(count[b] == 2)
        def _():
            r_copy(b, 1, p).wait_recv()
            second = rrun[1, p] + recv_r[b, 1, p].astype(F32)
            rrun[1, p] = second

            @pl.when(bit_of[b + 1] == 1)
            def _():
                send_r[b + 1, 2, p] = second.astype(BF16)
                r_copy(b + 1, 2, p).start()

            if b + 3 < nb:

                @pl.when(bit_of[b + 1] == 0)
                def _():
                    send_r[b + 1, 1, p] = second.astype(BF16)
                    r_copy(b + 1, 1, p).start()

    def take_own(b, p):
        @pl.when(c_came[b])
        def _():
            arrive(b, p, r_copy(b, 2, p) if b < end else c_last(0, p), c_relay)
            fsrc[p] = fsrc[p] + recv_r[b, 2, p].astype(F32)

    def primary(b, p):
        @pl.when(top == 0)
        def _():
            take_f(b, p)

        @pl.when(top == 1)
        def _():
            take_high(b, p)

    def secondary(b, p):
        @pl.when(top == 0)
        def _():
            take_high(b, p)

        take_second(b, p)

        @pl.when(top == 1)
        def _():
            take_f(b, p)

    def sources(p):
        picks = (
            lax.rem(lax.broadcasted_iota(jnp.int32, step_t.shape[1:] + (LANES,), 0), padded)
            == p * per + lax.broadcasted_iota(jnp.int32, step_t.shape[1:] + (LANES,), 1) // width
        ).astype(F32)
        grown = dot(step_t[...], picks.astype(BF16), 1, 0)
        sc = (x_ref[:, cols(p)].astype(F32) * grown).astype(BF16)
        st = [dot(bin_t[c], sc[spans[c]], 1, 0) for c in range(2)]
        block = st[0] + st[1]
        send_f[0, p] = block.astype(BF16)
        when_started(f_sent[0], f_copy(0, p))
        stepx[p] = grown
        scaled[p] = sc
        s0[p] = st[0]
        frun[p] = block

    def queries(p):
        q = [dot(mo2_t[c], g_ref[spans[c], cols(p)], 1, 0) for c in range(2)]
        both = [q[0][k * state : (k + 1) * state] + q[1][k * state : (k + 1) * state] for k in range(2)]
        if nb > 3:
            for k in range(2):
                rrun[k, p] = both[k]
        prepare_back(0, p, *both)
        start_high(0, p)
        if nb > 3:
            when_started(by_class[0], r_copy(0, 1, p))
        for k in range(2):
            q1[k, p] = q[1][k * state : (k + 1) * state]
            qown[k, p] = both[k]

    def rest_of(p):
        prepare_rest(0, p, qown[0, p], qown[1, p])
        if nb > 2:
            when_started(count[0] == 2, r_copy(0, 1, p))

    def each(body):
        def step(p, carry):
            body(p)
            return carry

        lax.fori_loop(0, pairs, step, 0)

    for load in loads[4:]:
        load.wait()
    pl.semaphore_wait(barrier, nb + n_head - 1)

    def send_own(i, carry):
        second = i >= pairs
        p = jnp.where(second, i - pairs, i)
        forward = second == (top == 1)

        @pl.when(second & (top == 1))
        def _():
            rest_of(p)

        @pl.when(forward)
        def _():
            sources(p)

        @pl.when(jnp.logical_not(forward))
        def _():
            queries(p)

        return carry

    lax.fori_loop(0, 2 * pairs, send_own, 0)

    def last_own(p):
        @pl.when(top == 0)
        def _():
            rest_of(p)

        when_started(c_sent[0], r_copy(0, 2, p))

    each(last_own)

    def tell(b):
        pl.semaphore_signal(
            known.at[b], inc=1, device_id={"seq": device ^ (1 << b)}, device_id_type=MESH
        )

    if nb > 1:
        tell(0)

    t_id = lax.broadcasted_iota(jnp.int32, (Q, Q), 0)
    s_id = lax.broadcasted_iota(jnp.int32, (Q, Q), 1)
    differ = t_id ^ s_id
    level_id = jnp.zeros((Q, Q), jnp.int32)
    for bit in range(sb):
        level_id = level_id + (differ >= (1 << bit)).astype(jnp.int32)
    lev[...] = jnp.where(t_id >= s_id, level_id, -1)
    for c in range(2):
        scores[c] = dot(cout_ref[spans[c], :], bin_ref[spans[c], :], 1, 1)
    for h in range(heads):
        for c in range(2):
            steprow[h, c : c + 1, :] = step_ref[h : h + 1, spans[c]]
    score_sum[...] = jnp.zeros_like(score_sum)
    out_acc[...] = jnp.zeros_like(out_acc)
    tab[...] = jnp.zeros_like(tab)
    fcs[...] = jnp.zeros_like(fcs)
    fsrc[...] = jnp.zeros_like(fsrc)

    def near(p, carry):
        lv = lev[...]
        hit = [lv == level for level in range(sb + 1)]
        weights = []
        for j in range(per):
            rows = []
            for k in range(2):
                acc = jnp.zeros((Q, Q), F32)
                for level in range(sb + 1):
                    acc = jnp.where(
                        hit[level], table_ref[p * per + j, k, level] * scale_of(level), acc
                    )
                rows.append(acc)
            weights.append(rows)
        terms = [[jnp.zeros((Q, Q), F32) for k in range(2)] for j in range(per)]
        for c in range(2):
            x = x_ref[spans[c], cols(p)]
            g = g_ref[spans[c], cols(p)]
            xs = jnp.concatenate([x * half_b[j] for j in range(per)], axis=0)
            gs = jnp.concatenate([g * half_b[j] for j in range(per)], axis=0)
            mg = dot(gs, x, 1, 1)
            is_one = clsb[spans[c], :] > 0.5
            score = scores[c]
            mixes = []
            total_sg = score_sum[c]
            for j in range(per):
                head = p * per + j
                step = steprow[head, c : c + 1, :]
                weight = jnp.where(is_one, weights[j][1], weights[j][0])
                ws = weight * step
                mgj = mg[j * Q : (j + 1) * Q]
                mixes.append((score * ws).astype(BF16))
                total_sg = total_sg + mgj * ws
                graded = mgj * score
                sgrow[head, c : c + 1, :] = jnp.sum(graded * weight, axis=0, keepdims=True)
                term = graded * step
                terms[j][0] = terms[j][0] + jnp.where(is_one, 0.0, term)
                terms[j][1] = terms[j][1] + jnp.where(is_one, term, 0.0)
            score_sum[c] = total_sg
            nout[p, spans[c], :] = dot(jnp.concatenate(mixes, axis=1), xs, 1, 0)
            nback[p, spans[c], :] = dot(jnp.concatenate(mixes, axis=0), gs, 0, 0)
        for j in range(per):
            for k in range(2):
                term = terms[j][k]
                for level in range(sb + 1):
                    if level <= 3:
                        value = jnp.sum(jnp.where(hit[level], term, 0.0), axis=0, keepdims=True)
                    else:
                        size = 1 << (level - 1)
                        value = jnp.zeros((1, LANES), F32)
                        for odd in range(1, Q // size, 2):
                            rows = jnp.sum(term[odd * size : (odd + 1) * size], axis=0, keepdims=True)
                            value = jnp.where(lane // size == odd - 1, rows, value)
                    tab[k * levels + level, pl.ds(p * per + j, 1), :] = value
        return carry
    def table_of(some):
        summed = jnp.zeros((heads, LANES), F32)
        for k in range(2):
            for level in some:
                at = k * levels + level
                col = jnp.sum(tab[at], axis=1, keepdims=True)
                summed = jnp.where(lane == at, col * (scale_of(level) / math.sqrt(total)), summed)
        return summed

    def forward_map(p, c):
        cs = []
        for k in range(2):
            value = fcs[k, p]
            if c == 1:
                value = value + wrow(p, k, mid) * s0[p]
            cs.append(value.astype(BF16))
        return jnp.concatenate(cs, axis=0)

    def backward_map(p, c):
        src = fsrc[p]
        if c == 0:
            src = src + wrow(p, 0, mid) * q1[0, p] + wrow(p, 1, mid) * q1[1, p]
        return src.astype(BF16)

    def map_forward(p):
        for c in range(2):
            cs = forward_map(p, c)
            maps[c, p] = cs
            out_acc[c] = out_acc[c] + dot(g_ref[spans[c], cols(p)], cs, 1, 1)

    def values_forward(p):
        for c in range(2):
            read = dot(mo2[c], maps[c, p], 1, 0)
            out_ref[spans[c], cols(p)] = (nout[p, spans[c], :] + read).astype(BF16)

    def map_backward(p):
        for c in range(2):
            src = backward_map(p, c)
            source_maps[c, p] = src
            grad[0, c] = grad[0, c] + dot(scaled[p, spans[c], :], src, 1, 1)

    def values_backward(p):
        for c in range(2):
            vg = dot(bin_ref[spans[c], :], source_maps[c, p], 1, 0)
            xg_ref[spans[c], cols(p)] = (
                nback[p, spans[c], :] + stepx[p, spans[c], :] * vg
            ).astype(BF16)
            whole = x_ref[spans[c], cols(p)].astype(F32) * vg
            coarse = whole.astype(BF16)
            fine = (whole - coarse.astype(F32)).astype(BF16)
            far_step = dot(picks, jnp.concatenate([coarse, fine], axis=1), 1, 1)
            for j in range(per):
                at = (p * per + j, slice(c, c + 1), slice(None))
                sgrow[at] = sgrow[at] + far_step[j : j + 1]

    def finish_forward():
        for c in range(2):
            is_one = clsb[spans[c], :] > 0.5
            acc = out_acc[c]
            grad[1, c] = grad[1, c] + jnp.where(is_one, acc[:, state:], acc[:, :state])

    def beside_copy(kind):
        return pltpu.make_async_remote_copy(
            grad.at[kind], core_recv.at[kind], c_ssem.at[kind], c_rsem.at[kind],
            device_id=across(0, 1), device_id_type=MESH,
        )

    def across_copy(kind, i, other, slot, part):
        return pltpu.make_async_remote_copy(
            x_recv.at[kind, group, low], x_recv.at[kind, slot, part],
            x_ssem.at[kind, i, other], x_rsem.at[kind, i, other],
            device_id=across(i, other), device_id_type=MESH,
        )

    def sum_beside(kind):
        beside_copy(kind).wait_recv()
        for c in range(2):
            x_recv[kind, group, c] = (grad[kind, c] + core_recv[kind, c]).astype(BF16)
        for i in range(1, groups):
            for other in range(2):
                across_copy(kind, i, other, group, low).start()

    def sum_across(kind):
        for i in range(1, groups):
            slot = lax.rem(group - i + groups, groups)
            for other in range(2):
                part = 1 - low if other else low
                across_copy(kind, i, other, slot, part).wait_recv()

    def whole_sum(kind, c):
        whole = x_recv[kind, 0, c].astype(F32)
        for i in range(1, groups):
            whole = whole + x_recv[kind, i, c].astype(F32)
        return whole

    for stage in range(nb):

        def rounds(p, stage=stage):
            if stage < nb - 1:
                primary(stage, p)
            if stage == 0:
                near(p, 0)
                for k in range(2):
                    put_rows(k, mid, p, jnp.sum(s0[p] * q1[k, p], axis=0, keepdims=True))
            if stage >= 1:
                secondary(stage - 1, p)
        each(rounds)
        if stage == 0:
            for c in range(2):
                sgb = score_sum[c].astype(BF16)
                grad[0, c] = dot(sgb, cout_ref[spans[c], :], 0, 0)
                grad[1, c] = dot(sgb, bin_ref[spans[c], :], 1, 0)
            near_sum[...] = table_of(range(mid + 1))
            for b in range(nb - 1):
                pl.semaphore_wait(known.at[b], 1)
                if b + 1 < nb - 1:
                    tell(b + 1)


    @pl.when(inner)
    def _():
        def hand_on(p, carry):
            @pl.when(top == 0)
            def _():
                c_last(0, p).wait_recv()
                c_relay(p).start()

            @pl.when(top == 1)
            def _():
                f_last(0, p).wait_recv()
                f_relay(p).start()

            return carry

        lax.fori_loop(0, relayed, hand_on, 0)

    def table_copy(i):
        return pltpu.make_async_remote_copy(
            tsend, trecv.at[i], t_ssem.at[i], t_rsem.at[i],
            device_id={"seq": device ^ i}, device_id_type=MESH,
        )

    def send_table():
        table_sum = near_sum[...] + table_of(range(far0, levels))
        tsend[:heads, :] = table_sum
        trecv[0, :heads, :] = table_sum
        for i in reversed(range(1, 1 << nb)):
            table_copy(i).start()

    @pl.when(top == 0)
    def _():
        send_table()

        def forward(p):
            map_forward(p)
            values_forward(p)

        each(forward)
        finish_forward()
        beside_copy(1).start()

    def last_values(p):
        values_backward(p)

        @pl.when(top == 1)
        def _():
            values_forward(p)

    def last_kind(p, carry):
        @pl.when(top == 1)
        def _():
            take_f(nb - 1, p)

        @pl.when(top == 0)
        def _():
            for b in range(nb - 1):
                take_own(b, p)

            @pl.when(p == 0)
            def _():
                sum_beside(1)

            take_own(nb - 1, p)
            map_backward(p)

        return carry

    lax.fori_loop(0, pairs, last_kind, 0)

    @pl.when(top == 1)
    def _():
        send_table()
        each(map_forward)
        finish_forward()
        beside_copy(1).start()

        def backward(p):
            for b in range(nb - 1):
                take_own(b, p)
            map_backward(p)

        each(backward)

    beside_copy(0).start()

    @pl.when(top == 1)
    def _():
        sum_beside(1)

    sum_beside(0)
    each(last_values)
    for h in range(heads):
        for c in range(2):
            sg_ref[h : h + 1, spans[c]] = sgrow[h, c : c + 1, :]
    sum_across(1)
    for b in range(end):

        def drain(p, b=b):
            @pl.when(f_sent[b])
            def _():
                f_copy(b, p).wait_send()

            @pl.when(c_sent[b])
            def _():
                r_copy(b, 2, p).wait_send()

            for slot in range(min(2, nb - 1 - b)):

                @pl.when(high_sent[b] if slot == 0 else count[b] > slot)
                def _(slot=slot):
                    r_copy(b, slot, p).wait_send()

        each(drain)

    def drain_last(p, copy, relay):
        copy(0, p).wait_send()

        @pl.when(p >= relayed)
        def _():
            copy(1, p).wait_send()

        @pl.when(p < relayed)
        def _():
            relay(p).wait_send()

    @pl.when(f_sent[end])
    def _():
        each(lambda p: drain_last(p, f_last, c_relay))

    @pl.when(c_sent[end])
    def _():
        each(lambda p: drain_last(p, c_last, f_relay))

    sum_across(0)
    for i in range(1, 1 << nb):
        table_copy(i).wait_recv()
    table_sum = trecv[device, :heads, :]
    for owner in range(1, 1 << nb):
        table_sum = table_sum + trecv[device ^ owner, :heads, :]
    for k in range(2):
        tg_ref[:, k, :] = table_sum[:, k * levels : (k + 1) * levels]

    for kind, ref in ((0, ing_ref), (1, outg_ref)):
        for c in range(2):
            ref[spans[c], :] = whole_sum(kind, c)

    for kind in range(2):
        beside_copy(kind).wait_send()
        for i in range(1, groups):
            for other in range(2):
                across_copy(kind, i, other, group, low).wait_send()
    for i in range(1, 1 << nb):
        table_copy(i).wait_send()


def write_out(*refs):
    sem = refs[-1]
    copies = [pltpu.make_async_copy(refs[i], refs[6 + i], sem.at[i]) for i in range(6)]
    for copy in copies:
        copy.start()
    for copy in copies:
        copy.wait()


def local(inputs, step_sizes, input_map, output_map, level_table, token_class, cotangent):
    tokens, state = input_map.shape
    heads = step_sizes.shape[0]
    width = inputs.shape[1] // heads
    levels = level_table.shape[2]
    n_seq = lax.axis_size("seq")
    n_head = lax.axis_size("head")
    nb = n_seq.bit_length() - 1
    per = LANES // width
    pairs = heads // per
    assert tokens == 2 * Q and heads % per == 0 and n_head % 2 == 0 and nb > 2
    assert level_table.shape[1] == 2 and state == Q and 2 * levels <= LANES
    dims = (heads, width, tokens, state, levels, nb, n_head, float(tokens * n_seq))
    vmem = pl.BlockSpec(memory_space=pltpu.VMEM)
    hbm = pl.BlockSpec(memory_space=pltpu.HBM)
    dma = pltpu.SemaphoreType.DMA
    unit = (pairs, state, LANES)
    tall = (pairs, tokens, LANES)
    padded = -(-heads // 16) * 16
    placed = [
        pltpu.with_memory_space_constraint(a, pltpu.HBM)
        for a in (
            inputs, step_sizes, input_map, output_map, level_table,
            token_class.reshape(1, tokens), cotangent,
        )
    ]
    results = pl.pallas_call(
        functools.partial(kernel, dims),
        out_shape=(
            jax.ShapeDtypeStruct(inputs.shape, BF16),
            jax.ShapeDtypeStruct(inputs.shape, BF16),
            jax.ShapeDtypeStruct(step_sizes.shape, F32),
            jax.ShapeDtypeStruct(input_map.shape, F32),
            jax.ShapeDtypeStruct(output_map.shape, F32),
            jax.ShapeDtypeStruct(level_table.shape, F32),
        ),
        in_specs=[hbm] * 7,
        out_specs=(vmem,) * 6,
        scratch_shapes=[
            pltpu.VMEM((padded, tokens), F32),
            pltpu.VMEM((tokens, 3 * padded), BF16),
            pltpu.VMEM((2, state, Q), BF16),
            pltpu.VMEM((2, 2 * state, Q), BF16),
            pltpu.VMEM(tall, F32),
            pltpu.VMEM(tall, BF16),
            pltpu.VMEM((tokens, LANES), F32),
            pltpu.VMEM((Q, Q), jnp.int32),
            pltpu.VMEM((2, Q, Q), F32),
            pltpu.VMEM((2, Q, 2 * state), BF16),
            pltpu.VMEM(unit, F32),
            pltpu.VMEM((2, *unit), F32),
            pltpu.VMEM((2, *unit), F32),
            pltpu.VMEM(unit, F32),
            pltpu.VMEM((2, *unit), F32),
            pltpu.VMEM((2, *unit), F32),
            pltpu.VMEM(unit, F32),
            pltpu.VMEM(tall, F32),
            pltpu.VMEM(tall, F32),
            pltpu.VMEM((2, Q, Q), F32),
            pltpu.VMEM((2, 2, Q, state), F32),
            pltpu.VMEM((2, Q, 2 * state), F32),
            pltpu.VMEM((2 * levels, heads, LANES), F32),
            pltpu.VMEM((nb, *unit), BF16),
            pltpu.VMEM((nb, *unit), BF16),
            pltpu.VMEM((nb, 3, *unit), BF16),
            pltpu.VMEM((nb, 3, *unit), BF16),
            pltpu.VMEM((2, 2, Q, state), F32),
            pltpu.VMEM((2, n_head // 2, 2, Q, state), BF16),
            pltpu.VMEM((2, pairs, 2 * state, LANES), BF16),
            pltpu.VMEM((2, *unit), BF16),
            pltpu.VMEM((heads, LANES), F32),
            pltpu.VMEM((padded, LANES), F32),
            pltpu.VMEM((n_seq, padded, LANES), F32),
            dma((nb, pairs)),
            dma((nb, pairs)),
            dma((nb, 3, pairs)),
            dma((nb, 3, pairs)),
            dma((2,)),
            dma((2,)),
            dma((2, n_head // 2, 2)),
            dma((2, n_head // 2, 2)),
            dma((n_seq,)),
            dma((n_seq,)),
            dma((2, pairs)),
            dma((pairs,)),
            dma((pairs,)),
            dma((pairs,)),
            pltpu.SemaphoreType.REGULAR((nb,)),
            pltpu.VMEM((heads, 2, LANES), F32),
            pltpu.VMEM((heads, 2, LANES), F32),
            pltpu.VMEM(inputs.shape, BF16),
            pltpu.VMEM(step_sizes.shape, F32),
            pltpu.VMEM(input_map.shape, BF16),
            pltpu.VMEM(output_map.shape, BF16),
            pltpu.VMEM((1, tokens), jnp.int32),
            pltpu.VMEM(cotangent.shape, BF16),
            pltpu.SMEM(level_table.shape, F32),
            dma((7,)),
        ],
        compiler_params=pltpu.CompilerParams(
            collective_id=0, has_side_effects=True, vmem_limit_bytes=48 << 20
        ),
    )(*placed)
    return pl.pallas_call(
        write_out,
        out_shape=tuple(jax.ShapeDtypeStruct(r.shape, r.dtype) for r in results),
        in_specs=[vmem] * 6,
        out_specs=(hbm,) * 6,
        scratch_shapes=[dma((6,))],
        compiler_params=pltpu.CompilerParams(vmem_limit_bytes=8 << 20),
    )(*results)


def solution(mesh):
    placed = (
        P("seq", "head"),
        P("head", "seq"),
        P("seq", None),
        P("seq", None),
        P("head", None, None),
        P("seq"),
        P("seq", "head"),
    )
    return jax.shard_map(
        local,
        mesh=mesh,
        in_specs=placed,
        out_specs=(
            P("seq", "head"),
            P("seq", "head"),
            P("head", "seq"),
            P("seq", None),
            P("seq", None),
            P("head", None, None),
        ),
        check_vma=False,
    )
```

```python
import functools
import math

import jax
import jax.numpy as jnp
from jax import lax
from jax.experimental import pallas as pl
from jax.experimental.pallas import tpu as pltpu
from jax.sharding import PartitionSpec as P

Q = 128
LANES = 128
SUB = 8
F32 = jnp.float32
BF16 = jnp.bfloat16
HIGH = lax.Precision.HIGHEST
MESH = pl.DeviceIdType.MESH


def dot(a, b, ca, cb, precision=None):
    return lax.dot_general(
        a, b, (((ca,), (cb,)), ((), ())), precision=precision, preferred_element_type=F32
    )


def scale_of(level):
    return 1.0 if level == 0 else 2.0 ** (-(level - 1) / 2)


def kernel(
    dims,
    x_hbm,
    step_hbm,
    bin_hbm,
    cout_hbm,
    table_hbm,
    class_hbm,
    g_hbm,
    out_ref,
    xg_ref,
    sg_ref,
    ing_ref,
    outg_ref,
    tg_ref,
    step_pad,
    step_t,
    bin_t,
    mo2_t,
    stepx,
    scaled,
    clsb,
    lev,
    scores,
    mo2,
    s0,
    q1,
    qown,
    frun,
    rrun,
    fcs,
    fsrc,
    nout,
    nback,
    score_sum,
    grad,
    out_acc,
    tab,
    send_f,
    recv_f,
    send_r,
    recv_r,
    core_recv,
    x_recv,
    maps,
    source_maps,
    near_sum,
    tsend,
    trecv,
    f_ssem,
    f_rsem,
    r_ssem,
    r_rsem,
    c_ssem,
    c_rsem,
    x_ssem,
    x_rsem,
    t_ssem,
    t_rsem,
    l_ssem,
    l_rsem,
    h_ssem,
    h_rsem,
    known,
    steprow,
    sgrow,
    x_ref,
    step_ref,
    bin_ref,
    cout_ref,
    class_ref,
    g_ref,
    table_ref,
    in_sem,
):
    heads, width, tokens, state, levels, nb, n_head, total = dims
    per = LANES // width
    pairs = heads // per
    sb = Q.bit_length() - 1
    mid = sb + 1
    far0 = mid + 1
    device = lax.axis_index("seq")
    mine = lax.axis_index("head")
    low = lax.rem(mine, 2)
    group = mine // 2
    groups = n_head // 2

    def across(i, other):
        return {"head": 2 * lax.rem(group + i, groups) + (1 - low if other else low)}

    barrier = pltpu.get_barrier_semaphore()
    for b in range(nb):
        pl.semaphore_signal(
            barrier, inc=1, device_id={"seq": device ^ (1 << b)}, device_id_type=MESH
        )
    for i in range(groups):
        for other in range(2):
            if i or other:
                pl.semaphore_signal(
                    barrier, inc=1, device_id=across(i, other), device_id_type=MESH
                )

    loads = [
        pltpu.make_async_copy(src, dst, in_sem.at[i])
        for i, (src, dst) in enumerate(
            [
                (class_hbm, class_ref),
                (cout_hbm, cout_ref),
                (bin_hbm, bin_ref),
                (step_hbm, step_ref),
                (x_hbm, x_ref),
                (g_hbm, g_ref),
                (table_hbm, table_ref),
            ]
        )
    ]
    for load in loads:
        load.start()

    lane = lax.broadcasted_iota(jnp.int32, (1, LANES), 1)
    halves = [(lane // width == j) for j in range(per)]
    picks = (
        lax.broadcasted_iota(jnp.int32, (16, 2 * LANES), 0)
        == lax.rem(lax.broadcasted_iota(jnp.int32, (16, 2 * LANES), 1), LANES) // width
    ).astype(F32).astype(BF16)
    half_f = [m.astype(F32) for m in halves]
    half_b = [m.astype(F32).astype(BF16) for m in halves]
    padded = step_pad.shape[0]
    relayed = 0

    def wrow(p, k, level):
        row = jnp.zeros((1, LANES), F32)
        for j in range(per):
            row = jnp.where(halves[j], table_ref[p * per + j, k, level] * scale_of(level), row)
        return row

    def cols(p):
        return pl.ds(pl.multiple_of(p * LANES, LANES), LANES)

    spans = [slice(c * Q, (c + 1) * Q) for c in range(2)]
    for load in loads[:4]:
        load.wait()
    row = class_ref[...].astype(F32)
    clsb[...] = dot(
        jnp.broadcast_to(row, (16, tokens)).astype(BF16),
        jnp.full((16, LANES), 0.0625, BF16),
        0,
        0,
    )
    step_pad[...] = jnp.zeros_like(step_pad)
    step_pad[:heads, :] = step_ref[...]
    rest = step_pad[...]
    parts = []
    for _ in range(3):
        parts.append(rest.astype(BF16))
        rest = rest - parts[-1].astype(F32)
    step_t[...] = jnp.concatenate(parts, axis=0).T
    for c in range(2):
        bin_t[c] = bin_ref[spans[c], :].T
        one = clsb[spans[c], :]
        mo = cout_ref[spans[c], :].astype(F32)
        for k, mask in ((0, 1.0 - one), (1, one)):
            masked = (mo * mask).astype(BF16)
            mo2[c, :, k * state : (k + 1) * state] = masked
            mo2_t[c, k * state : (k + 1) * state, :] = masked.T

    bit_of = [(device >> b) & 1 for b in range(nb)]
    above = [device >> (b + 1) for b in range(nb)]
    ones = [(1 << (nb - b - 1)) - 1 for b in range(nb)]
    f_sent = [(bit_of[b] == 0) | (above[b] != ones[b]) for b in range(nb)]
    f_came = [(bit_of[b] == 1) | (above[b] != ones[b]) for b in range(nb)]
    f_on = [above[b] != ones[b] for b in range(nb)]
    count = [sum(bit_of[b + 1 :], jnp.int32(0)) for b in range(nb)]
    by_class = [count[b] >= 3 for b in range(nb)]
    by_level = [count[b] <= 2 for b in range(nb)]
    c_sent = [(bit_of[b] == 1) & by_level[b] for b in range(nb)]
    c_came = [(bit_of[b] == 0) & by_level[b] for b in range(nb)]
    top = bit_of[nb - 1]
    side = bit_of[nb - 2]
    end = nb - 1
    inner = top != side
    f_sent[end - 1] = side == 0
    f_came[end - 1] = side == 1
    f_sent[end] = inner & (top == 0)
    f_came[end] = top == 1
    c_sent[end] = inner & (top == 1)
    high_sent = [count[b] >= 1 for b in range(nb)]
    high_came = list(high_sent)
    high_sent[end - 1] = (top == 1) & (side == 1)
    high_came[end - 1] = (top == 1) & (side == 0)

    def f_copy(b, p):
        return pltpu.make_async_remote_copy(
            send_f.at[b, p], recv_f.at[b, p], f_ssem.at[b, p], f_rsem.at[b, p],
            device_id={"seq": device ^ (1 << b)}, device_id_type=MESH,
        )

    def r_copy(b, slot, p):
        return pltpu.make_async_remote_copy(
            send_r.at[b, slot, p], recv_r.at[b, slot, p],
            r_ssem.at[b, slot, p], r_rsem.at[b, slot, p],
            device_id={"seq": device ^ (1 << b)}, device_id_type=MESH,
        )

    def last_copy(src, dst, far, p):
        return pltpu.make_async_remote_copy(
            src, dst, l_ssem.at[far, p], l_rsem.at[p],
            device_id={"seq": device ^ (2 << (end - 1) if far else 3 << (end - 1))},
            device_id_type=MESH,
        )

    def f_last(far, p):
        return last_copy(send_f.at[end, p], recv_f.at[end, p], far, p)

    def c_last(far, p):
        return last_copy(send_r.at[end, 2, p], recv_r.at[end, 2, p], far, p)

    def relay_copy(ref, p):
        return pltpu.make_async_remote_copy(
            ref, ref, h_ssem.at[p], h_rsem.at[p],
            device_id={"seq": device ^ (1 << (end - 1))}, device_id_type=MESH,
        )

    def f_relay(p):
        return relay_copy(recv_f.at[end, p], p)

    def c_relay(p):
        return relay_copy(recv_r.at[end, 2, p], p)

    def start_last(copy, p):
        copy(0, p).start()

        @pl.when(p >= relayed)
        def _():
            copy(1, p).start()

    def above_rows(b, p, k):
        high = jnp.zeros((1, LANES), F32)
        second = high
        for other in range(b + 1, nb):
            row = wrow(p, k, far0 + other)
            second = jnp.where(bit_of[other] == 1, high, second)
            high = jnp.where(bit_of[other] == 1, row, high)
        return high, second

    def prepare_back(b, p, r0, r1):
        if nb - 1 - b >= 3:

            @pl.when(by_class[b])
            def _():
                send_r[b, 0, p] = r0.astype(BF16)
                send_r[b, 1, p] = r1.astype(BF16)

        if b + 1 < nb:

            @pl.when(by_level[b] & (count[b] >= 1))
            def _():
                high = above_rows(b, p, 0)[0] * r0 + above_rows(b, p, 1)[0] * r1
                rrun[0, p] = high
                send_r[b, 0, p] = high.astype(BF16)

    def prepare_rest(b, p, r0, r1):
        @pl.when(c_sent[b])
        def _():
            own = wrow(p, 0, far0 + b) * r0 + wrow(p, 1, far0 + b) * r1
            send_r[b, 2, p] = own.astype(BF16)

        if b + 2 < nb:

            @pl.when(count[b] == 2)
            def _():
                second = above_rows(b, p, 0)[1] * r0 + above_rows(b, p, 1)[1] * r1
                rrun[1, p] = second
                send_r[b, 1, p] = second.astype(BF16)

    def when_started(flag, copy):
        @pl.when(flag)
        def _():
            copy.start()

    def start_high(b, p):
        if b + 1 < nb:
            when_started(high_sent[b], r_copy(b, 0, p))

    def start_second(b, p):
        if b + 2 < nb:
            when_started(count[b] >= 2, r_copy(b, 1, p))

    def put_rows(k, level, p, value):
        for j in range(per):
            tab[k * levels + level, pl.ds(p * per + j, 1), :] = value * half_f[j]

    def arrive(b, p, copy, relay):
        if b < end:
            copy.wait_recv()
        else:

            @pl.when(p >= relayed)
            def _():
                copy.wait_recv()

            @pl.when((p < relayed) & jnp.logical_not(inner))
            def _():
                relay(p).wait_recv()

    def take_f(b, p):
        @pl.when(f_came[b])
        def _():
            arrive(b, p, f_copy(b, p) if b < end else f_last(0, p), f_relay)
            got = recv_f[b, p].astype(F32)
            if b + 1 < nb:
                grown = frun[p] + got
                frun[p] = grown

                @pl.when(f_sent[b + 1])
                def _():
                    send_f[b + 1, p] = grown.astype(BF16)
                    if b + 1 == end:
                        start_last(f_last, p)
                    else:
                        f_copy(b + 1, p).start()

            @pl.when(bit_of[b] == 1)
            def _():
                for k in range(2):
                    fcs[k, p] = fcs[k, p] + wrow(p, k, far0 + b) * got
                    put_rows(k, far0 + b, p, jnp.sum(got * qown[k, p], axis=0, keepdims=True))

    def take_high(b, p):
        if b + 1 == nb:
            return

        @pl.when(high_came[b] & by_level[b])
        def _():
            r_copy(b, 0, p).wait_recv()
            high = rrun[0, p] + recv_r[b, 0, p].astype(F32)
            rrun[0, p] = high
            last = (count[b + 1] == 0) & (bit_of[b + 1] == 1)

            @pl.when(last)
            def _():
                send_r[b + 1, 2, p] = high.astype(BF16)
                if b + 1 == end:
                    start_last(c_last, p)
                else:
                    r_copy(b + 1, 2, p).start()

            if b + 2 < nb:

                @pl.when(high_sent[b + 1])
                def _():
                    send_r[b + 1, 0, p] = high.astype(BF16)
                    r_copy(b + 1, 0, p).start()

        if nb - 1 - b >= 3:

            @pl.when(by_class[b])
            def _():
                got = []
                for k in range(2):
                    r_copy(b, k, p).wait_recv()
                    got.append(recv_r[b, k, p].astype(F32))
                    rrun[k, p] = rrun[k, p] + got[k]

                @pl.when(bit_of[b] == 0)
                def _():
                    fsrc[p] = (
                        fsrc[p]
                        + wrow(p, 0, far0 + b) * got[0]
                        + wrow(p, 1, far0 + b) * got[1]
                    )

                r0 = rrun[0, p]
                r1 = rrun[1, p]
                prepare_back(b + 1, p, r0, r1)
                start_high(b + 1, p)
                prepare_rest(b + 1, p, r0, r1)
                start_second(b + 1, p)
                when_started(c_sent[b + 1], r_copy(b + 1, 2, p))

    def take_second(b, p):
        if b + 2 >= nb:
            return

        @pl.when(count[b] == 2)
        def _():
            r_copy(b, 1, p).wait_recv()
            second = rrun[1, p] + recv_r[b, 1, p].astype(F32)
            rrun[1, p] = second

            @pl.when(bit_of[b + 1] == 1)
            def _():
                send_r[b + 1, 2, p] = second.astype(BF16)
                r_copy(b + 1, 2, p).start()

            if b + 3 < nb:

                @pl.when(bit_of[b + 1] == 0)
                def _():
                    send_r[b + 1, 1, p] = second.astype(BF16)
                    r_copy(b + 1, 1, p).start()

    def take_own(b, p):
        @pl.when(c_came[b])
        def _():
            arrive(b, p, r_copy(b, 2, p) if b < end else c_last(0, p), c_relay)
            fsrc[p] = fsrc[p] + recv_r[b, 2, p].astype(F32)

    def primary(b, p):
        @pl.when(top == 0)
        def _():
            take_f(b, p)

        @pl.when(top == 1)
        def _():
            take_high(b, p)

    def secondary(b, p):
        @pl.when(top == 0)
        def _():
            take_high(b, p)

        take_second(b, p)

        @pl.when(top == 1)
        def _():
            take_f(b, p)

    def sources(p):
        picks = (
            lax.rem(lax.broadcasted_iota(jnp.int32, step_t.shape[1:] + (LANES,), 0), padded)
            == p * per + lax.broadcasted_iota(jnp.int32, step_t.shape[1:] + (LANES,), 1) // width
        ).astype(F32)
        grown = dot(step_t[...], picks.astype(BF16), 1, 0)
        sc = (x_ref[:, cols(p)].astype(F32) * grown).astype(BF16)
        st = [dot(bin_t[c], sc[spans[c]], 1, 0) for c in range(2)]
        block = st[0] + st[1]
        send_f[0, p] = block.astype(BF16)
        when_started(f_sent[0], f_copy(0, p))
        stepx[p] = grown
        scaled[p] = sc
        s0[p] = st[0]
        frun[p] = block

    def queries(p):
        q = [dot(mo2_t[c], g_ref[spans[c], cols(p)], 1, 0) for c in range(2)]
        both = [q[0][k * state : (k + 1) * state] + q[1][k * state : (k + 1) * state] for k in range(2)]
        if nb > 3:
            for k in range(2):
                rrun[k, p] = both[k]
        prepare_back(0, p, *both)
        start_high(0, p)
        if nb > 3:
            when_started(by_class[0], r_copy(0, 1, p))
        for k in range(2):
            q1[k, p] = q[1][k * state : (k + 1) * state]
            qown[k, p] = both[k]

    def rest_of(p):
        prepare_rest(0, p, qown[0, p], qown[1, p])
        if nb > 2:
            when_started(count[0] == 2, r_copy(0, 1, p))

    def each(body):
        def step(p, carry):
            body(p)
            return carry

        lax.fori_loop(0, pairs, step, 0)

    for load in loads[4:]:
        load.wait()
    pl.semaphore_wait(barrier, nb + n_head - 1)

    def send_own(i, carry):
        second = i >= pairs
        p = jnp.where(second, i - pairs, i)
        forward = second == (top == 1)

        @pl.when(second & (top == 1))
        def _():
            rest_of(p)

        @pl.when(forward)
        def _():
            sources(p)

        @pl.when(jnp.logical_not(forward))
        def _():
            queries(p)

        return carry

    lax.fori_loop(0, 2 * pairs, send_own, 0)

    def last_own(p):
        @pl.when(top == 0)
        def _():
            rest_of(p)

        when_started(c_sent[0], r_copy(0, 2, p))

    each(last_own)

    def tell(b):
        pl.semaphore_signal(
            known.at[b], inc=1, device_id={"seq": device ^ (1 << b)}, device_id_type=MESH
        )

    if nb > 1:
        tell(0)

    t_id = lax.broadcasted_iota(jnp.int32, (Q, Q), 0)
    s_id = lax.broadcasted_iota(jnp.int32, (Q, Q), 1)
    differ = t_id ^ s_id
    level_id = jnp.zeros((Q, Q), jnp.int32)
    for bit in range(sb):
        level_id = level_id + (differ >= (1 << bit)).astype(jnp.int32)
    lev[...] = jnp.where(t_id >= s_id, level_id, -1)
    for c in range(2):
        scores[c] = dot(cout_ref[spans[c], :], bin_ref[spans[c], :], 1, 1)
    for h in range(heads):
        for c in range(2):
            steprow[h, c : c + 1, :] = step_ref[h : h + 1, spans[c]]
    score_sum[...] = jnp.zeros_like(score_sum)
    out_acc[...] = jnp.zeros_like(out_acc)
    tab[...] = jnp.zeros_like(tab)
    fcs[...] = jnp.zeros_like(fcs)
    fsrc[...] = jnp.zeros_like(fsrc)

    def near(p, carry):
        lv = lev[...]
        lev8 = lv[:SUB]
        for i in range(1, Q // SUB):
            lev8 = jnp.where(lane // SUB == i, lv[i * SUB : (i + 1) * SUB], lev8)
        hit = [lv == level for level in range(sb + 1)]
        weights = []
        for j in range(per):
            rows = []
            for k in range(2):
                acc = jnp.zeros((Q, Q), F32)
                for level in range(sb + 1):
                    acc = jnp.where(
                        hit[level], table_ref[p * per + j, k, level] * scale_of(level), acc
                    )
                rows.append(acc)
            weights.append(rows)
        terms = [[jnp.zeros((Q, Q), F32) for k in range(2)] for j in range(per)]
        for c in range(2):
            x = x_ref[spans[c], cols(p)]
            g = g_ref[spans[c], cols(p)]
            xs = jnp.concatenate([x * half_b[j] for j in range(per)], axis=0)
            gs = jnp.concatenate([g * half_b[j] for j in range(per)], axis=0)
            mg = dot(gs, x, 1, 1)
            is_one = clsb[spans[c], :] > 0.5
            score = scores[c]
            mixes = []
            total_sg = score_sum[c]
            for j in range(per):
                head = p * per + j
                step = steprow[head, c : c + 1, :]
                weight = jnp.where(is_one, weights[j][1], weights[j][0])
                ws = weight * step
                mgj = mg[j * Q : (j + 1) * Q]
                mixes.append((score * ws).astype(BF16))
                total_sg = total_sg + mgj * ws
                graded = mgj * score
                sgrow[head, c : c + 1, :] = jnp.sum(graded * weight, axis=0, keepdims=True)
                term = graded * step
                terms[j][0] = terms[j][0] + jnp.where(is_one, 0.0, term)
                terms[j][1] = terms[j][1] + jnp.where(is_one, term, 0.0)
            score_sum[c] = total_sg
            nout[p, spans[c], :] = dot(jnp.concatenate(mixes, axis=1), xs, 1, 0)
            nback[p, spans[c], :] = dot(jnp.concatenate(mixes, axis=0), gs, 0, 0)
        for j in range(per):
            for k in range(2):
                term = terms[j][k]
                blocks = [term[i * SUB : (i + 1) * SUB] for i in range(Q // SUB)]
                inside = blocks[0]
                for i in range(1, Q // SUB):
                    inside = jnp.where(lane // SUB == i, blocks[i], inside)
                for level in range(sb + 1):
                    size = 1 << max(level - 1, 0)
                    if size < SUB:
                        value = jnp.where(lev8 == level, inside, 0.0)
                    else:
                        value = jnp.zeros((SUB, LANES), F32)
                        for odd in range(1, Q // size, 2):
                            first = odd * size // SUB
                            rows = sum(blocks[first + 1 : first + size // SUB], blocks[first])
                            value = jnp.where(lane // size == odd - 1, rows, value)
                    tab[k * levels + level, pl.ds(p * per + j, 1), :] = jnp.sum(
                        value, axis=0, keepdims=True
                    )
        return carry
    def table_of(some):
        summed = jnp.zeros((heads, LANES), F32)
        for k in range(2):
            for level in some:
                at = k * levels + level
                col = jnp.sum(tab[at], axis=1, keepdims=True)
                summed = jnp.where(lane == at, col * (scale_of(level) / math.sqrt(total)), summed)
        return summed

    def forward_map(p, c):
        cs = []
        for k in range(2):
            value = fcs[k, p]
            if c == 1:
                value = value + wrow(p, k, mid) * s0[p]
            cs.append(value.astype(BF16))
        return jnp.concatenate(cs, axis=0)

    def backward_map(p, c):
        src = fsrc[p]
        if c == 0:
            src = src + wrow(p, 0, mid) * q1[0, p] + wrow(p, 1, mid) * q1[1, p]
        return src.astype(BF16)

    def map_forward(p):
        for c in range(2):
            cs = forward_map(p, c)
            maps[c, p] = cs
            out_acc[c] = out_acc[c] + dot(g_ref[spans[c], cols(p)], cs, 1, 1)

    def values_forward(p):
        for c in range(2):
            read = dot(mo2[c], maps[c, p], 1, 0)
            out_ref[spans[c], cols(p)] = (nout[p, spans[c], :] + read).astype(BF16)

    def map_backward(p):
        for c in range(2):
            src = backward_map(p, c)
            source_maps[c, p] = src
            grad[0, c] = grad[0, c] + dot(scaled[p, spans[c], :], src, 1, 1)

    def values_backward(p):
        for c in range(2):
            vg = dot(bin_ref[spans[c], :], source_maps[c, p], 1, 0)
            xg_ref[spans[c], cols(p)] = (
                nback[p, spans[c], :] + stepx[p, spans[c], :] * vg
            ).astype(BF16)
            whole = x_ref[spans[c], cols(p)].astype(F32) * vg
            coarse = whole.astype(BF16)
            fine = (whole - coarse.astype(F32)).astype(BF16)
            far_step = dot(picks, jnp.concatenate([coarse, fine], axis=1), 1, 1)
            for j in range(per):
                at = (p * per + j, slice(c, c + 1), slice(None))
                sgrow[at] = sgrow[at] + far_step[j : j + 1]

    def finish_forward():
        for c in range(2):
            is_one = clsb[spans[c], :] > 0.5
            acc = out_acc[c]
            grad[1, c] = grad[1, c] + jnp.where(is_one, acc[:, state:], acc[:, :state])

    def beside_copy(kind):
        return pltpu.make_async_remote_copy(
            grad.at[kind], core_recv.at[kind], c_ssem.at[kind], c_rsem.at[kind],
            device_id=across(0, 1), device_id_type=MESH,
        )

    def across_copy(kind, i, other, slot, part):
        return pltpu.make_async_remote_copy(
            x_recv.at[kind, group, low], x_recv.at[kind, slot, part],
            x_ssem.at[kind, i, other], x_rsem.at[kind, i, other],
            device_id=across(i, other), device_id_type=MESH,
        )

    def sum_beside(kind):
        beside_copy(kind).wait_recv()
        for c in range(2):
            x_recv[kind, group, c] = (grad[kind, c] + core_recv[kind, c]).astype(BF16)
        for i in range(1, groups):
            for other in range(2):
                across_copy(kind, i, other, group, low).start()

    def sum_across(kind):
        for i in range(1, groups):
            slot = lax.rem(group - i + groups, groups)
            for other in range(2):
                part = 1 - low if other else low
                across_copy(kind, i, other, slot, part).wait_recv()

    def whole_sum(kind, c):
        whole = x_recv[kind, 0, c].astype(F32)
        for i in range(1, groups):
            whole = whole + x_recv[kind, i, c].astype(F32)
        return whole

    for stage in range(nb):

        def rounds(p, stage=stage):
            if stage < nb - 1:
                primary(stage, p)
            if stage == 0:
                near(p, 0)
                for k in range(2):
                    put_rows(k, mid, p, jnp.sum(s0[p] * q1[k, p], axis=0, keepdims=True))
            if stage >= 1:
                secondary(stage - 1, p)
        each(rounds)
        if stage == 0:
            for c in range(2):
                sgb = score_sum[c].astype(BF16)
                grad[0, c] = dot(sgb, cout_ref[spans[c], :], 0, 0)
                grad[1, c] = dot(sgb, bin_ref[spans[c], :], 1, 0)
            near_sum[...] = table_of(range(mid + 1))
            for b in range(nb - 1):
                pl.semaphore_wait(known.at[b], 1)
                if b + 1 < nb - 1:
                    tell(b + 1)


    @pl.when(inner)
    def _():
        def hand_on(p, carry):
            @pl.when(top == 0)
            def _():
                c_last(0, p).wait_recv()
                c_relay(p).start()

            @pl.when(top == 1)
            def _():
                f_last(0, p).wait_recv()
                f_relay(p).start()

            return carry

        lax.fori_loop(0, relayed, hand_on, 0)

    def table_copy(i):
        return pltpu.make_async_remote_copy(
            tsend, trecv.at[i], t_ssem.at[i], t_rsem.at[i],
            device_id={"seq": device ^ i}, device_id_type=MESH,
        )

    def send_table():
        table_sum = near_sum[...] + table_of(range(far0, levels))
        tsend[:heads, :] = table_sum
        trecv[0, :heads, :] = table_sum
        for i in reversed(range(1, 1 << nb)):
            table_copy(i).start()

    @pl.when(top == 0)
    def _():
        send_table()

        def forward(p):
            map_forward(p)
            values_forward(p)

        each(forward)
        finish_forward()
        beside_copy(1).start()

    def last_values(p):
        values_backward(p)

        @pl.when(top == 1)
        def _():
            values_forward(p)

    def last_kind(p, carry):
        @pl.when(top == 1)
        def _():
            take_f(nb - 1, p)

        @pl.when(top == 0)
        def _():
            for b in range(nb - 1):
                take_own(b, p)

            @pl.when(p == 0)
            def _():
                sum_beside(1)

            take_own(nb - 1, p)
            map_backward(p)

        return carry

    lax.fori_loop(0, pairs, last_kind, 0)

    @pl.when(top == 1)
    def _():
        send_table()
        each(map_forward)
        finish_forward()
        beside_copy(1).start()

        def backward(p):
            for b in range(nb - 1):
                take_own(b, p)
            map_backward(p)

        each(backward)

    beside_copy(0).start()

    @pl.when(top == 1)
    def _():
        sum_beside(1)

    sum_beside(0)
    each(last_values)
    for h in range(heads):
        for c in range(2):
            sg_ref[h : h + 1, spans[c]] = sgrow[h, c : c + 1, :]
    sum_across(1)
    for b in range(end):

        def drain(p, b=b):
            @pl.when(f_sent[b])
            def _():
                f_copy(b, p).wait_send()

            @pl.when(c_sent[b])
            def _():
                r_copy(b, 2, p).wait_send()

            for slot in range(min(2, nb - 1 - b)):

                @pl.when(high_sent[b] if slot == 0 else count[b] > slot)
                def _(slot=slot):
                    r_copy(b, slot, p).wait_send()

        each(drain)

    def drain_last(p, copy, relay):
        copy(0, p).wait_send()

        @pl.when(p >= relayed)
        def _():
            copy(1, p).wait_send()

        @pl.when(p < relayed)
        def _():
            relay(p).wait_send()

    @pl.when(f_sent[end])
    def _():
        each(lambda p: drain_last(p, f_last, c_relay))

    @pl.when(c_sent[end])
    def _():
        each(lambda p: drain_last(p, c_last, f_relay))

    sum_across(0)
    for i in range(1, 1 << nb):
        table_copy(i).wait_recv()
    table_sum = trecv[device, :heads, :]
    for owner in range(1, 1 << nb):
        table_sum = table_sum + trecv[device ^ owner, :heads, :]
    for k in range(2):
        tg_ref[:, k, :] = table_sum[:, k * levels : (k + 1) * levels]

    for kind, ref in ((0, ing_ref), (1, outg_ref)):
        for c in range(2):
            ref[spans[c], :] = whole_sum(kind, c)

    for kind in range(2):
        beside_copy(kind).wait_send()
        for i in range(1, groups):
            for other in range(2):
                across_copy(kind, i, other, group, low).wait_send()
    for i in range(1, 1 << nb):
        table_copy(i).wait_send()


def write_out(*refs):
    sem = refs[-1]
    copies = [pltpu.make_async_copy(refs[i], refs[6 + i], sem.at[i]) for i in range(6)]
    for copy in copies:
        copy.start()
    for copy in copies:
        copy.wait()


def local(inputs, step_sizes, input_map, output_map, level_table, token_class, cotangent):
    tokens, state = input_map.shape
    heads = step_sizes.shape[0]
    width = inputs.shape[1] // heads
    levels = level_table.shape[2]
    n_seq = lax.axis_size("seq")
    n_head = lax.axis_size("head")
    nb = n_seq.bit_length() - 1
    per = LANES // width
    pairs = heads // per
    assert tokens == 2 * Q and heads % per == 0 and n_head % 2 == 0 and nb > 2
    assert level_table.shape[1] == 2 and state == Q and 2 * levels <= LANES
    dims = (heads, width, tokens, state, levels, nb, n_head, float(tokens * n_seq))
    vmem = pl.BlockSpec(memory_space=pltpu.VMEM)
    hbm = pl.BlockSpec(memory_space=pltpu.HBM)
    dma = pltpu.SemaphoreType.DMA
    unit = (pairs, state, LANES)
    tall = (pairs, tokens, LANES)
    padded = -(-heads // 16) * 16
    placed = [
        pltpu.with_memory_space_constraint(a, pltpu.HBM)
        for a in (
            inputs, step_sizes, input_map, output_map, level_table,
            token_class.reshape(1, tokens), cotangent,
        )
    ]
    results = pl.pallas_call(
        functools.partial(kernel, dims),
        out_shape=(
            jax.ShapeDtypeStruct(inputs.shape, BF16),
            jax.ShapeDtypeStruct(inputs.shape, BF16),
            jax.ShapeDtypeStruct(step_sizes.shape, F32),
            jax.ShapeDtypeStruct(input_map.shape, F32),
            jax.ShapeDtypeStruct(output_map.shape, F32),
            jax.ShapeDtypeStruct(level_table.shape, F32),
        ),
        in_specs=[hbm] * 7,
        out_specs=(vmem,) * 6,
        scratch_shapes=[
            pltpu.VMEM((padded, tokens), F32),
            pltpu.VMEM((tokens, 3 * padded), BF16),
            pltpu.VMEM((2, state, Q), BF16),
            pltpu.VMEM((2, 2 * state, Q), BF16),
            pltpu.VMEM(tall, F32),
            pltpu.VMEM(tall, BF16),
            pltpu.VMEM((tokens, LANES), F32),
            pltpu.VMEM((Q, Q), jnp.int32),
            pltpu.VMEM((2, Q, Q), F32),
            pltpu.VMEM((2, Q, 2 * state), BF16),
            pltpu.VMEM(unit, F32),
            pltpu.VMEM((2, *unit), F32),
            pltpu.VMEM((2, *unit), F32),
            pltpu.VMEM(unit, F32),
            pltpu.VMEM((2, *unit), F32),
            pltpu.VMEM((2, *unit), F32),
            pltpu.VMEM(unit, F32),
            pltpu.VMEM(tall, F32),
            pltpu.VMEM(tall, F32),
            pltpu.VMEM((2, Q, Q), F32),
            pltpu.VMEM((2, 2, Q, state), F32),
            pltpu.VMEM((2, Q, 2 * state), F32),
            pltpu.VMEM((2 * levels, heads, LANES), F32),
            pltpu.VMEM((nb, *unit), BF16),
            pltpu.VMEM((nb, *unit), BF16),
            pltpu.VMEM((nb, 3, *unit), BF16),
            pltpu.VMEM((nb, 3, *unit), BF16),
            pltpu.VMEM((2, 2, Q, state), F32),
            pltpu.VMEM((2, n_head // 2, 2, Q, state), BF16),
            pltpu.VMEM((2, pairs, 2 * state, LANES), BF16),
            pltpu.VMEM((2, *unit), BF16),
            pltpu.VMEM((heads, LANES), F32),
            pltpu.VMEM((padded, LANES), F32),
            pltpu.VMEM((n_seq, padded, LANES), F32),
            dma((nb, pairs)),
            dma((nb, pairs)),
            dma((nb, 3, pairs)),
            dma((nb, 3, pairs)),
            dma((2,)),
            dma((2,)),
            dma((2, n_head // 2, 2)),
            dma((2, n_head // 2, 2)),
            dma((n_seq,)),
            dma((n_seq,)),
            dma((2, pairs)),
            dma((pairs,)),
            dma((pairs,)),
            dma((pairs,)),
            pltpu.SemaphoreType.REGULAR((nb,)),
            pltpu.VMEM((heads, 2, LANES), F32),
            pltpu.VMEM((heads, 2, LANES), F32),
            pltpu.VMEM(inputs.shape, BF16),
            pltpu.VMEM(step_sizes.shape, F32),
            pltpu.VMEM(input_map.shape, BF16),
            pltpu.VMEM(output_map.shape, BF16),
            pltpu.VMEM((1, tokens), jnp.int32),
            pltpu.VMEM(cotangent.shape, BF16),
            pltpu.SMEM(level_table.shape, F32),
            dma((7,)),
        ],
        compiler_params=pltpu.CompilerParams(
            collective_id=0, has_side_effects=True, vmem_limit_bytes=48 << 20
        ),
    )(*placed)
    return pl.pallas_call(
        write_out,
        out_shape=tuple(jax.ShapeDtypeStruct(r.shape, r.dtype) for r in results),
        in_specs=[vmem] * 6,
        out_specs=(hbm,) * 6,
        scratch_shapes=[dma((6,))],
        compiler_params=pltpu.CompilerParams(vmem_limit_bytes=8 << 20),
    )(*results)


def solution(mesh):
    placed = (
        P("seq", "head"),
        P("head", "seq"),
        P("seq", None),
        P("seq", None),
        P("head", None, None),
        P("seq"),
        P("seq", "head"),
    )
    return jax.shard_map(
        local,
        mesh=mesh,
        in_specs=placed,
        out_specs=(
            P("seq", "head"),
            P("seq", "head"),
            P("head", "seq"),
            P("seq", None),
            P("seq", None),
            P("head", None, None),
        ),
        check_vma=False,
    )
```

```python
import functools
import math

import jax
import jax.numpy as jnp
from jax import lax
from jax.experimental import pallas as pl
from jax.experimental.pallas import tpu as pltpu
from jax.sharding import PartitionSpec as P

Q = 128
LANES = 128
SUB = 8
F32 = jnp.float32
BF16 = jnp.bfloat16
HIGH = lax.Precision.HIGHEST
MESH = pl.DeviceIdType.MESH


def dot(a, b, ca, cb, precision=None):
    return lax.dot_general(
        a, b, (((ca,), (cb,)), ((), ())), precision=precision, preferred_element_type=F32
    )


def scale_of(level):
    return 1.0 if level == 0 else 2.0 ** (-(level - 1) / 2)


def kernel(
    dims,
    x_hbm,
    step_hbm,
    bin_hbm,
    cout_hbm,
    table_hbm,
    class_hbm,
    g_hbm,
    out_ref,
    xg_ref,
    sg_ref,
    ing_ref,
    outg_ref,
    tg_ref,
    step_pad,
    step_t,
    bin_t,
    mo2_t,
    stepx,
    scaled,
    clsb,
    lev,
    scores,
    mo2,
    s0,
    q1,
    qown,
    frun,
    rrun,
    fcs,
    fsrc,
    nout,
    nback,
    score_sum,
    grad,
    out_acc,
    tab,
    send_f,
    recv_f,
    send_r,
    recv_r,
    core_recv,
    x_recv,
    maps,
    source_maps,
    near_sum,
    tsend,
    trecv,
    f_ssem,
    f_rsem,
    r_ssem,
    r_rsem,
    c_ssem,
    c_rsem,
    x_ssem,
    x_rsem,
    t_ssem,
    t_rsem,
    l_ssem,
    l_rsem,
    known,
    steprow,
    sgrow,
    x_ref,
    step_ref,
    bin_ref,
    cout_ref,
    class_ref,
    g_ref,
    table_ref,
    in_sem,
):
    heads, width, tokens, state, levels, nb, n_head, total = dims
    per = LANES // width
    pairs = heads // per
    sb = Q.bit_length() - 1
    mid = sb + 1
    far0 = mid + 1
    device = lax.axis_index("seq")
    mine = lax.axis_index("head")
    low = lax.rem(mine, 2)
    group = mine // 2
    groups = n_head // 2

    def across(i, other):
        return {"head": 2 * lax.rem(group + i, groups) + (1 - low if other else low)}

    barrier = pltpu.get_barrier_semaphore()
    for b in range(nb):
        pl.semaphore_signal(
            barrier, inc=1, device_id={"seq": device ^ (1 << b)}, device_id_type=MESH
        )
    for i in range(groups):
        for other in range(2):
            if i or other:
                pl.semaphore_signal(
                    barrier, inc=1, device_id=across(i, other), device_id_type=MESH
                )

    loads = [
        pltpu.make_async_copy(src, dst, in_sem.at[i])
        for i, (src, dst) in enumerate(
            [
                (class_hbm, class_ref),
                (cout_hbm, cout_ref),
                (bin_hbm, bin_ref),
                (step_hbm, step_ref),
                (x_hbm, x_ref),
                (g_hbm, g_ref),
                (table_hbm, table_ref),
            ]
        )
    ]
    for load in loads:
        load.start()

    lane = lax.broadcasted_iota(jnp.int32, (1, LANES), 1)
    halves = [(lane // width == j) for j in range(per)]
    picks = (
        lax.broadcasted_iota(jnp.int32, (16, 2 * LANES), 0)
        == lax.rem(lax.broadcasted_iota(jnp.int32, (16, 2 * LANES), 1), LANES) // width
    ).astype(F32).astype(BF16)
    half_f = [m.astype(F32) for m in halves]
    half_b = [m.astype(F32).astype(BF16) for m in halves]
    padded = step_pad.shape[0]

    def wrow(p, k, level):
        row = jnp.zeros((1, LANES), F32)
        for j in range(per):
            row = jnp.where(halves[j], table_ref[p * per + j, k, level] * scale_of(level), row)
        return row

    def cols(p):
        return pl.ds(pl.multiple_of(p * LANES, LANES), LANES)

    t_id = lax.broadcasted_iota(jnp.int32, (Q, Q), 0)
    s_id = lax.broadcasted_iota(jnp.int32, (Q, Q), 1)
    differ = t_id ^ s_id
    level_id = jnp.zeros((Q, Q), jnp.int32)
    for bit in range(sb):
        level_id = level_id + (differ >= (1 << bit)).astype(jnp.int32)
    lev[...] = jnp.where(t_id >= s_id, level_id, -1)
    score_sum[...] = jnp.zeros_like(score_sum)
    out_acc[...] = jnp.zeros_like(out_acc)
    tab[...] = jnp.zeros_like(tab)
    fcs[...] = jnp.zeros_like(fcs)
    fsrc[...] = jnp.zeros_like(fsrc)
    spans = [slice(c * Q, (c + 1) * Q) for c in range(2)]
    for load in loads[:4]:
        load.wait()
    row = class_ref[...].astype(F32)
    clsb[...] = dot(
        jnp.broadcast_to(row, (16, tokens)).astype(BF16),
        jnp.full((16, LANES), 0.0625, BF16),
        0,
        0,
    )
    step_pad[...] = jnp.zeros_like(step_pad)
    step_pad[:heads, :] = step_ref[...]
    rest = step_pad[...]
    parts = []
    for _ in range(3):
        parts.append(rest.astype(BF16))
        rest = rest - parts[-1].astype(F32)
    step_t[...] = jnp.concatenate(parts, axis=0).T
    for c in range(2):
        bin_t[c] = bin_ref[spans[c], :].T
        one = clsb[spans[c], :]
        mo = cout_ref[spans[c], :].astype(F32)
        for k, mask in ((0, 1.0 - one), (1, one)):
            masked = (mo * mask).astype(BF16)
            mo2[c, :, k * state : (k + 1) * state] = masked
            mo2_t[c, k * state : (k + 1) * state, :] = masked.T

    bit_of = [(device >> b) & 1 for b in range(nb)]
    above = [device >> (b + 1) for b in range(nb)]
    ones = [(1 << (nb - b - 1)) - 1 for b in range(nb)]
    f_sent = [(bit_of[b] == 0) | (above[b] != ones[b]) for b in range(nb)]
    f_came = [(bit_of[b] == 1) | (above[b] != ones[b]) for b in range(nb)]
    f_on = [above[b] != ones[b] for b in range(nb)]
    count = [sum(bit_of[b + 1 :], jnp.int32(0)) for b in range(nb)]
    by_class = [count[b] >= 3 for b in range(nb)]
    by_level = [count[b] <= 2 for b in range(nb)]
    c_sent = [(bit_of[b] == 1) & by_level[b] for b in range(nb)]
    c_came = [(bit_of[b] == 0) & by_level[b] for b in range(nb)]
    top = bit_of[nb - 1]
    side = bit_of[nb - 2]
    end = nb - 1
    inner = top != side
    f_sent[end - 1] = side == 0
    f_came[end - 1] = side == 1
    f_sent[end] = inner & (top == 0)
    f_came[end] = top == 1
    c_sent[end] = inner & (top == 1)
    high_sent = [count[b] >= 1 for b in range(nb)]
    high_came = list(high_sent)
    high_sent[end - 1] = (top == 1) & (side == 1)
    high_came[end - 1] = (top == 1) & (side == 0)

    def f_copy(b, p):
        return pltpu.make_async_remote_copy(
            send_f.at[b, p], recv_f.at[b, p], f_ssem.at[b, p], f_rsem.at[b, p],
            device_id={"seq": device ^ (1 << b)}, device_id_type=MESH,
        )

    def r_copy(b, slot, p):
        return pltpu.make_async_remote_copy(
            send_r.at[b, slot, p], recv_r.at[b, slot, p],
            r_ssem.at[b, slot, p], r_rsem.at[b, slot, p],
            device_id={"seq": device ^ (1 << b)}, device_id_type=MESH,
        )

    def last_copy(src, dst, far, p):
        return pltpu.make_async_remote_copy(
            src, dst, l_ssem.at[far, p], l_rsem.at[p],
            device_id={"seq": device ^ (2 << (end - 1) if far else 3 << (end - 1))},
            device_id_type=MESH,
        )

    def f_last(far, p):
        return last_copy(send_f.at[end, p], recv_f.at[end, p], far, p)

    def c_last(far, p):
        return last_copy(send_r.at[end, 2, p], recv_r.at[end, 2, p], far, p)

    def start_last(copy, p):
        for far in range(2):
            copy(far, p).start()

    def above_rows(b, p, k):
        high = jnp.zeros((1, LANES), F32)
        second = high
        for other in range(b + 1, nb):
            row = wrow(p, k, far0 + other)
            second = jnp.where(bit_of[other] == 1, high, second)
            high = jnp.where(bit_of[other] == 1, row, high)
        return high, second

    def prepare_back(b, p, r0, r1):
        if nb - 1 - b >= 3:

            @pl.when(by_class[b])
            def _():
                send_r[b, 0, p] = r0.astype(BF16)
                send_r[b, 1, p] = r1.astype(BF16)

        if b + 1 < nb:

            @pl.when(by_level[b] & (count[b] >= 1))
            def _():
                high = above_rows(b, p, 0)[0] * r0 + above_rows(b, p, 1)[0] * r1
                rrun[0, p] = high
                send_r[b, 0, p] = high.astype(BF16)

    def prepare_rest(b, p, r0, r1):
        @pl.when(c_sent[b])
        def _():
            own = wrow(p, 0, far0 + b) * r0 + wrow(p, 1, far0 + b) * r1
            send_r[b, 2, p] = own.astype(BF16)

        if b + 2 < nb:

            @pl.when(count[b] == 2)
            def _():
                second = above_rows(b, p, 0)[1] * r0 + above_rows(b, p, 1)[1] * r1
                rrun[1, p] = second
                send_r[b, 1, p] = second.astype(BF16)

    def when_started(flag, copy):
        @pl.when(flag)
        def _():
            copy.start()

    def start_high(b, p):
        if b + 1 < nb:
            when_started(high_sent[b], r_copy(b, 0, p))

    def start_second(b, p):
        if b + 2 < nb:
            when_started(count[b] >= 2, r_copy(b, 1, p))

    def put_rows(k, level, p, value):
        for j in range(per):
            tab[k * levels + level, pl.ds(p * per + j, 1), :] = value * half_f[j]

    def take_f(b, p):
        @pl.when(f_came[b])
        def _():
            (f_copy(b, p) if b < end else f_last(0, p)).wait_recv()
            got = recv_f[b, p].astype(F32)
            if b + 1 < nb:
                grown = frun[p] + got
                frun[p] = grown

                @pl.when(f_sent[b + 1])
                def _():
                    send_f[b + 1, p] = grown.astype(BF16)
                    if b + 1 == end:
                        start_last(f_last, p)
                    else:
                        f_copy(b + 1, p).start()

            @pl.when(bit_of[b] == 1)
            def _():
                for k in range(2):
                    fcs[k, p] = fcs[k, p] + wrow(p, k, far0 + b) * got
                    put_rows(k, far0 + b, p, jnp.sum(got * qown[k, p], axis=0, keepdims=True))

    def take_high(b, p):
        if b + 1 == nb:
            return

        @pl.when(high_came[b] & by_level[b])
        def _():
            r_copy(b, 0, p).wait_recv()
            high = rrun[0, p] + recv_r[b, 0, p].astype(F32)
            rrun[0, p] = high
            last = (count[b + 1] == 0) & (bit_of[b + 1] == 1)

            @pl.when(last)
            def _():
                send_r[b + 1, 2, p] = high.astype(BF16)
                if b + 1 == end:
                    start_last(c_last, p)
                else:
                    r_copy(b + 1, 2, p).start()

            if b + 2 < nb:

                @pl.when(high_sent[b + 1])
                def _():
                    send_r[b + 1, 0, p] = high.astype(BF16)
                    r_copy(b + 1, 0, p).start()

        if nb - 1 - b >= 3:

            @pl.when(by_class[b])
            def _():
                got = []
                for k in range(2):
                    r_copy(b, k, p).wait_recv()
                    got.append(recv_r[b, k, p].astype(F32))
                    rrun[k, p] = rrun[k, p] + got[k]

                @pl.when(bit_of[b] == 0)
                def _():
                    fsrc[p] = (
                        fsrc[p]
                        + wrow(p, 0, far0 + b) * got[0]
                        + wrow(p, 1, far0 + b) * got[1]
                    )

                r0 = rrun[0, p]
                r1 = rrun[1, p]
                prepare_back(b + 1, p, r0, r1)
                start_high(b + 1, p)
                prepare_rest(b + 1, p, r0, r1)
                start_second(b + 1, p)
                when_started(c_sent[b + 1], r_copy(b + 1, 2, p))

    def take_second(b, p):
        if b + 2 >= nb:
            return

        @pl.when(count[b] == 2)
        def _():
            r_copy(b, 1, p).wait_recv()
            second = rrun[1, p] + recv_r[b, 1, p].astype(F32)
            rrun[1, p] = second

            @pl.when(bit_of[b + 1] == 1)
            def _():
                send_r[b + 1, 2, p] = second.astype(BF16)
                r_copy(b + 1, 2, p).start()

            if b + 3 < nb:

                @pl.when(bit_of[b + 1] == 0)
                def _():
                    send_r[b + 1, 1, p] = second.astype(BF16)
                    r_copy(b + 1, 1, p).start()

    def take_own(b, p):
        @pl.when(c_came[b])
        def _():
            (r_copy(b, 2, p) if b < end else c_last(0, p)).wait_recv()
            fsrc[p] = fsrc[p] + recv_r[b, 2, p].astype(F32)

    def primary(b, p):
        @pl.when(top == 0)
        def _():
            take_f(b, p)

        @pl.when(top == 1)
        def _():
            take_high(b, p)

    def secondary(b, p):
        @pl.when(top == 0)
        def _():
            take_high(b, p)

        take_second(b, p)

        @pl.when(top == 1)
        def _():
            take_f(b, p)

    def sources(p):
        picks = (
            lax.rem(lax.broadcasted_iota(jnp.int32, step_t.shape[1:] + (LANES,), 0), padded)
            == p * per + lax.broadcasted_iota(jnp.int32, step_t.shape[1:] + (LANES,), 1) // width
        ).astype(F32)
        grown = dot(step_t[...], picks.astype(BF16), 1, 0)
        sc = (x_ref[:, cols(p)].astype(F32) * grown).astype(BF16)
        st = [dot(bin_t[c], sc[spans[c]], 1, 0) for c in range(2)]
        block = st[0] + st[1]
        send_f[0, p] = block.astype(BF16)
        when_started(f_sent[0], f_copy(0, p))
        stepx[p] = grown
        scaled[p] = sc
        s0[p] = st[0]
        frun[p] = block

    def queries(p):
        q = [dot(mo2_t[c], g_ref[spans[c], cols(p)], 1, 0) for c in range(2)]
        both = [q[0][k * state : (k + 1) * state] + q[1][k * state : (k + 1) * state] for k in range(2)]
        if nb > 3:
            for k in range(2):
                rrun[k, p] = both[k]
        prepare_back(0, p, *both)
        start_high(0, p)
        if nb > 3:
            when_started(by_class[0], r_copy(0, 1, p))
        for k in range(2):
            q1[k, p] = q[1][k * state : (k + 1) * state]
            qown[k, p] = both[k]

    def rest_of(p):
        prepare_rest(0, p, qown[0, p], qown[1, p])
        if nb > 2:
            when_started(count[0] == 2, r_copy(0, 1, p))

    def each(body):
        def step(p, carry):
            body(p)
            return carry

        lax.fori_loop(0, pairs, step, 0)

    for load in loads[4:]:
        load.wait()
    pl.semaphore_wait(barrier, nb + n_head - 1)

    def send_own(i, carry):
        second = i >= pairs
        p = jnp.where(second, i - pairs, i)
        forward = second == (top == 1)

        @pl.when(second & (top == 1))
        def _():
            rest_of(p)

        @pl.when(forward)
        def _():
            sources(p)

        @pl.when(jnp.logical_not(forward))
        def _():
            queries(p)

        return carry

    lax.fori_loop(0, 2 * pairs, send_own, 0)

    def last_own(p):
        @pl.when(top == 0)
        def _():
            rest_of(p)

        when_started(c_sent[0], r_copy(0, 2, p))

    each(last_own)

    def tell(b):
        pl.semaphore_signal(
            known.at[b], inc=1, device_id={"seq": device ^ (1 << b)}, device_id_type=MESH
        )

    if nb > 1:
        tell(0)

    for c in range(2):
        scores[c] = dot(cout_ref[spans[c], :], bin_ref[spans[c], :], 1, 1)
    for h in range(heads):
        for c in range(2):
            steprow[h, c : c + 1, :] = step_ref[h : h + 1, spans[c]]
    def near(p, carry):
        lv = lev[...]
        lev8 = lv[:SUB]
        for i in range(1, Q // SUB):
            lev8 = jnp.where(lane // SUB == i, lv[i * SUB : (i + 1) * SUB], lev8)
        own8 = [lane // SUB == i for i in range(Q // SUB)]
        lev16 = jnp.concatenate([lv[i * SUB : i * SUB + 1] for i in range(Q // SUB)], axis=0)
        weights = []
        for j in range(per):
            rows = []
            for k in range(2):
                inner8 = jnp.zeros((SUB, LANES), F32)
                outer = jnp.zeros((Q // SUB, LANES), F32)
                for level in range(sb + 1):
                    scale = table_ref[p * per + j, k, level] * scale_of(level)
                    if (1 << max(level - 1, 0)) < SUB:
                        inner8 = jnp.where(lev8 == level, scale, inner8)
                    else:
                        outer = jnp.where(lev16 == level, scale, outer)
                rows.append(
                    jnp.concatenate(
                        [
                            jnp.where(
                                own8[i],
                                inner8,
                                jnp.broadcast_to(outer[i : i + 1], (SUB, LANES)),
                            )
                            for i in range(Q // SUB)
                        ],
                        axis=0,
                    )
                )
            weights.append(rows)
        terms = [[jnp.zeros((Q, Q), F32) for k in range(2)] for j in range(per)]
        for c in range(2):
            x = x_ref[spans[c], cols(p)]
            g = g_ref[spans[c], cols(p)]
            xs = jnp.concatenate([x * half_b[j] for j in range(per)], axis=0)
            gs = jnp.concatenate([g * half_b[j] for j in range(per)], axis=0)
            mg = dot(gs, x, 1, 1)
            is_one = clsb[spans[c], :] > 0.5
            score = scores[c]
            mixes = []
            total_sg = score_sum[c]
            for j in range(per):
                head = p * per + j
                step = steprow[head, c : c + 1, :]
                weight = jnp.where(is_one, weights[j][1], weights[j][0])
                ws = weight * step
                mgj = mg[j * Q : (j + 1) * Q]
                mixes.append((score * ws).astype(BF16))
                total_sg = total_sg + mgj * ws
                graded = mgj * score
                sgrow[head, c : c + 1, :] = jnp.sum(graded * weight, axis=0, keepdims=True)
                term = graded * step
                terms[j][0] = terms[j][0] + jnp.where(is_one, 0.0, term)
                terms[j][1] = terms[j][1] + jnp.where(is_one, term, 0.0)
            score_sum[c] = total_sg
            nout[p, spans[c], :] = dot(jnp.concatenate(mixes, axis=1), xs, 1, 0)
            nback[p, spans[c], :] = dot(jnp.concatenate(mixes, axis=0), gs, 0, 0)
        for j in range(per):
            for k in range(2):
                term = terms[j][k]
                blocks = [term[i * SUB : (i + 1) * SUB] for i in range(Q // SUB)]
                inside = blocks[0]
                for i in range(1, Q // SUB):
                    inside = jnp.where(lane // SUB == i, blocks[i], inside)
                for level in range(sb + 1):
                    size = 1 << max(level - 1, 0)
                    if size < SUB:
                        value = jnp.where(lev8 == level, inside, 0.0)
                    else:
                        value = jnp.zeros((SUB, LANES), F32)
                        for odd in range(1, Q // size, 2):
                            first = odd * size // SUB
                            rows = sum(blocks[first + 1 : first + size // SUB], blocks[first])
                            value = jnp.where(lane // size == odd - 1, rows, value)
                    tab[k * levels + level, pl.ds(p * per + j, 1), :] = jnp.sum(
                        value, axis=0, keepdims=True
                    )
        return carry
    def table_of(some):
        summed = jnp.zeros((heads, LANES), F32)
        for k in range(2):
            for level in some:
                at = k * levels + level
                col = jnp.sum(tab[at], axis=1, keepdims=True)
                summed = jnp.where(lane == at, col * (scale_of(level) / math.sqrt(total)), summed)
        return summed

    def forward_map(p, c):
        cs = []
        for k in range(2):
            value = fcs[k, p]
            if c == 1:
                value = value + wrow(p, k, mid) * s0[p]
            cs.append(value.astype(BF16))
        return jnp.concatenate(cs, axis=0)

    def backward_map(p, c):
        src = fsrc[p]
        if c == 0:
            src = src + wrow(p, 0, mid) * q1[0, p] + wrow(p, 1, mid) * q1[1, p]
        return src.astype(BF16)

    def map_forward(p):
        for c in range(2):
            cs = forward_map(p, c)
            maps[c, p] = cs
            out_acc[c] = out_acc[c] + dot(g_ref[spans[c], cols(p)], cs, 1, 1)

    def values_forward(p):
        for c in range(2):
            read = dot(mo2[c], maps[c, p], 1, 0)
            out_ref[spans[c], cols(p)] = (nout[p, spans[c], :] + read).astype(BF16)

    def map_backward(p):
        for c in range(2):
            src = backward_map(p, c)
            source_maps[c, p] = src
            grad[0, c] = grad[0, c] + dot(scaled[p, spans[c], :], src, 1, 1)

    def values_backward(p):
        for c in range(2):
            vg = dot(bin_ref[spans[c], :], source_maps[c, p], 1, 0)
            xg_ref[spans[c], cols(p)] = (
                nback[p, spans[c], :] + stepx[p, spans[c], :] * vg
            ).astype(BF16)
            whole = x_ref[spans[c], cols(p)].astype(F32) * vg
            coarse = whole.astype(BF16)
            fine = (whole - coarse.astype(F32)).astype(BF16)
            far_step = dot(picks, jnp.concatenate([coarse, fine], axis=1), 1, 1)
            for j in range(per):
                at = (p * per + j, slice(c, c + 1), slice(None))
                sgrow[at] = sgrow[at] + far_step[j : j + 1]

    def finish_forward():
        for c in range(2):
            is_one = clsb[spans[c], :] > 0.5
            acc = out_acc[c]
            grad[1, c] = grad[1, c] + jnp.where(is_one, acc[:, state:], acc[:, :state])

    def beside_copy(kind):
        return pltpu.make_async_remote_copy(
            grad.at[kind], core_recv.at[kind], c_ssem.at[kind], c_rsem.at[kind],
            device_id=across(0, 1), device_id_type=MESH,
        )

    def across_copy(kind, i, other, slot, part):
        return pltpu.make_async_remote_copy(
            x_recv.at[kind, group, low], x_recv.at[kind, slot, part],
            x_ssem.at[kind, i, other], x_rsem.at[kind, i, other],
            device_id=across(i, other), device_id_type=MESH,
        )

    def sum_beside(kind):
        beside_copy(kind).wait_recv()
        for c in range(2):
            x_recv[kind, group, c] = (grad[kind, c] + core_recv[kind, c]).astype(BF16)
        for i in range(1, groups):
            for other in range(2):
                across_copy(kind, i, other, group, low).start()

    def sum_across(kind):
        for i in range(1, groups):
            slot = lax.rem(group - i + groups, groups)
            for other in range(2):
                part = 1 - low if other else low
                across_copy(kind, i, other, slot, part).wait_recv()

    def whole_sum(kind, c):
        whole = x_recv[kind, 0, c].astype(F32)
        for i in range(1, groups):
            whole = whole + x_recv[kind, i, c].astype(F32)
        return whole

    for stage in range(nb):

        def rounds(p, stage=stage):
            if stage < nb - 1:
                primary(stage, p)
            if stage == 0:
                near(p, 0)
                for k in range(2):
                    put_rows(k, mid, p, jnp.sum(s0[p] * q1[k, p], axis=0, keepdims=True))
            if stage >= 1:
                secondary(stage - 1, p)
        each(rounds)
        if stage == 0:
            for c in range(2):
                sgb = score_sum[c].astype(BF16)
                grad[0, c] = dot(sgb, cout_ref[spans[c], :], 0, 0)
                grad[1, c] = dot(sgb, bin_ref[spans[c], :], 1, 0)
            near_sum[...] = table_of(range(mid + 1))
            for b in range(nb - 1):
                pl.semaphore_wait(known.at[b], 1)
                if b + 1 < nb - 1:
                    tell(b + 1)


    def table_copy(i):
        return pltpu.make_async_remote_copy(
            tsend, trecv.at[i], t_ssem.at[i], t_rsem.at[i],
            device_id={"seq": device ^ i}, device_id_type=MESH,
        )

    def send_table():
        table_sum = near_sum[...] + table_of(range(far0, levels))
        tsend[:heads, :] = table_sum
        trecv[0, :heads, :] = table_sum
        for i in reversed(range(1, 1 << nb)):
            table_copy(i).start()

    @pl.when(top == 0)
    def _():
        send_table()

        def forward(p):
            map_forward(p)
            values_forward(p)

        each(forward)
        finish_forward()
        beside_copy(1).start()

    def last_values(p):
        values_backward(p)

        @pl.when(top == 1)
        def _():
            values_forward(p)

    def last_kind(p, carry):
        @pl.when(top == 1)
        def _():
            take_f(nb - 1, p)

        @pl.when(top == 0)
        def _():
            for b in range(nb - 1):
                take_own(b, p)

            @pl.when(p == 0)
            def _():
                sum_beside(1)

            take_own(nb - 1, p)
            map_backward(p)

        return carry

    lax.fori_loop(0, pairs, last_kind, 0)

    @pl.when(top == 1)
    def _():
        send_table()
        each(map_forward)
        finish_forward()
        beside_copy(1).start()

        def backward(p):
            for b in range(nb - 1):
                take_own(b, p)
            map_backward(p)

        each(backward)

    beside_copy(0).start()

    @pl.when(top == 1)
    def _():
        sum_beside(1)

    sum_beside(0)
    each(last_values)
    for h in range(heads):
        for c in range(2):
            sg_ref[h : h + 1, spans[c]] = sgrow[h, c : c + 1, :]
    sum_across(1)
    for b in range(end):

        def drain(p, b=b):
            @pl.when(f_sent[b])
            def _():
                f_copy(b, p).wait_send()

            @pl.when(c_sent[b])
            def _():
                r_copy(b, 2, p).wait_send()

            for slot in range(min(2, nb - 1 - b)):

                @pl.when(high_sent[b] if slot == 0 else count[b] > slot)
                def _(slot=slot):
                    r_copy(b, slot, p).wait_send()

        each(drain)

    def drain_last(p, copy):
        for far in range(2):
            copy(far, p).wait_send()

    @pl.when(f_sent[end])
    def _():
        each(lambda p: drain_last(p, f_last))

    @pl.when(c_sent[end])
    def _():
        each(lambda p: drain_last(p, c_last))

    sum_across(0)
    for i in range(1, 1 << nb):
        table_copy(i).wait_recv()
    table_sum = trecv[device, :heads, :]
    for owner in range(1, 1 << nb):
        table_sum = table_sum + trecv[device ^ owner, :heads, :]
    for k in range(2):
        tg_ref[:, k, :] = table_sum[:, k * levels : (k + 1) * levels]

    for kind, ref in ((0, ing_ref), (1, outg_ref)):
        for c in range(2):
            ref[spans[c], :] = whole_sum(kind, c)

    for kind in range(2):
        beside_copy(kind).wait_send()
        for i in range(1, groups):
            for other in range(2):
                across_copy(kind, i, other, group, low).wait_send()
    for i in range(1, 1 << nb):
        table_copy(i).wait_send()


def write_out(*refs):
    sem = refs[-1]
    copies = [pltpu.make_async_copy(refs[i], refs[6 + i], sem.at[i]) for i in range(6)]
    for copy in copies:
        copy.start()
    for copy in copies:
        copy.wait()


def local(inputs, step_sizes, input_map, output_map, level_table, token_class, cotangent):
    tokens, state = input_map.shape
    heads = step_sizes.shape[0]
    width = inputs.shape[1] // heads
    levels = level_table.shape[2]
    n_seq = lax.axis_size("seq")
    n_head = lax.axis_size("head")
    nb = n_seq.bit_length() - 1
    per = LANES // width
    pairs = heads // per
    assert tokens == 2 * Q and heads % per == 0 and n_head % 2 == 0 and nb > 2
    assert level_table.shape[1] == 2 and state == Q and 2 * levels <= LANES
    dims = (heads, width, tokens, state, levels, nb, n_head, float(tokens * n_seq))
    vmem = pl.BlockSpec(memory_space=pltpu.VMEM)
    hbm = pl.BlockSpec(memory_space=pltpu.HBM)
    dma = pltpu.SemaphoreType.DMA
    unit = (pairs, state, LANES)
    tall = (pairs, tokens, LANES)
    padded = -(-heads // 16) * 16
    placed = [
        pltpu.with_memory_space_constraint(a, pltpu.HBM)
        for a in (
            inputs, step_sizes, input_map, output_map, level_table,
            token_class.reshape(1, tokens), cotangent,
        )
    ]
    results = pl.pallas_call(
        functools.partial(kernel, dims),
        out_shape=(
            jax.ShapeDtypeStruct(inputs.shape, BF16),
            jax.ShapeDtypeStruct(inputs.shape, BF16),
            jax.ShapeDtypeStruct(step_sizes.shape, F32),
            jax.ShapeDtypeStruct(input_map.shape, F32),
            jax.ShapeDtypeStruct(output_map.shape, F32),
            jax.ShapeDtypeStruct(level_table.shape, F32),
        ),
        in_specs=[hbm] * 7,
        out_specs=(vmem,) * 6,
        scratch_shapes=[
            pltpu.VMEM((padded, tokens), F32),
            pltpu.VMEM((tokens, 3 * padded), BF16),
            pltpu.VMEM((2, state, Q), BF16),
            pltpu.VMEM((2, 2 * state, Q), BF16),
            pltpu.VMEM(tall, F32),
            pltpu.VMEM(tall, BF16),
            pltpu.VMEM((tokens, LANES), F32),
            pltpu.VMEM((Q, Q), jnp.int32),
            pltpu.VMEM((2, Q, Q), F32),
            pltpu.VMEM((2, Q, 2 * state), BF16),
            pltpu.VMEM(unit, F32),
            pltpu.VMEM((2, *unit), F32),
            pltpu.VMEM((2, *unit), F32),
            pltpu.VMEM(unit, F32),
            pltpu.VMEM((2, *unit), F32),
            pltpu.VMEM((2, *unit), F32),
            pltpu.VMEM(unit, F32),
            pltpu.VMEM(tall, F32),
            pltpu.VMEM(tall, F32),
            pltpu.VMEM((2, Q, Q), F32),
            pltpu.VMEM((2, 2, Q, state), F32),
            pltpu.VMEM((2, Q, 2 * state), F32),
            pltpu.VMEM((2 * levels, heads, LANES), F32),
            pltpu.VMEM((nb, *unit), BF16),
            pltpu.VMEM((nb, *unit), BF16),
            pltpu.VMEM((nb, 3, *unit), BF16),
            pltpu.VMEM((nb, 3, *unit), BF16),
            pltpu.VMEM((2, 2, Q, state), F32),
            pltpu.VMEM((2, n_head // 2, 2, Q, state), BF16),
            pltpu.VMEM((2, pairs, 2 * state, LANES), BF16),
            pltpu.VMEM((2, *unit), BF16),
            pltpu.VMEM((heads, LANES), F32),
            pltpu.VMEM((padded, LANES), F32),
            pltpu.VMEM((n_seq, padded, LANES), F32),
            dma((nb, pairs)),
            dma((nb, pairs)),
            dma((nb, 3, pairs)),
            dma((nb, 3, pairs)),
            dma((2,)),
            dma((2,)),
            dma((2, n_head // 2, 2)),
            dma((2, n_head // 2, 2)),
            dma((n_seq,)),
            dma((n_seq,)),
            dma((2, pairs)),
            dma((pairs,)),
            pltpu.SemaphoreType.REGULAR((nb,)),
            pltpu.VMEM((heads, 2, LANES), F32),
            pltpu.VMEM((heads, 2, LANES), F32),
            pltpu.VMEM(inputs.shape, BF16),
            pltpu.VMEM(step_sizes.shape, F32),
            pltpu.VMEM(input_map.shape, BF16),
            pltpu.VMEM(output_map.shape, BF16),
            pltpu.VMEM((1, tokens), jnp.int32),
            pltpu.VMEM(cotangent.shape, BF16),
            pltpu.SMEM(level_table.shape, F32),
            dma((7,)),
        ],
        compiler_params=pltpu.CompilerParams(
            collective_id=0, has_side_effects=True, vmem_limit_bytes=48 << 20
        ),
    )(*placed)
    return pl.pallas_call(
        write_out,
        out_shape=tuple(jax.ShapeDtypeStruct(r.shape, r.dtype) for r in results),
        in_specs=[vmem] * 6,
        out_specs=(hbm,) * 6,
        scratch_shapes=[dma((6,))],
        compiler_params=pltpu.CompilerParams(vmem_limit_bytes=8 << 20),
    )(*results)


def solution(mesh):
    placed = (
        P("seq", "head"),
        P("head", "seq"),
        P("seq", None),
        P("seq", None),
        P("head", None, None),
        P("seq"),
        P("seq", "head"),
    )
    return jax.shard_map(
        local,
        mesh=mesh,
        in_specs=placed,
        out_specs=(
            P("seq", "head"),
            P("seq", "head"),
            P("head", "seq"),
            P("seq", None),
            P("seq", None),
            P("head", None, None),
        ),
        check_vma=False,
    )
```

```python
import functools
import math

import jax
import jax.numpy as jnp
from jax import lax
from jax.experimental import pallas as pl
from jax.experimental.pallas import tpu as pltpu
from jax.sharding import PartitionSpec as P

Q = 128
LANES = 128
SUB = 8
F32 = jnp.float32
BF16 = jnp.bfloat16
HIGH = lax.Precision.HIGHEST
MESH = pl.DeviceIdType.MESH


def dot(a, b, ca, cb, precision=None):
    return lax.dot_general(
        a, b, (((ca,), (cb,)), ((), ())), precision=precision, preferred_element_type=F32
    )


def scale_of(level):
    return 1.0 if level == 0 else 2.0 ** (-(level - 1) / 2)


def kernel(
    dims,
    x_hbm,
    step_hbm,
    bin_hbm,
    cout_hbm,
    table_hbm,
    class_hbm,
    g_hbm,
    out_ref,
    xg_ref,
    sg_ref,
    ing_ref,
    outg_ref,
    tg_ref,
    step_pad,
    step_t,
    bin_t,
    mo2_t,
    stepx,
    scaled,
    clsb,
    lev,
    scores,
    mo2,
    s0,
    q1,
    qown,
    frun,
    rrun,
    fcs,
    fsrc,
    nout,
    nback,
    score_sum,
    grad,
    out_acc,
    tab,
    send_f,
    recv_f,
    send_r,
    recv_r,
    core_recv,
    x_recv,
    maps,
    source_maps,
    near_sum,
    tsend,
    trecv,
    f_ssem,
    f_rsem,
    r_ssem,
    r_rsem,
    c_ssem,
    c_rsem,
    x_ssem,
    x_rsem,
    t_ssem,
    t_rsem,
    l_ssem,
    l_rsem,
    known,
    steprow,
    sgrow,
    x_ref,
    step_ref,
    bin_ref,
    cout_ref,
    class_ref,
    g_ref,
    table_ref,
    in_sem,
):
    heads, width, tokens, state, levels, nb, n_head, total = dims
    per = LANES // width
    pairs = heads // per
    sb = Q.bit_length() - 1
    mid = sb + 1
    far0 = mid + 1
    device = lax.axis_index("seq")
    mine = lax.axis_index("head")
    low = lax.rem(mine, 2)
    group = mine // 2
    groups = n_head // 2

    def across(i, other):
        return {"head": 2 * lax.rem(group + i, groups) + (1 - low if other else low)}

    barrier = pltpu.get_barrier_semaphore()
    for b in range(nb):
        pl.semaphore_signal(
            barrier, inc=1, device_id={"seq": device ^ (1 << b)}, device_id_type=MESH
        )
    for i in range(groups):
        for other in range(2):
            if i or other:
                pl.semaphore_signal(
                    barrier, inc=1, device_id=across(i, other), device_id_type=MESH
                )

    loads = [
        pltpu.make_async_copy(src, dst, in_sem.at[i])
        for i, (src, dst) in enumerate(
            [
                (class_hbm, class_ref),
                (cout_hbm, cout_ref),
                (bin_hbm, bin_ref),
                (step_hbm, step_ref),
                (x_hbm, x_ref),
                (g_hbm, g_ref),
                (table_hbm, table_ref),
            ]
        )
    ]
    for load in loads:
        load.start()

    lane = lax.broadcasted_iota(jnp.int32, (1, LANES), 1)
    halves = [(lane // width == j) for j in range(per)]
    picks = (
        lax.broadcasted_iota(jnp.int32, (16, 2 * LANES), 0)
        == lax.rem(lax.broadcasted_iota(jnp.int32, (16, 2 * LANES), 1), LANES) // width
    ).astype(F32).astype(BF16)
    half_f = [m.astype(F32) for m in halves]
    half_b = [m.astype(F32).astype(BF16) for m in halves]
    padded = step_pad.shape[0]

    def wrow(p, k, level):
        row = jnp.zeros((1, LANES), F32)
        for j in range(per):
            row = jnp.where(halves[j], table_ref[p * per + j, k, level] * scale_of(level), row)
        return row

    def cols(p):
        return pl.ds(pl.multiple_of(p * LANES, LANES), LANES)

    t_id = lax.broadcasted_iota(jnp.int32, (Q, Q), 0)
    s_id = lax.broadcasted_iota(jnp.int32, (Q, Q), 1)
    differ = t_id ^ s_id
    level_id = jnp.zeros((Q, Q), jnp.int32)
    for bit in range(sb):
        level_id = level_id + (differ >= (1 << bit)).astype(jnp.int32)
    lev[...] = jnp.where(t_id >= s_id, level_id, -1)
    score_sum[...] = jnp.zeros_like(score_sum)
    out_acc[...] = jnp.zeros_like(out_acc)
    tab[...] = jnp.zeros_like(tab)
    fcs[...] = jnp.zeros_like(fcs)
    fsrc[...] = jnp.zeros_like(fsrc)
    spans = [slice(c * Q, (c + 1) * Q) for c in range(2)]
    for load in loads[:4]:
        load.wait()
    row = class_ref[...].astype(F32)
    clsb[...] = dot(
        jnp.broadcast_to(row, (16, tokens)).astype(BF16),
        jnp.full((16, LANES), 0.0625, BF16),
        0,
        0,
    )
    step_pad[...] = jnp.zeros_like(step_pad)
    step_pad[:heads, :] = step_ref[...]
    rest = step_pad[...]
    parts = []
    for _ in range(3):
        parts.append(rest.astype(BF16))
        rest = rest - parts[-1].astype(F32)
    step_t[...] = jnp.concatenate(parts, axis=0).T
    for c in range(2):
        bin_t[c] = bin_ref[spans[c], :].T
        one = clsb[spans[c], :]
        mo = cout_ref[spans[c], :].astype(F32)
        for k, mask in ((0, 1.0 - one), (1, one)):
            masked = (mo * mask).astype(BF16)
            mo2[c, :, k * state : (k + 1) * state] = masked
            mo2_t[c, k * state : (k + 1) * state, :] = masked.T

    bit_of = [(device >> b) & 1 for b in range(nb)]
    above = [device >> (b + 1) for b in range(nb)]
    ones = [(1 << (nb - b - 1)) - 1 for b in range(nb)]
    f_sent = [(bit_of[b] == 0) | (above[b] != ones[b]) for b in range(nb)]
    f_came = [(bit_of[b] == 1) | (above[b] != ones[b]) for b in range(nb)]
    f_on = [above[b] != ones[b] for b in range(nb)]
    count = [sum(bit_of[b + 1 :], jnp.int32(0)) for b in range(nb)]
    by_class = [count[b] >= 3 for b in range(nb)]
    by_level = [count[b] <= 2 for b in range(nb)]
    c_sent = [(bit_of[b] == 1) & by_level[b] for b in range(nb)]
    c_came = [(bit_of[b] == 0) & by_level[b] for b in range(nb)]
    top = bit_of[nb - 1]
    side = bit_of[nb - 2]
    end = nb - 1
    inner = top != side
    f_sent[end - 1] = side == 0
    f_came[end - 1] = side == 1
    f_sent[end] = inner & (top == 0)
    f_came[end] = top == 1
    c_sent[end] = inner & (top == 1)
    high_sent = [count[b] >= 1 for b in range(nb)]
    high_came = list(high_sent)
    high_sent[end - 1] = (top == 1) & (side == 1)
    high_came[end - 1] = (top == 1) & (side == 0)

    def f_copy(b, p):
        return pltpu.make_async_remote_copy(
            send_f.at[b, p], recv_f.at[b, p], f_ssem.at[b, p], f_rsem.at[b, p],
            device_id={"seq": device ^ (1 << b)}, device_id_type=MESH,
        )

    def r_copy(b, slot, p):
        return pltpu.make_async_remote_copy(
            send_r.at[b, slot, p], recv_r.at[b, slot, p],
            r_ssem.at[b, slot, p], r_rsem.at[b, slot, p],
            device_id={"seq": device ^ (1 << b)}, device_id_type=MESH,
        )

    def last_copy(src, dst, far, p):
        return pltpu.make_async_remote_copy(
            src, dst, l_ssem.at[far, p], l_rsem.at[p],
            device_id={"seq": device ^ (2 << (end - 1) if far else 3 << (end - 1))},
            device_id_type=MESH,
        )

    def f_last(far, p):
        return last_copy(send_f.at[end, p], recv_f.at[end, p], far, p)

    def c_last(far, p):
        return last_copy(send_r.at[end, 2, p], recv_r.at[end, 2, p], far, p)

    def start_last(copy, p):
        for far in range(2):
            copy(far, p).start()

    def above_rows(b, p, k):
        high = jnp.zeros((1, LANES), F32)
        second = high
        for other in range(b + 1, nb):
            row = wrow(p, k, far0 + other)
            second = jnp.where(bit_of[other] == 1, high, second)
            high = jnp.where(bit_of[other] == 1, row, high)
        return high, second

    def prepare_back(b, p, r0, r1):
        if nb - 1 - b >= 3:

            @pl.when(by_class[b])
            def _():
                send_r[b, 0, p] = r0.astype(BF16)
                send_r[b, 1, p] = r1.astype(BF16)

        if b + 1 < nb:

            @pl.when(by_level[b] & (count[b] >= 1))
            def _():
                high = above_rows(b, p, 0)[0] * r0 + above_rows(b, p, 1)[0] * r1
                rrun[0, p] = high
                send_r[b, 0, p] = high.astype(BF16)

    def prepare_rest(b, p, r0, r1):
        @pl.when(c_sent[b])
        def _():
            own = wrow(p, 0, far0 + b) * r0 + wrow(p, 1, far0 + b) * r1
            send_r[b, 2, p] = own.astype(BF16)

        if b + 2 < nb:

            @pl.when(count[b] == 2)
            def _():
                second = above_rows(b, p, 0)[1] * r0 + above_rows(b, p, 1)[1] * r1
                rrun[1, p] = second
                send_r[b, 1, p] = second.astype(BF16)

    def when_started(flag, copy):
        @pl.when(flag)
        def _():
            copy.start()

    def start_high(b, p):
        if b + 1 < nb:
            when_started(high_sent[b], r_copy(b, 0, p))

    def start_second(b, p):
        if b + 2 < nb:
            when_started(count[b] >= 2, r_copy(b, 1, p))

    def put_rows(k, level, p, value):
        for j in range(per):
            tab[k * levels + level, pl.ds(p * per + j, 1), :] = value * half_f[j]

    def take_f(b, p):
        @pl.when(f_came[b])
        def _():
            (f_copy(b, p) if b < end else f_last(0, p)).wait_recv()
            got = recv_f[b, p].astype(F32)
            if b + 1 < nb:
                grown = frun[p] + got
                frun[p] = grown

                @pl.when(f_sent[b + 1])
                def _():
                    send_f[b + 1, p] = grown.astype(BF16)
                    if b + 1 == end:
                        start_last(f_last, p)
                    else:
                        f_copy(b + 1, p).start()

            @pl.when(bit_of[b] == 1)
            def _():
                for k in range(2):
                    fcs[k, p] = fcs[k, p] + wrow(p, k, far0 + b) * got
                    put_rows(k, far0 + b, p, jnp.sum(got * qown[k, p], axis=0, keepdims=True))

    def take_high(b, p):
        if b + 1 == nb:
            return

        @pl.when(high_came[b] & by_level[b])
        def _():
            r_copy(b, 0, p).wait_recv()
            high = rrun[0, p] + recv_r[b, 0, p].astype(F32)
            rrun[0, p] = high
            last = (count[b + 1] == 0) & (bit_of[b + 1] == 1)

            @pl.when(last)
            def _():
                send_r[b + 1, 2, p] = high.astype(BF16)
                if b + 1 == end:
                    start_last(c_last, p)
                else:
                    r_copy(b + 1, 2, p).start()

            if b + 2 < nb:

                @pl.when(high_sent[b + 1])
                def _():
                    send_r[b + 1, 0, p] = high.astype(BF16)
                    r_copy(b + 1, 0, p).start()

        if nb - 1 - b >= 3:

            @pl.when(by_class[b])
            def _():
                got = []
                for k in range(2):
                    r_copy(b, k, p).wait_recv()
                    got.append(recv_r[b, k, p].astype(F32))
                    rrun[k, p] = rrun[k, p] + got[k]

                @pl.when(bit_of[b] == 0)
                def _():
                    fsrc[p] = (
                        fsrc[p]
                        + wrow(p, 0, far0 + b) * got[0]
                        + wrow(p, 1, far0 + b) * got[1]
                    )

                r0 = rrun[0, p]
                r1 = rrun[1, p]
                prepare_back(b + 1, p, r0, r1)
                start_high(b + 1, p)
                prepare_rest(b + 1, p, r0, r1)
                start_second(b + 1, p)
                when_started(c_sent[b + 1], r_copy(b + 1, 2, p))

    def take_second(b, p):
        if b + 2 >= nb:
            return

        @pl.when(count[b] == 2)
        def _():
            r_copy(b, 1, p).wait_recv()
            second = rrun[1, p] + recv_r[b, 1, p].astype(F32)
            rrun[1, p] = second

            @pl.when(bit_of[b + 1] == 1)
            def _():
                send_r[b + 1, 2, p] = second.astype(BF16)
                r_copy(b + 1, 2, p).start()

            if b + 3 < nb:

                @pl.when(bit_of[b + 1] == 0)
                def _():
                    send_r[b + 1, 1, p] = second.astype(BF16)
                    r_copy(b + 1, 1, p).start()

    def take_own(b, p):
        @pl.when(c_came[b])
        def _():
            (r_copy(b, 2, p) if b < end else c_last(0, p)).wait_recv()
            fsrc[p] = fsrc[p] + recv_r[b, 2, p].astype(F32)

    def primary(b, p):
        @pl.when(top == 0)
        def _():
            take_f(b, p)

        @pl.when(top == 1)
        def _():
            take_high(b, p)

    def secondary(b, p):
        @pl.when(top == 0)
        def _():
            take_high(b, p)

        take_second(b, p)

        @pl.when(top == 1)
        def _():
            take_f(b, p)

    def sources(p):
        picks = (
            lax.rem(lax.broadcasted_iota(jnp.int32, step_t.shape[1:] + (LANES,), 0), padded)
            == p * per + lax.broadcasted_iota(jnp.int32, step_t.shape[1:] + (LANES,), 1) // width
        ).astype(F32)
        grown = dot(step_t[...], picks.astype(BF16), 1, 0)
        sc = (x_ref[:, cols(p)].astype(F32) * grown).astype(BF16)
        st = [dot(bin_t[c], sc[spans[c]], 1, 0) for c in range(2)]
        block = st[0] + st[1]
        send_f[0, p] = block.astype(BF16)
        when_started(f_sent[0], f_copy(0, p))
        stepx[p] = grown
        scaled[p] = sc
        s0[p] = st[0]
        frun[p] = block

    def queries(p):
        q = [dot(mo2_t[c], g_ref[spans[c], cols(p)], 1, 0) for c in range(2)]
        both = [q[0][k * state : (k + 1) * state] + q[1][k * state : (k + 1) * state] for k in range(2)]
        if nb > 3:
            for k in range(2):
                rrun[k, p] = both[k]
        prepare_back(0, p, *both)
        start_high(0, p)
        if nb > 3:
            when_started(by_class[0], r_copy(0, 1, p))
        for k in range(2):
            q1[k, p] = q[1][k * state : (k + 1) * state]
            qown[k, p] = both[k]

    def rest_of(p):
        prepare_rest(0, p, qown[0, p], qown[1, p])
        if nb > 2:
            when_started(count[0] == 2, r_copy(0, 1, p))

    def each(body):
        def step(p, carry):
            body(p)
            return carry

        lax.fori_loop(0, pairs, step, 0)

    for load in loads[4:]:
        load.wait()
    pl.semaphore_wait(barrier, nb + n_head - 1)

    def send_own(i, carry):
        second = i >= pairs
        p = jnp.where(second, i - pairs, i)
        forward = second == (top == 1)

        @pl.when(second & (top == 1))
        def _():
            rest_of(p)

        @pl.when(forward)
        def _():
            sources(p)

        @pl.when(jnp.logical_not(forward))
        def _():
            queries(p)

        return carry

    lax.fori_loop(0, 2 * pairs, send_own, 0)

    def last_own(p):
        @pl.when(top == 0)
        def _():
            rest_of(p)

        when_started(c_sent[0], r_copy(0, 2, p))

    each(last_own)

    def tell(b):
        pl.semaphore_signal(
            known.at[b], inc=1, device_id={"seq": device ^ (1 << b)}, device_id_type=MESH
        )

    if nb > 1:
        tell(0)

    for c in range(2):
        scores[c] = dot(cout_ref[spans[c], :], bin_ref[spans[c], :], 1, 1)
    for h in range(heads):
        for c in range(2):
            steprow[h, c : c + 1, :] = step_ref[h : h + 1, spans[c]]
    def near(p, carry):
        lv = lev[...]
        lev8 = lv[:SUB]
        for i in range(1, Q // SUB):
            lev8 = jnp.where(lane // SUB == i, lv[i * SUB : (i + 1) * SUB], lev8)
        own8 = [lane // SUB == i for i in range(Q // SUB)]
        lev16 = jnp.concatenate([lv[i * SUB : i * SUB + 1] for i in range(Q // SUB)], axis=0)
        weights = []
        for j in range(per):
            rows = []
            for k in range(2):
                inner8 = jnp.zeros((SUB, LANES), F32)
                outer = jnp.zeros((Q // SUB, LANES), F32)
                for level in range(sb + 1):
                    scale = table_ref[p * per + j, k, level] * scale_of(level)
                    if (1 << max(level - 1, 0)) < SUB:
                        inner8 = jnp.where(lev8 == level, scale, inner8)
                    else:
                        outer = jnp.where(lev16 == level, scale, outer)
                rows.append(
                    jnp.concatenate(
                        [
                            jnp.where(
                                own8[i],
                                inner8,
                                jnp.broadcast_to(outer[i : i + 1], (SUB, LANES)),
                            )
                            for i in range(Q // SUB)
                        ],
                        axis=0,
                    )
                )
            weights.append(rows)
        terms = [[jnp.zeros((Q, Q), F32) for k in range(2)] for j in range(per)]
        for c in range(2):
            x = x_ref[spans[c], cols(p)]
            g = g_ref[spans[c], cols(p)]
            xs = jnp.concatenate([x * half_b[j] for j in range(per)], axis=0)
            gs = jnp.concatenate([g * half_b[j] for j in range(per)], axis=0)
            mg = dot(gs, x, 1, 1)
            is_one = clsb[spans[c], :] > 0.5
            score = scores[c]
            mixes = []
            total_sg = score_sum[c]
            for j in range(per):
                head = p * per + j
                step = steprow[head, c : c + 1, :]
                weight = jnp.where(is_one, weights[j][1], weights[j][0])
                ws = weight * step
                mgj = mg[j * Q : (j + 1) * Q]
                mixes.append((score * ws).astype(BF16))
                total_sg = total_sg + mgj * ws
                graded = mgj * score
                sgrow[head, c : c + 1, :] = jnp.sum(graded * weight, axis=0, keepdims=True)
                term = graded * step
                terms[j][0] = terms[j][0] + jnp.where(is_one, 0.0, term)
                terms[j][1] = terms[j][1] + jnp.where(is_one, term, 0.0)
            score_sum[c] = total_sg
            nout[p, spans[c], :] = dot(jnp.concatenate(mixes, axis=1), xs, 1, 0)
            nback[p, spans[c], :] = dot(jnp.concatenate(mixes, axis=0), gs, 0, 0)
        for j in range(per):
            for k in range(2):
                term = terms[j][k]
                blocks = [term[i * SUB : (i + 1) * SUB] for i in range(Q // SUB)]
                inside = blocks[0]
                for i in range(1, Q // SUB):
                    inside = jnp.where(lane // SUB == i, blocks[i], inside)
                for level in range(sb + 1):
                    size = 1 << max(level - 1, 0)
                    if size < SUB:
                        value = jnp.where(lev8 == level, inside, 0.0)
                    else:
                        value = jnp.zeros((SUB, LANES), F32)
                        for odd in range(1, Q // size, 2):
                            first = odd * size // SUB
                            rows = sum(blocks[first + 1 : first + size // SUB], blocks[first])
                            value = jnp.where(lane // size == odd - 1, rows, value)
                    tab[k * levels + level, pl.ds(p * per + j, 1), :] = jnp.sum(
                        value, axis=0, keepdims=True
                    )
        return carry
    def table_of(some):
        summed = jnp.zeros((heads, LANES), F32)
        for k in range(2):
            for level in some:
                at = k * levels + level
                col = jnp.sum(tab[at], axis=1, keepdims=True)
                summed = jnp.where(lane == at, col * (scale_of(level) / math.sqrt(total)), summed)
        return summed

    def forward_map(p, c):
        cs = []
        for k in range(2):
            value = fcs[k, p]
            if c == 1:
                value = value + wrow(p, k, mid) * s0[p]
            cs.append(value.astype(BF16))
        return jnp.concatenate(cs, axis=0)

    def backward_map(p, c):
        src = fsrc[p]
        if c == 0:
            src = src + wrow(p, 0, mid) * q1[0, p] + wrow(p, 1, mid) * q1[1, p]
        return src.astype(BF16)

    def map_forward(p):
        for c in range(2):
            cs = forward_map(p, c)
            maps[c, p] = cs
            out_acc[c] = out_acc[c] + dot(g_ref[spans[c], cols(p)], cs, 1, 1)

    def values_forward(p):
        for c in range(2):
            read = dot(mo2[c], maps[c, p], 1, 0)
            out_ref[spans[c], cols(p)] = (nout[p, spans[c], :] + read).astype(BF16)

    def map_backward(p):
        for c in range(2):
            src = backward_map(p, c)
            source_maps[c, p] = src
            grad[0, c] = grad[0, c] + dot(scaled[p, spans[c], :], src, 1, 1)

    def values_backward(p):
        for c in range(2):
            vg = dot(bin_ref[spans[c], :], source_maps[c, p], 1, 0)
            xg_ref[spans[c], cols(p)] = (
                nback[p, spans[c], :] + stepx[p, spans[c], :] * vg
            ).astype(BF16)
            whole = x_ref[spans[c], cols(p)].astype(F32) * vg
            coarse = whole.astype(BF16)
            fine = (whole - coarse.astype(F32)).astype(BF16)
            far_step = dot(picks, jnp.concatenate([coarse, fine], axis=1), 1, 1)
            for j in range(per):
                at = (p * per + j, slice(c, c + 1), slice(None))
                sgrow[at] = sgrow[at] + far_step[j : j + 1]

    def finish_forward():
        for c in range(2):
            is_one = clsb[spans[c], :] > 0.5
            acc = out_acc[c]
            grad[1, c] = grad[1, c] + jnp.where(is_one, acc[:, state:], acc[:, :state])

    def beside_copy(kind):
        return pltpu.make_async_remote_copy(
            grad.at[kind], core_recv.at[kind], c_ssem.at[kind], c_rsem.at[kind],
            device_id=across(0, 1), device_id_type=MESH,
        )

    def across_copy(kind, i, other, slot, part):
        return pltpu.make_async_remote_copy(
            x_recv.at[kind, group, low], x_recv.at[kind, slot, part],
            x_ssem.at[kind, i, other], x_rsem.at[kind, i, other],
            device_id=across(i, other), device_id_type=MESH,
        )

    def sum_beside(kind):
        beside_copy(kind).wait_recv()
        for c in range(2):
            x_recv[kind, group, c] = (grad[kind, c] + core_recv[kind, c]).astype(BF16)
        for i in range(1, groups):
            for other in range(2):
                across_copy(kind, i, other, group, low).start()

    def sum_across(kind):
        for i in range(1, groups):
            slot = lax.rem(group - i + groups, groups)
            for other in range(2):
                part = 1 - low if other else low
                across_copy(kind, i, other, slot, part).wait_recv()

    def whole_sum(kind, c):
        whole = x_recv[kind, 0, c].astype(F32)
        for i in range(1, groups):
            whole = whole + x_recv[kind, i, c].astype(F32)
        return whole

    for stage in range(nb):

        def rounds(p, stage=stage):
            if stage == 0:
                near(p, 0)
                for k in range(2):
                    put_rows(k, mid, p, jnp.sum(s0[p] * q1[k, p], axis=0, keepdims=True))
            if stage < nb - 1:
                primary(stage, p)
            if stage >= 1:
                secondary(stage - 1, p)
        each(rounds)
        if stage == 0:
            for c in range(2):
                sgb = score_sum[c].astype(BF16)
                grad[0, c] = dot(sgb, cout_ref[spans[c], :], 0, 0)
                grad[1, c] = dot(sgb, bin_ref[spans[c], :], 1, 0)
            near_sum[...] = table_of(range(mid + 1))
            for b in range(nb - 1):
                pl.semaphore_wait(known.at[b], 1)
                if b + 1 < nb - 1:
                    tell(b + 1)


    def table_copy(i):
        return pltpu.make_async_remote_copy(
            tsend, trecv.at[i], t_ssem.at[i], t_rsem.at[i],
            device_id={"seq": device ^ i}, device_id_type=MESH,
        )

    def send_table():
        table_sum = near_sum[...] + table_of(range(far0, levels))
        tsend[:heads, :] = table_sum
        trecv[0, :heads, :] = table_sum
        for i in reversed(range(1, 1 << nb)):
            table_copy(i).start()

    @pl.when(top == 0)
    def _():
        send_table()

        def forward(p):
            map_forward(p)
            values_forward(p)

        each(forward)
        finish_forward()
        beside_copy(1).start()

    def last_values(p):
        values_backward(p)

        @pl.when(top == 1)
        def _():
            values_forward(p)

    def last_kind(p, carry):
        @pl.when(top == 1)
        def _():
            take_f(nb - 1, p)

        @pl.when(top == 0)
        def _():
            for b in range(nb - 1):
                take_own(b, p)

            @pl.when(p == 0)
            def _():
                sum_beside(1)

            take_own(nb - 1, p)
            map_backward(p)

        return carry

    lax.fori_loop(0, pairs, last_kind, 0)

    @pl.when(top == 1)
    def _():
        send_table()
        each(map_forward)
        finish_forward()
        beside_copy(1).start()

        def backward(p):
            for b in range(nb - 1):
                take_own(b, p)
            map_backward(p)

        each(backward)

    beside_copy(0).start()

    @pl.when(top == 1)
    def _():
        sum_beside(1)

    sum_beside(0)
    each(last_values)
    for h in range(heads):
        for c in range(2):
            sg_ref[h : h + 1, spans[c]] = sgrow[h, c : c + 1, :]
    sum_across(1)
    for b in range(end):

        def drain(p, b=b):
            @pl.when(f_sent[b])
            def _():
                f_copy(b, p).wait_send()

            @pl.when(c_sent[b])
            def _():
                r_copy(b, 2, p).wait_send()

            for slot in range(min(2, nb - 1 - b)):

                @pl.when(high_sent[b] if slot == 0 else count[b] > slot)
                def _(slot=slot):
                    r_copy(b, slot, p).wait_send()

        each(drain)

    def drain_last(p, copy):
        for far in range(2):
            copy(far, p).wait_send()

    @pl.when(f_sent[end])
    def _():
        each(lambda p: drain_last(p, f_last))

    @pl.when(c_sent[end])
    def _():
        each(lambda p: drain_last(p, c_last))

    sum_across(0)
    for i in range(1, 1 << nb):
        table_copy(i).wait_recv()
    table_sum = trecv[device, :heads, :]
    for owner in range(1, 1 << nb):
        table_sum = table_sum + trecv[device ^ owner, :heads, :]
    for k in range(2):
        tg_ref[:, k, :] = table_sum[:, k * levels : (k + 1) * levels]

    for kind, ref in ((0, ing_ref), (1, outg_ref)):
        for c in range(2):
            ref[spans[c], :] = whole_sum(kind, c)

    for kind in range(2):
        beside_copy(kind).wait_send()
        for i in range(1, groups):
            for other in range(2):
                across_copy(kind, i, other, group, low).wait_send()
    for i in range(1, 1 << nb):
        table_copy(i).wait_send()


def write_out(*refs):
    sem = refs[-1]
    copies = [pltpu.make_async_copy(refs[i], refs[6 + i], sem.at[i]) for i in range(6)]
    for copy in copies:
        copy.start()
    for copy in copies:
        copy.wait()


def local(inputs, step_sizes, input_map, output_map, level_table, token_class, cotangent):
    tokens, state = input_map.shape
    heads = step_sizes.shape[0]
    width = inputs.shape[1] // heads
    levels = level_table.shape[2]
    n_seq = lax.axis_size("seq")
    n_head = lax.axis_size("head")
    nb = n_seq.bit_length() - 1
    per = LANES // width
    pairs = heads // per
    assert tokens == 2 * Q and heads % per == 0 and n_head % 2 == 0 and nb > 2
    assert level_table.shape[1] == 2 and state == Q and 2 * levels <= LANES
    dims = (heads, width, tokens, state, levels, nb, n_head, float(tokens * n_seq))
    vmem = pl.BlockSpec(memory_space=pltpu.VMEM)
    hbm = pl.BlockSpec(memory_space=pltpu.HBM)
    dma = pltpu.SemaphoreType.DMA
    unit = (pairs, state, LANES)
    tall = (pairs, tokens, LANES)
    padded = -(-heads // 16) * 16
    placed = [
        pltpu.with_memory_space_constraint(a, pltpu.HBM)
        for a in (
            inputs, step_sizes, input_map, output_map, level_table,
            token_class.reshape(1, tokens), cotangent,
        )
    ]
    results = pl.pallas_call(
        functools.partial(kernel, dims),
        out_shape=(
            jax.ShapeDtypeStruct(inputs.shape, BF16),
            jax.ShapeDtypeStruct(inputs.shape, BF16),
            jax.ShapeDtypeStruct(step_sizes.shape, F32),
            jax.ShapeDtypeStruct(input_map.shape, F32),
            jax.ShapeDtypeStruct(output_map.shape, F32),
            jax.ShapeDtypeStruct(level_table.shape, F32),
        ),
        in_specs=[hbm] * 7,
        out_specs=(vmem,) * 6,
        scratch_shapes=[
            pltpu.VMEM((padded, tokens), F32),
            pltpu.VMEM((tokens, 3 * padded), BF16),
            pltpu.VMEM((2, state, Q), BF16),
            pltpu.VMEM((2, 2 * state, Q), BF16),
            pltpu.VMEM(tall, F32),
            pltpu.VMEM(tall, BF16),
            pltpu.VMEM((tokens, LANES), F32),
            pltpu.VMEM((Q, Q), jnp.int32),
            pltpu.VMEM((2, Q, Q), F32),
            pltpu.VMEM((2, Q, 2 * state), BF16),
            pltpu.VMEM(unit, F32),
            pltpu.VMEM((2, *unit), F32),
            pltpu.VMEM((2, *unit), F32),
            pltpu.VMEM(unit, F32),
            pltpu.VMEM((2, *unit), F32),
            pltpu.VMEM((2, *unit), F32),
            pltpu.VMEM(unit, F32),
            pltpu.VMEM(tall, F32),
            pltpu.VMEM(tall, F32),
            pltpu.VMEM((2, Q, Q), F32),
            pltpu.VMEM((2, 2, Q, state), F32),
            pltpu.VMEM((2, Q, 2 * state), F32),
            pltpu.VMEM((2 * levels, heads, LANES), F32),
            pltpu.VMEM((nb, *unit), BF16),
            pltpu.VMEM((nb, *unit), BF16),
            pltpu.VMEM((nb, 3, *unit), BF16),
            pltpu.VMEM((nb, 3, *unit), BF16),
            pltpu.VMEM((2, 2, Q, state), F32),
            pltpu.VMEM((2, n_head // 2, 2, Q, state), BF16),
            pltpu.VMEM((2, pairs, 2 * state, LANES), BF16),
            pltpu.VMEM((2, *unit), BF16),
            pltpu.VMEM((heads, LANES), F32),
            pltpu.VMEM((padded, LANES), F32),
            pltpu.VMEM((n_seq, padded, LANES), F32),
            dma((nb, pairs)),
            dma((nb, pairs)),
            dma((nb, 3, pairs)),
            dma((nb, 3, pairs)),
            dma((2,)),
            dma((2,)),
            dma((2, n_head // 2, 2)),
            dma((2, n_head // 2, 2)),
            dma((n_seq,)),
            dma((n_seq,)),
            dma((2, pairs)),
            dma((pairs,)),
            pltpu.SemaphoreType.REGULAR((nb,)),
            pltpu.VMEM((heads, 2, LANES), F32),
            pltpu.VMEM((heads, 2, LANES), F32),
            pltpu.VMEM(inputs.shape, BF16),
            pltpu.VMEM(step_sizes.shape, F32),
            pltpu.VMEM(input_map.shape, BF16),
            pltpu.VMEM(output_map.shape, BF16),
            pltpu.VMEM((1, tokens), jnp.int32),
            pltpu.VMEM(cotangent.shape, BF16),
            pltpu.SMEM(level_table.shape, F32),
            dma((7,)),
        ],
        compiler_params=pltpu.CompilerParams(
            collective_id=0, has_side_effects=True, vmem_limit_bytes=48 << 20
        ),
    )(*placed)
    return pl.pallas_call(
        write_out,
        out_shape=tuple(jax.ShapeDtypeStruct(r.shape, r.dtype) for r in results),
        in_specs=[vmem] * 6,
        out_specs=(hbm,) * 6,
        scratch_shapes=[dma((6,))],
        compiler_params=pltpu.CompilerParams(vmem_limit_bytes=8 << 20),
    )(*results)


def solution(mesh):
    placed = (
        P("seq", "head"),
        P("head", "seq"),
        P("seq", None),
        P("seq", None),
        P("head", None, None),
        P("seq"),
        P("seq", "head"),
    )
    return jax.shard_map(
        local,
        mesh=mesh,
        in_specs=placed,
        out_specs=(
            P("seq", "head"),
            P("seq", "head"),
            P("head", "seq"),
            P("seq", None),
            P("seq", None),
            P("head", None, None),
        ),
        check_vma=False,
    )
```

```python
import functools
import math

import jax
import jax.numpy as jnp
from jax import lax
from jax.experimental import pallas as pl
from jax.experimental.pallas import tpu as pltpu
from jax.sharding import PartitionSpec as P

Q = 128
LANES = 128
SUB = 8
F32 = jnp.float32
BF16 = jnp.bfloat16
HIGH = lax.Precision.HIGHEST
MESH = pl.DeviceIdType.MESH


def dot(a, b, ca, cb, precision=None):
    return lax.dot_general(
        a, b, (((ca,), (cb,)), ((), ())), precision=precision, preferred_element_type=F32
    )


def scale_of(level):
    return 1.0 if level == 0 else 2.0 ** (-(level - 1) / 2)


def kernel(
    dims,
    x_hbm,
    step_hbm,
    bin_hbm,
    cout_hbm,
    table_hbm,
    class_hbm,
    g_hbm,
    out_ref,
    xg_ref,
    sg_ref,
    ing_ref,
    outg_ref,
    tg_ref,
    step_pad,
    step_t,
    bin_t,
    mo2_t,
    stepx,
    scaled,
    clsb,
    lev,
    scores,
    mo2,
    s0,
    q1,
    qown,
    frun,
    rrun,
    fcs,
    fsrc,
    nout,
    nback,
    score_sum,
    grad,
    out_acc,
    tab,
    send_f,
    recv_f,
    send_r,
    recv_r,
    core_recv,
    x_recv,
    maps,
    source_maps,
    near_sum,
    tsend,
    trecv,
    f_ssem,
    f_rsem,
    r_ssem,
    r_rsem,
    c_ssem,
    c_rsem,
    x_ssem,
    x_rsem,
    t_ssem,
    t_rsem,
    l_ssem,
    l_rsem,
    known,
    steprow,
    sgrow,
    x_ref,
    step_ref,
    bin_ref,
    cout_ref,
    class_ref,
    g_ref,
    table_ref,
    in_sem,
):
    heads, width, tokens, state, levels, nb, n_head, total = dims
    per = LANES // width
    pairs = heads // per
    sb = Q.bit_length() - 1
    mid = sb + 1
    far0 = mid + 1
    device = lax.axis_index("seq")
    mine = lax.axis_index("head")
    low = lax.rem(mine, 2)
    group = mine // 2
    groups = n_head // 2

    def across(i, other):
        return {"head": 2 * lax.rem(group + i, groups) + (1 - low if other else low)}

    barrier = pltpu.get_barrier_semaphore()
    for b in range(nb):
        pl.semaphore_signal(
            barrier, inc=1, device_id={"seq": device ^ (1 << b)}, device_id_type=MESH
        )
    for i in range(groups):
        for other in range(2):
            if i or other:
                pl.semaphore_signal(
                    barrier, inc=1, device_id=across(i, other), device_id_type=MESH
                )

    loads = [
        pltpu.make_async_copy(src, dst, in_sem.at[i])
        for i, (src, dst) in enumerate(
            [
                (class_hbm, class_ref),
                (cout_hbm, cout_ref),
                (bin_hbm, bin_ref),
                (step_hbm, step_ref),
                (x_hbm, x_ref),
                (g_hbm, g_ref),
                (table_hbm, table_ref),
            ]
        )
    ]
    for load in loads:
        load.start()

    lane = lax.broadcasted_iota(jnp.int32, (1, LANES), 1)
    halves = [(lane // width == j) for j in range(per)]
    picks = (
        lax.broadcasted_iota(jnp.int32, (16, 2 * LANES), 0)
        == lax.rem(lax.broadcasted_iota(jnp.int32, (16, 2 * LANES), 1), LANES) // width
    ).astype(F32).astype(BF16)
    half_f = [m.astype(F32) for m in halves]
    half_b = [m.astype(F32).astype(BF16) for m in halves]
    padded = step_pad.shape[0]

    def wrow(p, k, level):
        row = jnp.zeros((1, LANES), F32)
        for j in range(per):
            row = jnp.where(halves[j], table_ref[p * per + j, k, level] * scale_of(level), row)
        return row

    def cols(p):
        return pl.ds(pl.multiple_of(p * LANES, LANES), LANES)

    t_id = lax.broadcasted_iota(jnp.int32, (Q, Q), 0)
    s_id = lax.broadcasted_iota(jnp.int32, (Q, Q), 1)
    differ = t_id ^ s_id
    level_id = jnp.zeros((Q, Q), jnp.int32)
    for bit in range(sb):
        level_id = level_id + (differ >= (1 << bit)).astype(jnp.int32)
    lev[...] = jnp.where(t_id >= s_id, level_id, -1)
    score_sum[...] = jnp.zeros_like(score_sum)
    out_acc[...] = jnp.zeros_like(out_acc)
    tab[...] = jnp.zeros_like(tab)
    fcs[...] = jnp.zeros_like(fcs)
    fsrc[...] = jnp.zeros_like(fsrc)
    spans = [slice(c * Q, (c + 1) * Q) for c in range(2)]
    for load in loads[:4]:
        load.wait()
    row = class_ref[...].astype(F32)
    clsb[...] = dot(
        jnp.broadcast_to(row, (16, tokens)).astype(BF16),
        jnp.full((16, LANES), 0.0625, BF16),
        0,
        0,
    )
    step_pad[...] = jnp.zeros_like(step_pad)
    step_pad[:heads, :] = step_ref[...]
    rest = step_pad[...]
    parts = []
    for _ in range(3):
        parts.append(rest.astype(BF16))
        rest = rest - parts[-1].astype(F32)
    step_t[...] = jnp.concatenate(parts, axis=0).T
    for c in range(2):
        bin_t[c] = bin_ref[spans[c], :].T
        one = clsb[spans[c], :]
        mo = cout_ref[spans[c], :].astype(F32)
        for k, mask in ((0, 1.0 - one), (1, one)):
            masked = (mo * mask).astype(BF16)
            mo2[c, :, k * state : (k + 1) * state] = masked
            mo2_t[c, k * state : (k + 1) * state, :] = masked.T

    bit_of = [(device >> b) & 1 for b in range(nb)]
    above = [device >> (b + 1) for b in range(nb)]
    ones = [(1 << (nb - b - 1)) - 1 for b in range(nb)]
    f_sent = [(bit_of[b] == 0) | (above[b] != ones[b]) for b in range(nb)]
    f_came = [(bit_of[b] == 1) | (above[b] != ones[b]) for b in range(nb)]
    f_on = [above[b] != ones[b] for b in range(nb)]
    count = [sum(bit_of[b + 1 :], jnp.int32(0)) for b in range(nb)]
    by_class = [count[b] >= 3 for b in range(nb)]
    by_level = [count[b] <= 2 for b in range(nb)]
    c_sent = [(bit_of[b] == 1) & by_level[b] for b in range(nb)]
    c_came = [(bit_of[b] == 0) & by_level[b] for b in range(nb)]
    top = bit_of[nb - 1]
    side = bit_of[nb - 2]
    end = nb - 1
    inner = top != side
    f_sent[end - 1] = side == 0
    f_came[end - 1] = side == 1
    f_sent[end] = inner & (top == 0)
    f_came[end] = top == 1
    c_sent[end] = inner & (top == 1)
    high_sent = [count[b] >= 1 for b in range(nb)]
    high_came = list(high_sent)
    high_sent[end - 1] = (top == 1) & (side == 1)
    high_came[end - 1] = (top == 1) & (side == 0)

    def f_copy(b, p):
        return pltpu.make_async_remote_copy(
            send_f.at[b, p], recv_f.at[b, p], f_ssem.at[b, p], f_rsem.at[b, p],
            device_id={"seq": device ^ (1 << b)}, device_id_type=MESH,
        )

    def r_copy(b, slot, p):
        return pltpu.make_async_remote_copy(
            send_r.at[b, slot, p], recv_r.at[b, slot, p],
            r_ssem.at[b, slot, p], r_rsem.at[b, slot, p],
            device_id={"seq": device ^ (1 << b)}, device_id_type=MESH,
        )

    def last_copy(src, dst, far, p):
        return pltpu.make_async_remote_copy(
            src, dst, l_ssem.at[far, p], l_rsem.at[p],
            device_id={"seq": device ^ (2 << (end - 1) if far else 3 << (end - 1))},
            device_id_type=MESH,
        )

    def f_last(far, p):
        return last_copy(send_f.at[end, p], recv_f.at[end, p], far, p)

    def c_last(far, p):
        return last_copy(send_r.at[end, 2, p], recv_r.at[end, 2, p], far, p)

    def start_last(copy, p):
        for far in range(2):
            copy(far, p).start()

    def above_rows(b, p, k):
        high = jnp.zeros((1, LANES), F32)
        second = high
        for other in range(b + 1, nb):
            row = wrow(p, k, far0 + other)
            second = jnp.where(bit_of[other] == 1, high, second)
            high = jnp.where(bit_of[other] == 1, row, high)
        return high, second

    def prepare_back(b, p, r0, r1):
        if nb - 1 - b >= 3:

            @pl.when(by_class[b])
            def _():
                send_r[b, 0, p] = r0.astype(BF16)
                send_r[b, 1, p] = r1.astype(BF16)

        if b + 1 < nb:

            @pl.when(by_level[b] & (count[b] >= 1))
            def _():
                high = above_rows(b, p, 0)[0] * r0 + above_rows(b, p, 1)[0] * r1
                rrun[0, p] = high
                send_r[b, 0, p] = high.astype(BF16)

    def prepare_rest(b, p, r0, r1):
        @pl.when(c_sent[b])
        def _():
            own = wrow(p, 0, far0 + b) * r0 + wrow(p, 1, far0 + b) * r1
            send_r[b, 2, p] = own.astype(BF16)

        if b + 2 < nb:

            @pl.when(count[b] == 2)
            def _():
                second = above_rows(b, p, 0)[1] * r0 + above_rows(b, p, 1)[1] * r1
                rrun[1, p] = second
                send_r[b, 1, p] = second.astype(BF16)

    def when_started(flag, copy):
        @pl.when(flag)
        def _():
            copy.start()

    def start_high(b, p):
        if b + 1 < nb:
            when_started(high_sent[b], r_copy(b, 0, p))

    def start_second(b, p):
        if b + 2 < nb:
            when_started(count[b] >= 2, r_copy(b, 1, p))

    def put_rows(k, level, p, value):
        for j in range(per):
            tab[k * levels + level, pl.ds(p * per + j, 1), :] = value * half_f[j]

    def take_f(b, p):
        @pl.when(f_came[b])
        def _():
            (f_copy(b, p) if b < end else f_last(0, p)).wait_recv()
            got = recv_f[b, p].astype(F32)
            if b + 1 < nb:
                grown = frun[p] + got
                frun[p] = grown

                @pl.when(f_sent[b + 1])
                def _():
                    send_f[b + 1, p] = grown.astype(BF16)
                    if b + 1 == end:
                        start_last(f_last, p)
                    else:
                        f_copy(b + 1, p).start()

            @pl.when(bit_of[b] == 1)
            def _():
                for k in range(2):
                    fcs[k, p] = fcs[k, p] + wrow(p, k, far0 + b) * got
                    put_rows(k, far0 + b, p, jnp.sum(got * qown[k, p], axis=0, keepdims=True))

    def take_high(b, p):
        if b + 1 == nb:
            return

        @pl.when(high_came[b] & by_level[b])
        def _():
            r_copy(b, 0, p).wait_recv()
            high = rrun[0, p] + recv_r[b, 0, p].astype(F32)
            rrun[0, p] = high
            last = (count[b + 1] == 0) & (bit_of[b + 1] == 1)

            @pl.when(last)
            def _():
                send_r[b + 1, 2, p] = high.astype(BF16)
                if b + 1 == end:
                    start_last(c_last, p)
                else:
                    r_copy(b + 1, 2, p).start()

            if b + 2 < nb:

                @pl.when(high_sent[b + 1])
                def _():
                    send_r[b + 1, 0, p] = high.astype(BF16)
                    r_copy(b + 1, 0, p).start()

        if nb - 1 - b >= 3:

            @pl.when(by_class[b])
            def _():
                got = []
                for k in range(2):
                    r_copy(b, k, p).wait_recv()
                    got.append(recv_r[b, k, p].astype(F32))
                    rrun[k, p] = rrun[k, p] + got[k]

                @pl.when(bit_of[b] == 0)
                def _():
                    fsrc[p] = (
                        fsrc[p]
                        + wrow(p, 0, far0 + b) * got[0]
                        + wrow(p, 1, far0 + b) * got[1]
                    )

                r0 = rrun[0, p]
                r1 = rrun[1, p]
                prepare_back(b + 1, p, r0, r1)
                start_high(b + 1, p)
                prepare_rest(b + 1, p, r0, r1)
                start_second(b + 1, p)
                when_started(c_sent[b + 1], r_copy(b + 1, 2, p))

    def take_second(b, p):
        if b + 2 >= nb:
            return

        @pl.when(count[b] == 2)
        def _():
            r_copy(b, 1, p).wait_recv()
            second = rrun[1, p] + recv_r[b, 1, p].astype(F32)
            rrun[1, p] = second

            @pl.when(bit_of[b + 1] == 1)
            def _():
                send_r[b + 1, 2, p] = second.astype(BF16)
                r_copy(b + 1, 2, p).start()

            if b + 3 < nb:

                @pl.when(bit_of[b + 1] == 0)
                def _():
                    send_r[b + 1, 1, p] = second.astype(BF16)
                    r_copy(b + 1, 1, p).start()

    def take_own(b, p):
        @pl.when(c_came[b])
        def _():
            (r_copy(b, 2, p) if b < end else c_last(0, p)).wait_recv()
            fsrc[p] = fsrc[p] + recv_r[b, 2, p].astype(F32)

    def primary(b, p):
        @pl.when(top == 0)
        def _():
            take_f(b, p)

        @pl.when(top == 1)
        def _():
            take_high(b, p)

    def secondary(b, p):
        @pl.when(top == 0)
        def _():
            take_high(b, p)

        take_second(b, p)

        @pl.when(top == 1)
        def _():
            take_f(b, p)

    def sources(p):
        picks = (
            lax.rem(lax.broadcasted_iota(jnp.int32, step_t.shape[1:] + (LANES,), 0), padded)
            == p * per + lax.broadcasted_iota(jnp.int32, step_t.shape[1:] + (LANES,), 1) // width
        ).astype(F32)
        grown = dot(step_t[...], picks.astype(BF16), 1, 0)
        sc = (x_ref[:, cols(p)].astype(F32) * grown).astype(BF16)
        st = [dot(bin_t[c], sc[spans[c]], 1, 0) for c in range(2)]
        block = st[0] + st[1]
        send_f[0, p] = block.astype(BF16)
        when_started(f_sent[0], f_copy(0, p))
        stepx[p] = grown
        scaled[p] = sc
        s0[p] = st[0]
        frun[p] = block

    def queries(p):
        q = [dot(mo2_t[c], g_ref[spans[c], cols(p)], 1, 0) for c in range(2)]
        both = [q[0][k * state : (k + 1) * state] + q[1][k * state : (k + 1) * state] for k in range(2)]
        if nb > 3:
            for k in range(2):
                rrun[k, p] = both[k]
        prepare_back(0, p, *both)
        start_high(0, p)
        if nb > 3:
            when_started(by_class[0], r_copy(0, 1, p))
        for k in range(2):
            q1[k, p] = q[1][k * state : (k + 1) * state]
            qown[k, p] = both[k]

    def rest_of(p):
        prepare_rest(0, p, qown[0, p], qown[1, p])
        if nb > 2:
            when_started(count[0] == 2, r_copy(0, 1, p))

    def each(body):
        def step(p, carry):
            body(p)
            return carry

        lax.fori_loop(0, pairs, step, 0)

    for c in range(2):
        scores[c] = dot(cout_ref[spans[c], :], bin_ref[spans[c], :], 1, 1)
    for h in range(heads):
        for c in range(2):
            steprow[h, c : c + 1, :] = step_ref[h : h + 1, spans[c]]
    for load in loads[4:]:
        load.wait()
    pl.semaphore_wait(barrier, nb + n_head - 1)

    def send_own(i, carry):
        second = i >= pairs
        p = jnp.where(second, i - pairs, i)
        forward = second == (top == 1)

        @pl.when(second & (top == 1))
        def _():
            rest_of(p)

        @pl.when(forward)
        def _():
            sources(p)

        @pl.when(jnp.logical_not(forward))
        def _():
            queries(p)

        return carry

    lax.fori_loop(0, 2 * pairs, send_own, 0)

    def last_own(p):
        @pl.when(top == 0)
        def _():
            rest_of(p)

        when_started(c_sent[0], r_copy(0, 2, p))

    each(last_own)

    def tell(b):
        pl.semaphore_signal(
            known.at[b], inc=1, device_id={"seq": device ^ (1 << b)}, device_id_type=MESH
        )

    if nb > 1:
        tell(0)

    def near(p, carry):
        lv = lev[...]
        lev8 = lv[:SUB]
        for i in range(1, Q // SUB):
            lev8 = jnp.where(lane // SUB == i, lv[i * SUB : (i + 1) * SUB], lev8)
        own8 = [lane // SUB == i for i in range(Q // SUB)]
        lev16 = jnp.concatenate([lv[i * SUB : i * SUB + 1] for i in range(Q // SUB)], axis=0)
        weights = []
        for j in range(per):
            rows = []
            for k in range(2):
                inner8 = jnp.zeros((SUB, LANES), F32)
                outer = jnp.zeros((Q // SUB, LANES), F32)
                for level in range(sb + 1):
                    scale = table_ref[p * per + j, k, level] * scale_of(level)
                    if (1 << max(level - 1, 0)) < SUB:
                        inner8 = jnp.where(lev8 == level, scale, inner8)
                    else:
                        outer = jnp.where(lev16 == level, scale, outer)
                rows.append(
                    jnp.concatenate(
                        [
                            jnp.where(
                                own8[i],
                                inner8,
                                jnp.broadcast_to(outer[i : i + 1], (SUB, LANES)),
                            )
                            for i in range(Q // SUB)
                        ],
                        axis=0,
                    )
                )
            weights.append(rows)
        terms = [[jnp.zeros((Q, Q), F32) for k in range(2)] for j in range(per)]
        for c in range(2):
            x = x_ref[spans[c], cols(p)]
            g = g_ref[spans[c], cols(p)]
            xs = jnp.concatenate([x * half_b[j] for j in range(per)], axis=0)
            gs = jnp.concatenate([g * half_b[j] for j in range(per)], axis=0)
            mg = dot(gs, x, 1, 1)
            is_one = clsb[spans[c], :] > 0.5
            score = scores[c]
            mixes = []
            total_sg = score_sum[c]
            for j in range(per):
                head = p * per + j
                step = steprow[head, c : c + 1, :]
                weight = jnp.where(is_one, weights[j][1], weights[j][0])
                ws = weight * step
                mgj = mg[j * Q : (j + 1) * Q]
                mixes.append((score * ws).astype(BF16))
                total_sg = total_sg + mgj * ws
                graded = mgj * score
                sgrow[head, c : c + 1, :] = jnp.sum(graded * weight, axis=0, keepdims=True)
                term = graded * step
                terms[j][0] = terms[j][0] + jnp.where(is_one, 0.0, term)
                terms[j][1] = terms[j][1] + jnp.where(is_one, term, 0.0)
            score_sum[c] = total_sg
            nout[p, spans[c], :] = dot(jnp.concatenate(mixes, axis=1), xs, 1, 0)
            nback[p, spans[c], :] = dot(jnp.concatenate(mixes, axis=0), gs, 0, 0)
        for j in range(per):
            for k in range(2):
                term = terms[j][k]
                blocks = [term[i * SUB : (i + 1) * SUB] for i in range(Q // SUB)]
                inside = blocks[0]
                for i in range(1, Q // SUB):
                    inside = jnp.where(lane // SUB == i, blocks[i], inside)
                for level in range(sb + 1):
                    size = 1 << max(level - 1, 0)
                    if size < SUB:
                        value = jnp.where(lev8 == level, inside, 0.0)
                    else:
                        value = jnp.zeros((SUB, LANES), F32)
                        for odd in range(1, Q // size, 2):
                            first = odd * size // SUB
                            rows = sum(blocks[first + 1 : first + size // SUB], blocks[first])
                            value = jnp.where(lane // size == odd - 1, rows, value)
                    tab[k * levels + level, pl.ds(p * per + j, 1), :] = jnp.sum(
                        value, axis=0, keepdims=True
                    )
        return carry
    def table_of(some):
        summed = jnp.zeros((heads, LANES), F32)
        for k in range(2):
            for level in some:
                at = k * levels + level
                col = jnp.sum(tab[at], axis=1, keepdims=True)
                summed = jnp.where(lane == at, col * (scale_of(level) / math.sqrt(total)), summed)
        return summed

    def forward_map(p, c):
        cs = []
        for k in range(2):
            value = fcs[k, p]
            if c == 1:
                value = value + wrow(p, k, mid) * s0[p]
            cs.append(value.astype(BF16))
        return jnp.concatenate(cs, axis=0)

    def backward_map(p, c):
        src = fsrc[p]
        if c == 0:
            src = src + wrow(p, 0, mid) * q1[0, p] + wrow(p, 1, mid) * q1[1, p]
        return src.astype(BF16)

    def map_forward(p):
        for c in range(2):
            cs = forward_map(p, c)
            maps[c, p] = cs
            out_acc[c] = out_acc[c] + dot(g_ref[spans[c], cols(p)], cs, 1, 1)

    def values_forward(p):
        for c in range(2):
            read = dot(mo2[c], maps[c, p], 1, 0)
            out_ref[spans[c], cols(p)] = (nout[p, spans[c], :] + read).astype(BF16)

    def map_backward(p):
        for c in range(2):
            src = backward_map(p, c)
            source_maps[c, p] = src
            grad[0, c] = grad[0, c] + dot(scaled[p, spans[c], :], src, 1, 1)

    def values_backward(p):
        for c in range(2):
            vg = dot(bin_ref[spans[c], :], source_maps[c, p], 1, 0)
            xg_ref[spans[c], cols(p)] = (
                nback[p, spans[c], :] + stepx[p, spans[c], :] * vg
            ).astype(BF16)
            whole = x_ref[spans[c], cols(p)].astype(F32) * vg
            coarse = whole.astype(BF16)
            fine = (whole - coarse.astype(F32)).astype(BF16)
            far_step = dot(picks, jnp.concatenate([coarse, fine], axis=1), 1, 1)
            for j in range(per):
                at = (p * per + j, slice(c, c + 1), slice(None))
                sgrow[at] = sgrow[at] + far_step[j : j + 1]

    def finish_forward():
        for c in range(2):
            is_one = clsb[spans[c], :] > 0.5
            acc = out_acc[c]
            grad[1, c] = grad[1, c] + jnp.where(is_one, acc[:, state:], acc[:, :state])

    def beside_copy(kind):
        return pltpu.make_async_remote_copy(
            grad.at[kind], core_recv.at[kind], c_ssem.at[kind], c_rsem.at[kind],
            device_id=across(0, 1), device_id_type=MESH,
        )

    def across_copy(kind, i, other, slot, part):
        return pltpu.make_async_remote_copy(
            x_recv.at[kind, group, low], x_recv.at[kind, slot, part],
            x_ssem.at[kind, i, other], x_rsem.at[kind, i, other],
            device_id=across(i, other), device_id_type=MESH,
        )

    def sum_beside(kind):
        beside_copy(kind).wait_recv()
        for c in range(2):
            x_recv[kind, group, c] = (grad[kind, c] + core_recv[kind, c]).astype(BF16)
        for i in range(1, groups):
            for other in range(2):
                across_copy(kind, i, other, group, low).start()

    def sum_across(kind):
        for i in range(1, groups):
            slot = lax.rem(group - i + groups, groups)
            for other in range(2):
                part = 1 - low if other else low
                across_copy(kind, i, other, slot, part).wait_recv()

    def whole_sum(kind, c):
        whole = x_recv[kind, 0, c].astype(F32)
        for i in range(1, groups):
            whole = whole + x_recv[kind, i, c].astype(F32)
        return whole

    for stage in range(nb):

        def rounds(p, stage=stage):
            if stage == 0:
                near(p, 0)
                for k in range(2):
                    put_rows(k, mid, p, jnp.sum(s0[p] * q1[k, p], axis=0, keepdims=True))
            if stage < nb - 1:
                primary(stage, p)
            if stage >= 1:
                secondary(stage - 1, p)
        each(rounds)
        if stage == 0:
            for c in range(2):
                sgb = score_sum[c].astype(BF16)
                grad[0, c] = dot(sgb, cout_ref[spans[c], :], 0, 0)
                grad[1, c] = dot(sgb, bin_ref[spans[c], :], 1, 0)
            near_sum[...] = table_of(range(mid + 1))
            for b in range(nb - 1):
                pl.semaphore_wait(known.at[b], 1)
                if b + 1 < nb - 1:
                    tell(b + 1)


    def table_copy(i):
        return pltpu.make_async_remote_copy(
            tsend, trecv.at[i], t_ssem.at[i], t_rsem.at[i],
            device_id={"seq": device ^ i}, device_id_type=MESH,
        )

    def send_table():
        table_sum = near_sum[...] + table_of(range(far0, levels))
        tsend[:heads, :] = table_sum
        trecv[0, :heads, :] = table_sum
        for i in reversed(range(1, 1 << nb)):
            table_copy(i).start()

    @pl.when(top == 0)
    def _():
        send_table()

        def forward(p):
            map_forward(p)
            values_forward(p)

        each(forward)
        finish_forward()
        beside_copy(1).start()

    def last_values(p):
        values_backward(p)

        @pl.when(top == 1)
        def _():
            values_forward(p)

    def last_kind(p, carry):
        @pl.when(top == 1)
        def _():
            take_f(nb - 1, p)

        @pl.when(top == 0)
        def _():
            for b in range(nb - 1):
                take_own(b, p)

            @pl.when(p == 0)
            def _():
                sum_beside(1)

            take_own(nb - 1, p)
            map_backward(p)

        return carry

    lax.fori_loop(0, pairs, last_kind, 0)

    @pl.when(top == 1)
    def _():
        send_table()
        each(map_forward)
        finish_forward()
        beside_copy(1).start()

        def backward(p):
            for b in range(nb - 1):
                take_own(b, p)
            map_backward(p)

        each(backward)

    beside_copy(0).start()

    @pl.when(top == 1)
    def _():
        sum_beside(1)

    sum_beside(0)
    each(last_values)
    for h in range(heads):
        for c in range(2):
            sg_ref[h : h + 1, spans[c]] = sgrow[h, c : c + 1, :]
    sum_across(1)
    for b in range(end):

        def drain(p, b=b):
            @pl.when(f_sent[b])
            def _():
                f_copy(b, p).wait_send()

            @pl.when(c_sent[b])
            def _():
                r_copy(b, 2, p).wait_send()

            for slot in range(min(2, nb - 1 - b)):

                @pl.when(high_sent[b] if slot == 0 else count[b] > slot)
                def _(slot=slot):
                    r_copy(b, slot, p).wait_send()

        each(drain)

    def drain_last(p, copy):
        for far in range(2):
            copy(far, p).wait_send()

    @pl.when(f_sent[end])
    def _():
        each(lambda p: drain_last(p, f_last))

    @pl.when(c_sent[end])
    def _():
        each(lambda p: drain_last(p, c_last))

    sum_across(0)
    for i in range(1, 1 << nb):
        table_copy(i).wait_recv()
    table_sum = trecv[device, :heads, :]
    for owner in range(1, 1 << nb):
        table_sum = table_sum + trecv[device ^ owner, :heads, :]
    for k in range(2):
        tg_ref[:, k, :] = table_sum[:, k * levels : (k + 1) * levels]

    for kind, ref in ((0, ing_ref), (1, outg_ref)):
        for c in range(2):
            ref[spans[c], :] = whole_sum(kind, c)

    for kind in range(2):
        beside_copy(kind).wait_send()
        for i in range(1, groups):
            for other in range(2):
                across_copy(kind, i, other, group, low).wait_send()
    for i in range(1, 1 << nb):
        table_copy(i).wait_send()


def write_out(*refs):
    sem = refs[-1]
    copies = [pltpu.make_async_copy(refs[i], refs[6 + i], sem.at[i]) for i in range(6)]
    for copy in copies:
        copy.start()
    for copy in copies:
        copy.wait()


def local(inputs, step_sizes, input_map, output_map, level_table, token_class, cotangent):
    tokens, state = input_map.shape
    heads = step_sizes.shape[0]
    width = inputs.shape[1] // heads
    levels = level_table.shape[2]
    n_seq = lax.axis_size("seq")
    n_head = lax.axis_size("head")
    nb = n_seq.bit_length() - 1
    per = LANES // width
    pairs = heads // per
    assert tokens == 2 * Q and heads % per == 0 and n_head % 2 == 0 and nb > 2
    assert level_table.shape[1] == 2 and state == Q and 2 * levels <= LANES
    dims = (heads, width, tokens, state, levels, nb, n_head, float(tokens * n_seq))
    vmem = pl.BlockSpec(memory_space=pltpu.VMEM)
    hbm = pl.BlockSpec(memory_space=pltpu.HBM)
    dma = pltpu.SemaphoreType.DMA
    unit = (pairs, state, LANES)
    tall = (pairs, tokens, LANES)
    padded = -(-heads // 16) * 16
    placed = [
        pltpu.with_memory_space_constraint(a, pltpu.HBM)
        for a in (
            inputs, step_sizes, input_map, output_map, level_table,
            token_class.reshape(1, tokens), cotangent,
        )
    ]
    results = pl.pallas_call(
        functools.partial(kernel, dims),
        out_shape=(
            jax.ShapeDtypeStruct(inputs.shape, BF16),
            jax.ShapeDtypeStruct(inputs.shape, BF16),
            jax.ShapeDtypeStruct(step_sizes.shape, F32),
            jax.ShapeDtypeStruct(input_map.shape, F32),
            jax.ShapeDtypeStruct(output_map.shape, F32),
            jax.ShapeDtypeStruct(level_table.shape, F32),
        ),
        in_specs=[hbm] * 7,
        out_specs=(vmem,) * 6,
        scratch_shapes=[
            pltpu.VMEM((padded, tokens), F32),
            pltpu.VMEM((tokens, 3 * padded), BF16),
            pltpu.VMEM((2, state, Q), BF16),
            pltpu.VMEM((2, 2 * state, Q), BF16),
            pltpu.VMEM(tall, F32),
            pltpu.VMEM(tall, BF16),
            pltpu.VMEM((tokens, LANES), F32),
            pltpu.VMEM((Q, Q), jnp.int32),
            pltpu.VMEM((2, Q, Q), F32),
            pltpu.VMEM((2, Q, 2 * state), BF16),
            pltpu.VMEM(unit, F32),
            pltpu.VMEM((2, *unit), F32),
            pltpu.VMEM((2, *unit), F32),
            pltpu.VMEM(unit, F32),
            pltpu.VMEM((2, *unit), F32),
            pltpu.VMEM((2, *unit), F32),
            pltpu.VMEM(unit, F32),
            pltpu.VMEM(tall, F32),
            pltpu.VMEM(tall, F32),
            pltpu.VMEM((2, Q, Q), F32),
            pltpu.VMEM((2, 2, Q, state), F32),
            pltpu.VMEM((2, Q, 2 * state), F32),
            pltpu.VMEM((2 * levels, heads, LANES), F32),
            pltpu.VMEM((nb, *unit), BF16),
            pltpu.VMEM((nb, *unit), BF16),
            pltpu.VMEM((nb, 3, *unit), BF16),
            pltpu.VMEM((nb, 3, *unit), BF16),
            pltpu.VMEM((2, 2, Q, state), F32),
            pltpu.VMEM((2, n_head // 2, 2, Q, state), BF16),
            pltpu.VMEM((2, pairs, 2 * state, LANES), BF16),
            pltpu.VMEM((2, *unit), BF16),
            pltpu.VMEM((heads, LANES), F32),
            pltpu.VMEM((padded, LANES), F32),
            pltpu.VMEM((n_seq, padded, LANES), F32),
            dma((nb, pairs)),
            dma((nb, pairs)),
            dma((nb, 3, pairs)),
            dma((nb, 3, pairs)),
            dma((2,)),
            dma((2,)),
            dma((2, n_head // 2, 2)),
            dma((2, n_head // 2, 2)),
            dma((n_seq,)),
            dma((n_seq,)),
            dma((2, pairs)),
            dma((pairs,)),
            pltpu.SemaphoreType.REGULAR((nb,)),
            pltpu.VMEM((heads, 2, LANES), F32),
            pltpu.VMEM((heads, 2, LANES), F32),
            pltpu.VMEM(inputs.shape, BF16),
            pltpu.VMEM(step_sizes.shape, F32),
            pltpu.VMEM(input_map.shape, BF16),
            pltpu.VMEM(output_map.shape, BF16),
            pltpu.VMEM((1, tokens), jnp.int32),
            pltpu.VMEM(cotangent.shape, BF16),
            pltpu.SMEM(level_table.shape, F32),
            dma((7,)),
        ],
        compiler_params=pltpu.CompilerParams(
            collective_id=0, has_side_effects=True, vmem_limit_bytes=48 << 20
        ),
    )(*placed)
    return pl.pallas_call(
        write_out,
        out_shape=tuple(jax.ShapeDtypeStruct(r.shape, r.dtype) for r in results),
        in_specs=[vmem] * 6,
        out_specs=(hbm,) * 6,
        scratch_shapes=[dma((6,))],
        compiler_params=pltpu.CompilerParams(vmem_limit_bytes=8 << 20),
    )(*results)


def solution(mesh):
    placed = (
        P("seq", "head"),
        P("head", "seq"),
        P("seq", None),
        P("seq", None),
        P("head", None, None),
        P("seq"),
        P("seq", "head"),
    )
    return jax.shard_map(
        local,
        mesh=mesh,
        in_specs=placed,
        out_specs=(
            P("seq", "head"),
            P("seq", "head"),
            P("head", "seq"),
            P("seq", None),
            P("seq", None),
            P("head", None, None),
        ),
        check_vma=False,
    )
```
